32 devices in a mesh: tm: 4 (over z), det: 8 (over y, x, core).
Axes of the slice: x: 2, y: 2, z: 4, core: 2. Of those that a mesh axis runs over, the one named last changes fastest.
Arguments:
- time_stream: bfloat16 [1024, 32768], P('det', 'tm'), may hold values from -6 to 6
- filter_taps: bfloat16 [1024, 129], P('det'), may hold values from -0.5 to 0.5
- det_precision: bfloat16 [1024, 1024], replicated
- left_weight: float32 [128, 32], replicated, may hold values from -0.046875 to 0.046875
- right_weight: float32 [128, 32], replicated, may hold values from -1 to 1
- frame_tile: int32 [32768, 1], P(('tm', 'det')), may hold values from 0 to 63; in each aligned block of 1024 rows (0 to 1023, 1024 to 2047, ...) at most 24 rows name the same one
- tile_owner: int32 [64], replicated, may hold values from 0 to 31, as said below
- frame_count: int32 [32], P(('tm', 'det')), may hold values from 512 to 1024, as said below
Outputs:
- sky_map: float32 [64, 16384], P(('tm', 'det'))
The draws below stay inside these ranges and needn't reach their ends.
Inputs may be any that keep to these rules, and one draw needn't show every extreme that they name: `frame_tile`: within the frames of one segment (aligned blocks of 1024 rows) no tile is named more than 24 times, a bound that some block reaches. `tile_owner`: every device number is the owner of exactly 2 tiles. `frame_count`: some segment has all 1024 frames live.
All inputs are finite; a program needn't handle non-finite values.
Results may differ from the reference program's by a relative error of at most 0.0041.
Values may be sent and summed in bfloat16 or wider, within the bound.
A program may use at most 64 MiB of HBM per device.

```python
import math
import jax
import jax.numpy as jnp
import numpy as np
from jax import lax

NDET = 1024
HW = 64
FD = 32
FT = 32
TL = 128
SPAN = 1024
TILE_DEV = 2
TAPS = 129
NSAMP = 32768
F_DEV = 1024
NFRAMES = 32768
NTILES = 64
CAP = 24
N_TM = 4
N_DET = 8


def draw_det_precision(key, part):
    first_key, second_key = jax.random.split(jax.random.fold_in(key, 11))
    noise = jax.random.normal(first_key, (NDET, NDET), jnp.float32) * 0.02
    noise = (noise + noise.T) * 0.7071
    diagonal = jax.random.uniform(second_key, (NDET,), jnp.float32, 0.5, 1.5)
    matrix = noise + jnp.diag(diagonal)
    return matrix.astype(jnp.bfloat16)


def draw_tile_owner(key, part):
    order = jax.random.permutation(jax.random.fold_in(key, 23), NTILES)
    return (order // TILE_DEV).astype(jnp.int32)


def draw_frame_count(key, part):
    first_key, second_key = jax.random.split(jax.random.fold_in(key, 37))
    counts = jax.random.randint(first_key, (N_TM * N_DET,), F_DEV // 2, F_DEV + 1, dtype=jnp.int32)
    chosen = jax.random.randint(second_key, (), 0, N_TM * N_DET, dtype=jnp.int32)
    return counts.at[chosen].set(F_DEV).astype(jnp.int32)


def shard_levels(key, dims, cuts, smallest, top_value):
    level = 1.0
    for axis_at, parts in cuts:
        heights = jax.random.uniform(jax.random.fold_in(jax.random.fold_in(key, 6), axis_at), (parts,), jnp.float32, smallest / len(cuts), top_value / len(cuts))
        level = level * jnp.repeat(jnp.exp(heights), dims[axis_at] // parts).reshape((-1,) + (1,) * (len(dims) - 1 - axis_at))
    return level


def routed_block(key, own, number, rows, amount, top, limit, lean):
    ranking = jax.random.permutation(key, amount)
    crowded, usual = load_shares(amount, rows * top, limit, lean, True), load_shares(amount, rows * top, limit, lean, False)
    places = jnp.arange(amount)

    def named(tallies, offset_by):
        used = int((tallies > 0).sum())
        fixed = max(1, used // 4)
        passed = fixed + (places - fixed + offset_by * (used - fixed)) % max(1, amount - fixed)
        return jnp.zeros((amount,), jnp.int32).at[ranking[jnp.where(places < fixed, places, passed)]].set(jnp.asarray(tallies, jnp.int32))

    tallies = jnp.where(number % 4 == 0, named(crowded, number // 4), named(usual, number - number // 4 - 1))
    mixed = jax.random.permutation(jax.random.fold_in(own, 3), amount)
    giver, receiver = mixed[0:amount // 2 * 2:2], mixed[1:amount // 2 * 2:2]
    margin = jnp.minimum(tallies[giver] - 1, limit - tallies[receiver]) // 2
    margin = jnp.where((giver == ranking[0]) | (receiver == ranking[0]) | (tallies[receiver] == 0), 0, jnp.maximum(margin, 0))
    passed = jax.random.randint(jax.random.fold_in(own, 4), (amount // 2,), 0, 1 << 20) % (margin + 1)
    tallies = tallies.at[giver].add(-passed).at[receiver].add(passed)
    members = jnp.searchsorted(jnp.cumsum(tallies), jnp.arange(rows * top), side="right").astype(jnp.int32)
    table = members.reshape(top, rows).T
    table = table[jax.random.permutation(jax.random.fold_in(own, 1), rows)]
    offset_by = jax.random.randint(jax.random.fold_in(own, 2), (rows, 1), 0, top)
    return jnp.take_along_axis(table, (jnp.arange(top)[None, :] + offset_by) % top, axis=1)


def load_shares(number_of, total, limit, lean, full):
    portions = [(1 << 20) // math.isqrt(grade ** lean) + 1 for grade in range(1, number_of + 1)]
    largest = limit if full else min(limit, max(-(-total // number_of), total * portions[0] // sum(portions)))
    least = 1 if total - largest >= number_of - 1 else 0
    holding, rest = [largest] + [least] * (number_of - 1), total - largest - least * (number_of - 1)
    while rest > 0:
        candidates = [i for i in range(1, number_of) if holding[i] < largest] or [i for i in range(1, number_of) if holding[i] < limit]
        mass, remaining = sum([portions[i] for i in candidates]), rest
        for i in candidates:
            addition = min(limit - holding[i], max(1, remaining * portions[i] // mass), rest)
            holding[i] = holding[i] + addition
            rest = rest - addition
    return np.array(holding)


def centred(stream_key, dims, scale, limit, cuts=(), kind=jnp.bfloat16):
    gain = shard_levels(stream_key, dims, cuts, -0.22, 0.18) if cuts else 1.0
    values = jax.random.normal(stream_key, dims, jnp.float32) * scale * gain
    return jnp.minimum(jnp.maximum(values, -limit), limit).astype(kind)


def setup_inputs(seed: int = 0) -> dict:
    key_list = jax.random.split(jax.random.key(seed), 9)
    time_stream = centred(key_list[0], (NDET, NSAMP), 1.0, 6.0, ((0, 8), (1, 4)))
    filter_taps = centred(key_list[1], (NDET, TAPS), TAPS ** -0.5, 0.5, ((0, 8),))
    det_precision = draw_det_precision(jax.random.fold_in(key_list[8], 71), 0)
    left_weight = centred(key_list[3], (TL, FD), (FD * F_DEV // TILE_DEV) ** -0.5, 0.046875, (), jnp.float32)
    right_weight = centred(key_list[4], (TL, FT), FT ** -0.5, 1.0, (), jnp.float32)
    frame_tile_keys = jax.random.split(jax.random.fold_in(key_list[5], 1), NFRAMES // F_DEV)
    frame_tile_turns = jax.random.permutation(jax.random.fold_in(key_list[5], 3), NFRAMES // F_DEV)
    frame_tile = jax.vmap(lambda own, number: routed_block(jax.random.fold_in(key_list[5], 2), own, number, F_DEV, NTILES, 1, CAP, 2))(frame_tile_keys, frame_tile_turns).reshape((NFRAMES, 1))
    tile_owner = draw_tile_owner(jax.random.fold_in(key_list[8], 71), 0)
    frame_count = draw_frame_count(jax.random.fold_in(key_list[8], 71), 0)
    return {"time_stream": time_stream, "filter_taps": filter_taps, "det_precision": det_precision, "left_weight": left_weight, "right_weight": right_weight, "frame_tile": frame_tile, "tile_owner": tile_owner, "frame_count": frame_count}


def toeplitz_block(filter_taps, half_width):
    row_index = jnp.arange(4 * half_width, dtype=jnp.int32)[:, None]
    col_index = jnp.arange(2 * half_width, dtype=jnp.int32)[None, :]
    offset = row_index - col_index
    inside = (offset >= 0) & (offset <= 2 * half_width)
    picked = jnp.take(filter_taps, jnp.clip(offset, 0, 2 * half_width), axis=1)
    return jnp.where(inside[None, :, :], picked, jnp.zeros((), filter_taps.dtype))


def apply_filter(padded, filter_taps, half_width):
    detectors = padded.shape[0]
    blocks = (padded.shape[1] - 2 * half_width) // (2 * half_width)
    pieces = padded.reshape(detectors, blocks + 1, 2 * half_width)
    windows = jnp.concatenate([pieces[:, :-1], pieces[:, 1:]], axis=2)
    matrix = toeplitz_block(filter_taps, half_width)
    result = jnp.einsum("dbj,dji->dbi", windows.astype(jnp.float32), matrix.astype(jnp.float32))
    return result.reshape(detectors, blocks * 2 * half_width)


def frame_rows(whitened):
    groups = whitened.shape[0] // FD
    columns = whitened.shape[1] // FT
    frame_cube = whitened.reshape(groups, FD, columns, FT).transpose(0, 2, 1, 3)
    return frame_cube.reshape(groups * columns, FD * FT)


def owner_rows(tile_owner):
    total_tiles = tile_owner.shape[0]
    same_owner = tile_owner[:, None] == tile_owner[None, :]
    earlier = jnp.arange(total_tiles)[None, :] < jnp.arange(total_tiles)[:, None]
    slot_rank = jnp.sum((same_owner & earlier).astype(jnp.int32), axis=1)
    return (tile_owner * TILE_DEV + slot_rank).astype(jnp.int32)


def project(summed, left_weight, right_weight):
    tiles_here = summed.shape[0]
    frame_cube = summed.reshape(tiles_here, FD, FT)
    partial_value = jnp.einsum("naf,jf->naj", frame_cube, right_weight, precision=lax.Precision.HIGHEST)
    result = jnp.einsum("ia,naj->nij", left_weight, partial_value, precision=lax.Precision.HIGHEST)
    return result.reshape(tiles_here, TL * TL)


def reference(time_stream, filter_taps, det_precision, left_weight, right_weight, frame_tile, tile_owner, frame_count):
    padded = jnp.pad(time_stream, ((0, 0), (HW, HW)))
    tile_index = jnp.arange(NTILES, dtype=jnp.int32)
    frame_index = jnp.arange(F_DEV, dtype=jnp.int32)
    tile_column = frame_tile[:, 0]

    def segment(totals, segment_id):
        offset = (segment_id * SPAN).astype(jnp.int32)
        window = lax.dynamic_slice(padded, (jnp.int32(0), offset), (NDET, SPAN + 2 * HW))
        filtered = apply_filter(window, filter_taps, HW).astype(jnp.bfloat16)
        whitened = jnp.dot(det_precision, filtered, preferred_element_type=jnp.float32).astype(jnp.bfloat16)
        frames = frame_rows(whitened)
        tile_ids = lax.dynamic_slice_in_dim(tile_column, (segment_id * F_DEV).astype(jnp.int32), F_DEV)
        alive_mask = frame_index < frame_count[segment_id]
        onehot = ((tile_ids[:, None] == tile_index[None, :]) & alive_mask[:, None]).astype(jnp.bfloat16)
        added = jnp.einsum("ft,fc->tc", onehot, frames, preferred_element_type=jnp.float32)
        return totals + added, None

    totals, unused = lax.scan(segment, jnp.zeros((NTILES, FD * FT), jnp.float32), jnp.arange(N_TM * N_DET, dtype=jnp.int32))
    ordered = jnp.zeros_like(totals).at[owner_rows(tile_owner)].set(totals)
    return project(ordered, left_weight, right_weight)
```

```python
import functools

import jax
import jax.numpy as jnp
from jax import lax
from jax.experimental import pallas as pl
from jax.experimental.pallas import tpu as pltpu
from jax.sharding import PartitionSpec as P

TILE_DEV = 2
LANES = 128
MESH = pl.DeviceIdType.MESH
VMEM = pltpu.VMEM
F32 = jnp.float32
BF16 = jnp.bfloat16
CONTRACT = (((1,), (1,)), ((), ()))


def owner_rows(tile_owner):
    total_tiles = tile_owner.shape[0]
    same_owner = tile_owner[:, None] == tile_owner[None, :]
    earlier = jnp.arange(total_tiles)[None, :] < jnp.arange(total_tiles)[:, None]
    slot_rank = jnp.sum((same_owner & earlier).astype(jnp.int32), axis=1)
    return tile_owner * TILE_DEV + slot_rank


def start_edges(n_tm, n_det, width, x_ref, low_ref, high_ref, all_ref, rows_ref, send_sem, recv_sem, halo_send, halo_recv, own_sem):
    tm, det = lax.axis_index("tm"), lax.axis_index("det")
    has_low, has_high = tm > 0, tm < n_tm - 1
    down = pltpu.make_async_remote_copy(
        src_ref=x_ref.at[:, 0:width], dst_ref=high_ref, send_sem=halo_send.at[0], recv_sem=halo_recv.at[0],
        device_id=(tm - 1, det), device_id_type=MESH)
    up = pltpu.make_async_remote_copy(
        src_ref=x_ref.at[:, x_ref.shape[1] - width:], dst_ref=low_ref, send_sem=halo_send.at[1], recv_sem=halo_recv.at[1],
        device_id=(tm + 1, det), device_id_type=MESH)

    @pl.when(has_low)
    def _():
        down.start()

    @pl.when(has_high)
    def _():
        up.start()

    copies = []
    for step in range(1, n_det):
        copy = pltpu.make_async_remote_copy(
            src_ref=rows_ref, dst_ref=all_ref.at[det], send_sem=send_sem.at[step], recv_sem=recv_sem.at[step],
            device_id=(tm, lax.rem(det + step, n_det)), device_id_type=MESH)
        copy.start()
        copies.append(copy)
    own = pltpu.make_async_copy(rows_ref, all_ref.at[det], own_sem)
    own.start()

    @pl.when(jnp.logical_not(has_low))
    def _():
        low_ref[...] = jnp.zeros_like(low_ref)

    @pl.when(jnp.logical_not(has_high))
    def _():
        high_ref[...] = jnp.zeros_like(high_ref)

    def finish():
        own.wait()
        for copy in copies:
            copy.wait()

        @pl.when(has_low)
        def _():
            down.wait_send()
            up.wait_recv()

        @pl.when(has_high)
        def _():
            up.wait_send()
            down.wait_recv()

    return finish


def live_rows(tile_ref, count_ref, rows_ref):
    tile = tile_ref[...]
    frame = lax.broadcasted_iota(jnp.int32, tile.shape, 0) * tile.shape[1] + lax.broadcasted_iota(jnp.int32, tile.shape, 1)
    rows_ref[...] = jnp.where(frame < count_ref[0], tile, -1)


def edge_kernel(n_tm, n_det, width, x_ref, tile_ref, count_ref, low_ref, high_ref, all_ref, rows_ref, *sems):
    tm, det = lax.axis_index("tm"), lax.axis_index("det")
    has_low, has_high = tm > 0, tm < n_tm - 1
    barrier = pltpu.get_barrier_semaphore()
    for step in range(1, n_det):
        pl.semaphore_signal(barrier, inc=1, device_id=(tm, lax.rem(det + step, n_det)), device_id_type=MESH)

    @pl.when(has_low)
    def _():
        pl.semaphore_signal(barrier, inc=1, device_id=(tm - 1, det), device_id_type=MESH)

    @pl.when(has_high)
    def _():
        pl.semaphore_signal(barrier, inc=1, device_id=(tm + 1, det), device_id_type=MESH)

    live_rows(tile_ref, count_ref, rows_ref)
    pl.semaphore_wait(barrier, n_det - 1 + has_low.astype(jnp.int32) + has_high.astype(jnp.int32))
    start_edges(n_tm, n_det, width, x_ref, low_ref, high_ref, all_ref, rows_ref, *sems)()


def edge_sems(n_det):
    return [
        pltpu.SemaphoreType.DMA((n_det,)),
        pltpu.SemaphoreType.DMA((n_det,)),
        pltpu.SemaphoreType.DMA((2,)),
        pltpu.SemaphoreType.DMA((2,)),
        pltpu.SemaphoreType.DMA,
    ]


def exchange_edges(n_tm, n_det, width, x, tile, count):
    vmem = pl.BlockSpec(memory_space=VMEM)
    halo = jax.ShapeDtypeStruct((x.shape[0], width), x.dtype)
    return pl.pallas_call(
        functools.partial(edge_kernel, n_tm, n_det, width),
        out_shape=(halo, halo, jax.ShapeDtypeStruct((n_det,) + tile.shape, tile.dtype)),
        in_specs=[pl.BlockSpec(memory_space=pl.ANY), vmem, pl.BlockSpec(memory_space=pltpu.SMEM)],
        out_specs=(vmem,) * 3,
        scratch_shapes=[
            VMEM(tile.shape, tile.dtype),
        ] + edge_sems(n_det),
        compiler_params=pltpu.CompilerParams(collective_id=0, has_side_effects=True),
        name="edges",
    )(x, tile, count)


def fast_path(n_det, half, fd, ft, x):
    width = 2 * half
    return (
        n_det % 2 == 0 and x.shape[0] == LANES and width == LANES and x.shape[1] == half * LANES
        and fd == ft and half == 2 * ft and (x.shape[1] // ft) % (4 * n_det) == 0)


def load_blocks(half, x_hbm, x_ref, load_sem, cur, mid, pitch):
    dets, samples = x_ref.shape
    width = 2 * half
    pieces = load_sem.shape[0]
    span = samples // pieces
    loads = []
    for piece in range(pieces):
        part = pl.ds(piece * span, span)
        load = pltpu.make_async_copy(x_hbm.at[:, part], x_ref.at[:, part], load_sem.at[piece])
        load.start()
        loads.append(load)

    def finish():
        per = span // width
        for piece, load in enumerate(loads):
            load.wait()
            for b in range(piece * per, (piece + 1) * per):
                at = b * width
                cur[b * pitch:b * pitch + dets, :] = x_ref[:, at:at + width].astype(F32)
                if b:
                    mid[b * pitch:b * pitch + dets, :] = x_ref[:, at - half:at + half].astype(F32)

    return finish


def edge_blocks(half, x_ref, low_ref, high_ref, cur, mid, pitch):
    dets, samples = x_ref.shape
    last = samples // (2 * half) * pitch
    first = jnp.concatenate([low_ref[:, half:], x_ref[:, 0:half]], axis=1)
    mid[0:dets, :] = first.astype(F32)
    mid[last:last + dets, :] = jnp.concatenate([x_ref[:, samples - half:], high_ref[:, 0:half]], axis=1).astype(F32)
    cur[last:last + dets, :] = high_ref[...].astype(F32)


def spread_taps(tapst_ref, wide, taps_ref):
    wide[...] = jnp.zeros(wide.shape, F32)
    wide[0:tapst_ref.shape[0], :] = tapst_ref[...].astype(F32)
    taps_ref[...] = wide[...].T


def owner_order(owner_ref, tiles):
    across_owner = jnp.broadcast_to(owner_ref[...].astype(F32), (tiles, tiles))
    down = lax.broadcasted_iota(jnp.int32, (tiles, tiles), 0)
    across_tile = lax.broadcasted_iota(jnp.int32, (tiles, tiles), 1)
    earlier = (across_owner.T == across_owner) & (down < across_tile)
    rank = jnp.sum(jnp.where(earlier, 1.0, 0.0), axis=0, keepdims=True)
    place = across_owner * TILE_DEV + rank
    order = jnp.sum(jnp.where(place == down.astype(F32), across_tile.astype(F32), 0.0), axis=1, keepdims=True)
    return jnp.broadcast_to(order, (tiles, LANES))


def filter_chunks(half, ft, core, cur, mid, pitch, taps_ref, stage, kept, sent, send):
    chunks, frames, unroll, _ = sent.shape
    dets = chunks * unroll
    blocks = LANES // 2
    step_rows = stage.shape[1] // ft

    def chunk_step(c, carry):
        for k in range(unroll):
            d = c * unroll + k
            spread = jnp.broadcast_to(taps_ref[pl.ds(d, 1), :], (half, 4 * half))
            matrix = pltpu.roll(spread, 0, 1, stride=1, stride_axis=0).astype(BF16)
            rows = []
            for source in (mid, cur):
                lower = source[pl.ds(d, blocks, stride=pitch), :]
                upper = source[pl.ds(d + pitch, blocks, stride=pitch), :]
                rows.append(jnp.concatenate([lower, upper], axis=1))
            window = jnp.concatenate(rows, axis=0).astype(BF16)
            result = lax.dot_general(matrix, window, CONTRACT, preferred_element_type=F32)
            for q in range(2):
                stage[q, pl.ds(k, ft, stride=step_rows), :] = result[q * ft:(q + 1) * ft, :]
        at = pl.multiple_of(core * dets + c * unroll, unroll)
        for f in range(frames):
            rows = slice(f * step_rows, f * step_rows + unroll)
            kept[f, pl.ds(at, unroll), :] = stage[core, rows, :].astype(BF16)
            sent[c, f] = stage[1 - core, rows, :].astype(BF16)
        send(c).start()
        return carry

    lax.fori_loop(0, chunks, chunk_step, 0)


def pick_frames(core, fd, ft, order, rows_ref, picks):
    segments, rows, width = rows_ref.shape
    tiles = order.shape[0]
    per_row = width // fd
    spans = LANES // 2 // segments
    lane = lax.broadcasted_iota(jnp.int32, (LANES, per_row * LANES), 1)
    at = lax.broadcasted_iota(jnp.int32, (LANES, per_row * LANES), 0)
    h, inner = lane // LANES, lane % LANES
    p, m = inner // (LANES // 2), inner % (LANES // 2)
    target = (m // spans) * width + h * fd + 4 * (m % spans) + 2 * p + core - at
    found = jnp.zeros((2 * rows, per_row * LANES), F32)
    for s in range(segments):
        one = jnp.where(target == s * width, 1.0, 0.0).astype(BF16)
        tile = rows_ref[s].astype(F32)
        found += jnp.dot(jnp.concatenate([tile, tile], axis=0).astype(BF16), one, preferred_element_type=F32)
    for r in range(rows):
        for k in range(per_row):
            g = r * per_row + k
            picks[:, g * LANES:(g + 1) * LANES] = jnp.where(
                order == found[r:r + 1, k * LANES:(k + 1) * LANES], 1.0, 0.0).astype(BF16)


def whiten(fd, prec_ref, kept, whitened):
    frames = kept.shape[0]
    across = LANES // fd
    low = frames // across
    groups = prec_ref.shape[0] // fd

    def step(u, carry):
        for v in range(0, across, 2):
            weight = jnp.concatenate([kept[(v + i) * low + u] for i in range(2)], axis=1)
            result = jnp.dot(prec_ref[...], weight, preferred_element_type=F32).astype(BF16)
            for i in range(2):
                at = pl.multiple_of((u * across + v + i) * fd, fd)
                for g in range(groups):
                    whitened[pl.ds(at, fd), g * LANES:(g + 1) * LANES] = (
                        result[g * fd:(g + 1) * fd, i * LANES:(i + 1) * LANES])
        return carry

    lax.fori_loop(0, low, step, 0, unroll=2)


def tile_sums(picks, whitened, packed, out_ref):
    tiles = picks.shape[0]
    low = whitened.shape[0] // LANES
    pitch = packed.shape[0] // low
    for u in range(low):
        packed[u * pitch:u * pitch + tiles, :] = lax.dot_general(
            picks[...], whitened[u * LANES:(u + 1) * LANES, :], CONTRACT, preferred_element_type=F32)
    for owner in range(out_ref.shape[0]):
        mine = [packed[pl.ds(owner * TILE_DEV + k, low, stride=pitch), :] for k in range(TILE_DEV)]
        out_ref[owner] = jnp.concatenate(mine, axis=0).astype(out_ref.dtype)


CHUNK = 32
PITCH = 4


def partial_scratch(half, fd, ft, tiles, x, precision):
    dets, samples = x.shape
    width = 2 * half
    blocks = (samples // width + 1) * (dets + PITCH)
    chunks = dets // CHUNK
    return [
        VMEM(x.shape, BF16),
        VMEM((precision.shape[0], 2 * dets), BF16),
        pltpu.SemaphoreType.DMA((4,)),
        pltpu.SemaphoreType.DMA,
        pltpu.SemaphoreType.DMA((chunks,)),
        pltpu.SemaphoreType.DMA((chunks,)),
        VMEM((2 * width, dets), F32),
        VMEM((dets, 2 * width), F32),
        VMEM((blocks, width), F32),
        VMEM((blocks, width), F32),
        VMEM((2, ft * (CHUNK + 1), LANES), F32),
        VMEM((ft, 2 * dets, LANES), BF16),
        VMEM((chunks, ft, CHUNK, LANES), BF16),
        VMEM((tiles, precision.shape[0] // fd * LANES), BF16),
        VMEM((ft * fd, precision.shape[0] // fd * LANES), BF16),
        VMEM((ft * fd // LANES * (tiles + PITCH), LANES), F32),
    ]


def part_shape(fd, ft, tiles):
    return (tiles // TILE_DEV, TILE_DEV * ft // (LANES // fd), LANES)


def plain_partial_sums(x, low, high, taps, rows, owner, precision, half, fd, ft, tiles):
    dets, samples = x.shape
    width = 2 * half
    groups = precision.shape[0] // fd
    blocks = samples // width
    padded = jnp.concatenate([low[:, -half:], x, high[:, :half]], axis=1).reshape(dets, blocks + 1, width)
    length = 4 * half + 1
    tiled = jnp.broadcast_to(jnp.pad(taps, ((0, 0), (0, length - taps.shape[1])))[:, None, :], (dets, width, length))
    matrix = tiled.reshape(dets, width * length)[:, :width * 2 * width].reshape(dets, width, 2 * width)
    near = jnp.einsum("dbj,dij->dbi", padded, matrix[:, :, :width], preferred_element_type=F32)
    far = jnp.einsum("dbj,dij->dbi", padded, matrix[:, :, width:], preferred_element_type=F32)
    filtered = (near[:, :-1] + far[:, 1:]).astype(BF16).reshape(dets, samples // ft, ft)
    order = jnp.argsort(owner_rows(owner)).astype(jnp.int32)
    rows = rows.reshape(rows.shape[0], groups, -1).transpose(1, 0, 2).reshape(groups, 1, -1)
    picks = (rows == order[None, :, None]).astype(BF16)
    sums = jnp.einsum("gkt,dtf->gkfd", picks, filtered, preferred_element_type=F32).astype(BF16)
    out = jnp.einsum("gkfd,gad->kfa", sums, precision.reshape(groups, fd, dets), preferred_element_type=F32)
    across = LANES // fd
    low_part = ft // across
    out = out.reshape(tiles, across, low_part, fd).transpose(0, 2, 1, 3)
    return out.reshape(tiles // TILE_DEV, TILE_DEV * low_part, LANES).astype(BF16)


def peer(me, step, n_tm, n_det):
    other = lax.rem(me + step, n_tm * n_det)
    return other, (other // n_det, lax.rem(other, n_det))


def greet(n_tm, n_det):
    me = lax.axis_index("tm") * n_det + lax.axis_index("det")
    barrier = pltpu.get_barrier_semaphore()
    for step in range(1, n_tm * n_det):
        pl.semaphore_signal(barrier, inc=1, device_id=peer(me, step, n_tm, n_det)[1], device_id_type=MESH)
    return me, barrier


def gather_body(n_tm, n_det, me, part_ref, left_ref, right_ref, out_ref, held, send_sem, recv_sem, own_sem):
    count = n_tm * n_det
    fd = left_ref.shape[0]
    copies = []
    far = range(n_det, count)
    for step in [*far, *range(1, n_det)]:
        other, where = peer(me, step, n_tm, n_det)
        copy = pltpu.make_async_remote_copy(
            src_ref=part_ref.at[other], dst_ref=held.at[me], send_sem=send_sem.at[step], recv_sem=recv_sem.at[step],
            device_id=where, device_id_type=MESH)
        copy.start()
        copies.append(copy)
    own = pltpu.make_async_copy(part_ref.at[me], held.at[me], own_sem)
    own.start()
    own.wait()
    for copy in copies:
        copy.wait()
    total = jnp.sum(held[...].astype(F32), axis=0)
    low = total.shape[0] // TILE_DEV
    across = total.shape[1] // fd
    tiles = []
    for k in range(TILE_DEV):
        tile = total[k * low:(k + 1) * low, :]
        stacked = jnp.concatenate([tile[:, v * fd:(v + 1) * fd] for v in range(across)], axis=0)
        rows = jnp.dot(stacked, left_ref[...], precision=lax.Precision.HIGHEST, preferred_element_type=F32)
        tiles.append(lax.dot_general(
            rows, right_ref[...], (((0,), (0,)), ((), ())), precision=lax.Precision.HIGHEST,
            preferred_element_type=F32))
    width = right_ref.shape[1]
    for i in range(left_ref.shape[1]):
        out_ref[:, i * width:(i + 1) * width] = jnp.concatenate([tile[i:i + 1, :] for tile in tiles], axis=0)


def gather_kernel(n_tm, n_det, part_ref, left_ref, right_ref, out_ref, *scratch):
    me, barrier = greet(n_tm, n_det)
    pl.semaphore_wait(barrier, n_tm * n_det - 1)
    gather_body(n_tm, n_det, me, part_ref, left_ref, right_ref, out_ref, *scratch)


def whole_kernel(n_tm, n_det, sizes, x_hbm, tapst_ref, owner_ref, prec_hbm, tile_ref, left_ref, right_ref, count_ref, out_ref, part, low, high, held_rows, own_rows, *rest):
    half, fd, ft, tiles = sizes
    edge, gather = rest[:5], rest[5:9]
    (x_ref, prec_ref, load_sem, prec_sem, pair_send, pair_recv, wide, taps_ref, cur, mid, stage, kept, sent, picks,
     whitened, packed) = rest[9:]
    tm, det = lax.axis_index("tm"), lax.axis_index("det")
    core = lax.rem(det, 2)
    dets = x_ref.shape[0]
    pitch = dets + PITCH
    unroll = sent.shape[2]
    build = load_blocks(half, x_hbm, x_ref, load_sem, cur, mid, pitch)
    first = pl.multiple_of((det - core) * dets, 2 * dets)
    load = pltpu.make_async_copy(prec_hbm.at[:, pl.ds(first, 2 * dets)], prec_ref, prec_sem)
    load.start()
    live_rows(tile_ref, count_ref, own_rows)
    me, barrier = greet(n_tm, n_det)
    build()
    pl.semaphore_wait(barrier, n_tm * n_det - 1)
    finish = start_edges(n_tm, n_det, 2 * half, x_hbm, low, high, held_rows, own_rows, *edge)
    spread_taps(tapst_ref, wide, taps_ref)
    finish()
    edge_blocks(half, x_ref, low, high, cur, mid, pitch)

    def send(c):
        at = pl.multiple_of(core * dets + c * unroll, unroll)
        return pltpu.make_async_remote_copy(
            src_ref=sent.at[c], dst_ref=kept.at[:, pl.ds(at, unroll), :], send_sem=pair_send.at[c],
            recv_sem=pair_recv.at[c], device_id=(tm, det + 1 - 2 * core), device_id_type=MESH)

    filter_chunks(half, ft, core, cur, mid, pitch, taps_ref, stage, kept, sent, send)
    pick_frames(core, fd, ft, owner_order(owner_ref, tiles), held_rows, picks)
    load.wait()
    for c in range(sent.shape[0]):
        send(c).wait()
    whiten(fd, prec_ref, kept, whitened)
    tile_sums(picks, whitened, packed, part)
    gather_body(n_tm, n_det, me, part, left_ref, right_ref, out_ref, *gather)


def gather_scratch(count, shape):
    return [
        VMEM(shape, BF16),
        pltpu.SemaphoreType.DMA((count,)),
        pltpu.SemaphoreType.DMA((count,)),
        pltpu.SemaphoreType.DMA,
    ]


def call(kernel, specs, inputs, scratch, flat, name):
    return pl.pallas_call(
        kernel,
        out_shape=jax.ShapeDtypeStruct((TILE_DEV, flat), F32),
        in_specs=[pl.BlockSpec(memory_space=space) for space in specs],
        out_specs=pl.BlockSpec(memory_space=VMEM),
        scratch_shapes=scratch,
        compiler_params=pltpu.CompilerParams(
            collective_id=1, has_side_effects=True, vmem_limit_bytes=60 * 1024 * 1024),
        name=name,
    )(*inputs)


def local(
    n_tm, n_det,
    time_stream, filter_taps, det_precision, left_weight, right_weight, frame_tile, tile_owner, frame_count,
):
    half = filter_taps.shape[1] // 2
    fd, ft = left_weight.shape[1], right_weight.shape[1]
    dets = time_stream.shape[0]
    tiles = tile_owner.shape[0]
    count = n_tm * n_det
    tile = frame_tile.reshape(-1, LANES)
    sizes = (half, fd, ft, tiles)
    shape = part_shape(fd, ft, tiles)
    flat = left_weight.shape[0] * right_weight.shape[0]
    weights = (left_weight.T, right_weight.T)
    gather = gather_scratch(count, shape)
    if fast_path(n_det, half, fd, ft, time_stream):
        inputs = (time_stream, filter_taps.T, tile_owner.reshape(1, -1), det_precision, tile) + weights + (frame_count,)
        specs = (pl.ANY, VMEM, VMEM, pl.ANY, VMEM, VMEM, VMEM, pltpu.SMEM)
        halo = VMEM((dets, 2 * half), BF16)
        scratch = [VMEM(shape, BF16), halo, halo, VMEM((n_det,) + tile.shape, tile.dtype), VMEM(tile.shape, tile.dtype)]
        scratch += edge_sems(n_det) + gather + partial_scratch(half, fd, ft, tiles, time_stream, det_precision)
        return call(functools.partial(whole_kernel, n_tm, n_det, sizes), specs, inputs, scratch, flat, "whole")
    low, high, rows = exchange_edges(n_tm, n_det, 2 * half, time_stream, tile, frame_count)
    precision = lax.dynamic_slice_in_dim(det_precision, lax.axis_index("det") * dets, dets, axis=1)
    part = plain_partial_sums(time_stream, low, high, filter_taps, rows, tile_owner, precision, *sizes)
    return call(functools.partial(gather_kernel, n_tm, n_det), (VMEM,) * 3, (part,) + weights, gather, flat, "gather")


def solution(mesh):
    return jax.shard_map(
        functools.partial(local, mesh.shape["tm"], mesh.shape["det"]),
        mesh=mesh,
        in_specs=(
            P("det", "tm"),
            P("det", None),
            P(),
            P(),
            P(),
            P(("tm", "det"), None),
            P(),
            P(("tm", "det")),
        ),
        out_specs=P(("tm", "det"), None),
        check_vma=False,
    )
```

```python
import functools

import jax
import jax.numpy as jnp
from jax import lax
from jax.experimental import pallas as pl
from jax.experimental.pallas import tpu as pltpu
from jax.sharding import PartitionSpec as P

TILE_DEV = 2
LANES = 128
MESH = pl.DeviceIdType.MESH
VMEM = pltpu.VMEM
F32 = jnp.float32
BF16 = jnp.bfloat16
CONTRACT = (((1,), (1,)), ((), ()))


def owner_rows(tile_owner):
    total_tiles = tile_owner.shape[0]
    same_owner = tile_owner[:, None] == tile_owner[None, :]
    earlier = jnp.arange(total_tiles)[None, :] < jnp.arange(total_tiles)[:, None]
    slot_rank = jnp.sum((same_owner & earlier).astype(jnp.int32), axis=1)
    return tile_owner * TILE_DEV + slot_rank


def start_edges(n_tm, n_det, width, x_ref, low_ref, high_ref, all_ref, rows_ref, send_sem, recv_sem, halo_send, halo_recv, own_sem):
    tm, det = lax.axis_index("tm"), lax.axis_index("det")
    has_low, has_high = tm > 0, tm < n_tm - 1
    down = pltpu.make_async_remote_copy(
        src_ref=x_ref.at[:, 0:width], dst_ref=high_ref, send_sem=halo_send.at[0], recv_sem=halo_recv.at[0],
        device_id=(tm - 1, det), device_id_type=MESH)
    up = pltpu.make_async_remote_copy(
        src_ref=x_ref.at[:, x_ref.shape[1] - width:], dst_ref=low_ref, send_sem=halo_send.at[1], recv_sem=halo_recv.at[1],
        device_id=(tm + 1, det), device_id_type=MESH)

    @pl.when(has_low)
    def _():
        down.start()

    @pl.when(has_high)
    def _():
        up.start()

    copies = []
    for step in range(1, n_det):
        copy = pltpu.make_async_remote_copy(
            src_ref=rows_ref, dst_ref=all_ref.at[det], send_sem=send_sem.at[step], recv_sem=recv_sem.at[step],
            device_id=(tm, lax.rem(det + step, n_det)), device_id_type=MESH)
        copy.start()
        copies.append(copy)
    own = pltpu.make_async_copy(rows_ref, all_ref.at[det], own_sem)
    own.start()

    @pl.when(jnp.logical_not(has_low))
    def _():
        low_ref[...] = jnp.zeros_like(low_ref)

    @pl.when(jnp.logical_not(has_high))
    def _():
        high_ref[...] = jnp.zeros_like(high_ref)

    def finish():
        own.wait()
        for copy in copies:
            copy.wait()

        @pl.when(has_low)
        def _():
            down.wait_send()
            up.wait_recv()

        @pl.when(has_high)
        def _():
            up.wait_send()
            down.wait_recv()

    return finish


def live_rows(tile_ref, count_ref, rows_ref):
    tile = tile_ref[...]
    frame = lax.broadcasted_iota(jnp.int32, tile.shape, 0) * tile.shape[1] + lax.broadcasted_iota(jnp.int32, tile.shape, 1)
    rows_ref[...] = jnp.where(frame < count_ref[0], tile, -1)


def edge_kernel(n_tm, n_det, width, x_ref, tile_ref, count_ref, low_ref, high_ref, all_ref, rows_ref, *sems):
    tm, det = lax.axis_index("tm"), lax.axis_index("det")
    has_low, has_high = tm > 0, tm < n_tm - 1
    barrier = pltpu.get_barrier_semaphore()
    for step in range(1, n_det):
        pl.semaphore_signal(barrier, inc=1, device_id=(tm, lax.rem(det + step, n_det)), device_id_type=MESH)

    @pl.when(has_low)
    def _():
        pl.semaphore_signal(barrier, inc=1, device_id=(tm - 1, det), device_id_type=MESH)

    @pl.when(has_high)
    def _():
        pl.semaphore_signal(barrier, inc=1, device_id=(tm + 1, det), device_id_type=MESH)

    live_rows(tile_ref, count_ref, rows_ref)
    pl.semaphore_wait(barrier, n_det - 1 + has_low.astype(jnp.int32) + has_high.astype(jnp.int32))
    start_edges(n_tm, n_det, width, x_ref, low_ref, high_ref, all_ref, rows_ref, *sems)()


def edge_sems(n_det):
    return [
        pltpu.SemaphoreType.DMA((n_det,)),
        pltpu.SemaphoreType.DMA((n_det,)),
        pltpu.SemaphoreType.DMA((2,)),
        pltpu.SemaphoreType.DMA((2,)),
        pltpu.SemaphoreType.DMA,
    ]


def exchange_edges(n_tm, n_det, width, x, tile, count):
    vmem = pl.BlockSpec(memory_space=VMEM)
    halo = jax.ShapeDtypeStruct((x.shape[0], width), x.dtype)
    return pl.pallas_call(
        functools.partial(edge_kernel, n_tm, n_det, width),
        out_shape=(halo, halo, jax.ShapeDtypeStruct((n_det,) + tile.shape, tile.dtype)),
        in_specs=[pl.BlockSpec(memory_space=pl.ANY), vmem, pl.BlockSpec(memory_space=pltpu.SMEM)],
        out_specs=(vmem,) * 3,
        scratch_shapes=[
            VMEM(tile.shape, tile.dtype),
        ] + edge_sems(n_det),
        compiler_params=pltpu.CompilerParams(collective_id=0, has_side_effects=True),
        name="edges",
    )(x, tile, count)


def fast_path(n_tm, n_det, half, fd, ft, x):
    width = 2 * half
    return (
        n_det % 2 == 0 and n_tm * TILE_DEV == 8 and x.shape[0] == LANES and width == LANES and x.shape[1] == half * LANES
        and fd == ft and half == 2 * ft and (x.shape[1] // ft) % (4 * n_det) == 0)


def load_blocks(half, x_hbm, x_ref, load_sem, cur, mid, pitch):
    dets, samples = x_ref.shape
    width = 2 * half
    pieces = load_sem.shape[0]
    span = samples // pieces
    loads = []
    for piece in range(pieces):
        part = pl.ds(piece * span, span)
        load = pltpu.make_async_copy(x_hbm.at[:, part], x_ref.at[:, part], load_sem.at[piece])
        load.start()
        loads.append(load)

    def finish():
        per = span // width
        for piece, load in enumerate(loads):
            load.wait()
            for b in range(piece * per, (piece + 1) * per):
                at = b * width
                cur[b * pitch:b * pitch + dets, :] = x_ref[:, at:at + width].astype(F32)
                if b:
                    mid[b * pitch:b * pitch + dets, :] = x_ref[:, at - half:at + half].astype(F32)

    return finish


def edge_blocks(half, x_ref, low_ref, high_ref, cur, mid, pitch):
    dets, samples = x_ref.shape
    last = samples // (2 * half) * pitch
    first = jnp.concatenate([low_ref[:, half:], x_ref[:, 0:half]], axis=1)
    mid[0:dets, :] = first.astype(F32)
    mid[last:last + dets, :] = jnp.concatenate([x_ref[:, samples - half:], high_ref[:, 0:half]], axis=1).astype(F32)
    cur[last:last + dets, :] = high_ref[...].astype(F32)


def spread_taps(tapst_ref, wide, taps_ref):
    wide[...] = jnp.zeros(wide.shape, F32)
    wide[0:tapst_ref.shape[0], :] = tapst_ref[...].astype(F32)
    taps_ref[...] = wide[...].T


def owner_order(n_tm, n_det, owner_ref, tiles):
    across_owner = jnp.broadcast_to(owner_ref[...].astype(F32), (tiles, tiles))
    down = lax.broadcasted_iota(jnp.int32, (tiles, tiles), 0)
    across_tile = lax.broadcasted_iota(jnp.int32, (tiles, tiles), 1)
    earlier = (across_owner.T == across_owner) & (down < across_tile)
    rank = jnp.sum(jnp.where(earlier, 1.0, 0.0), axis=0, keepdims=True)
    place = across_owner * TILE_DEV + rank
    group = n_tm * TILE_DEV
    inner = down % group
    wanted = (inner // TILE_DEV * n_det + down // group) * TILE_DEV + inner % TILE_DEV
    order = jnp.sum(jnp.where(place == wanted.astype(F32), across_tile.astype(F32), 0.0), axis=1, keepdims=True)
    return jnp.broadcast_to(order, (tiles, LANES))


def filter_chunks(half, ft, core, cur, mid, pitch, taps_ref, stage, kept, sent, send):
    chunks, frames, unroll, _ = sent.shape
    dets = chunks * unroll
    blocks = LANES // 2
    step_rows = stage.shape[1] // ft

    def chunk_step(c, carry):
        for k in range(unroll):
            d = c * unroll + k
            spread = jnp.broadcast_to(taps_ref[pl.ds(d, 1), :], (half, 4 * half))
            matrix = pltpu.roll(spread, 0, 1, stride=1, stride_axis=0).astype(BF16)
            rows = []
            for source in (mid, cur):
                lower = source[pl.ds(d, blocks, stride=pitch), :]
                upper = source[pl.ds(d + pitch, blocks, stride=pitch), :]
                rows.append(jnp.concatenate([lower, upper], axis=1))
            window = jnp.concatenate(rows, axis=0).astype(BF16)
            result = lax.dot_general(matrix, window, CONTRACT, preferred_element_type=F32)
            for q in range(2):
                stage[q, pl.ds(k, ft, stride=step_rows), :] = result[q * ft:(q + 1) * ft, :]
        at = pl.multiple_of(core * dets + c * unroll, unroll)
        for f in range(frames):
            rows = slice(f * step_rows, f * step_rows + unroll)
            kept[f, pl.ds(at, unroll), :] = stage[core, rows, :].astype(BF16)
            sent[c, f] = stage[1 - core, rows, :].astype(BF16)
        send(c).start()
        return carry

    lax.fori_loop(0, chunks, chunk_step, 0)


def pick_frames(core, fd, ft, order, rows_ref, picks):
    segments, rows, width = rows_ref.shape
    tiles = order.shape[0]
    per_row = width // fd
    spans = LANES // 2 // segments
    lane = lax.broadcasted_iota(jnp.int32, (LANES, per_row * LANES), 1)
    at = lax.broadcasted_iota(jnp.int32, (LANES, per_row * LANES), 0)
    h, inner = lane // LANES, lane % LANES
    p, m = inner // (LANES // 2), inner % (LANES // 2)
    target = (m // spans) * width + h * fd + 4 * (m % spans) + 2 * p + core - at
    found = jnp.zeros((2 * rows, per_row * LANES), F32)
    for s in range(segments):
        one = jnp.where(target == s * width, 1.0, 0.0).astype(BF16)
        tile = rows_ref[s].astype(F32)
        found += jnp.dot(jnp.concatenate([tile, tile], axis=0).astype(BF16), one, preferred_element_type=F32)
    for r in range(rows):
        for k in range(per_row):
            g = r * per_row + k
            picks[:, g * LANES:(g + 1) * LANES] = jnp.where(
                order == found[r:r + 1, k * LANES:(k + 1) * LANES], 1.0, 0.0).astype(BF16)


def whiten(fd, half, prec_ref, kept, whitened):
    frames = kept.shape[0]
    across = LANES // fd
    low = frames // across
    groups = prec_ref.shape[0] // fd
    for u in range(half * low // 2, (half + 1) * low // 2):
        for v in range(0, across, 2):
            weight = jnp.concatenate([kept[(v + i) * low + u] for i in range(2)], axis=1)
            result = jnp.dot(prec_ref[...], weight, preferred_element_type=F32).astype(BF16)
            for i in range(2):
                at = (u * across + v + i) * fd
                for g in range(groups):
                    whitened[at:at + fd, g * LANES:(g + 1) * LANES] = (
                        result[g * fd:(g + 1) * fd, i * LANES:(i + 1) * LANES])


def tile_sums(half, picks, whitened, out_ref):
    peers = out_ref.shape[1]
    rows = picks.shape[0] // peers
    size = whitened.shape[0] // 2
    wide = 2 * LANES
    for n in range(size // wide):
        at = half * size + n * wide
        sums = lax.dot_general(picks[...], whitened[at:at + wide, :], CONTRACT, preferred_element_type=F32)
        for j in range(peers):
            both = [sums[j * rows:(j + 1) * rows, i * LANES:(i + 1) * LANES] for i in range(2)]
            out_ref[half, j, n * 2 * rows:(n + 1) * 2 * rows, :] = jnp.concatenate(both, axis=0).astype(out_ref.dtype)


CHUNK = 32
PITCH = 4


def partial_scratch(half, fd, ft, tiles, x, precision):
    dets, samples = x.shape
    width = 2 * half
    blocks = (samples // width + 1) * (dets + PITCH)
    chunks = dets // CHUNK
    return [
        VMEM(x.shape, BF16),
        VMEM((precision.shape[0], 2 * dets), BF16),
        pltpu.SemaphoreType.DMA((4,)),
        pltpu.SemaphoreType.DMA,
        pltpu.SemaphoreType.DMA((chunks,)),
        pltpu.SemaphoreType.DMA((chunks,)),
        VMEM((2 * width, dets), F32),
        VMEM((dets, 2 * width), F32),
        VMEM((blocks, width), F32),
        VMEM((blocks, width), F32),
        VMEM((2, ft * (CHUNK + 1), LANES), F32),
        VMEM((ft, 2 * dets, LANES), BF16),
        VMEM((chunks, ft, CHUNK, LANES), BF16),
        VMEM((tiles, precision.shape[0] // fd * LANES), BF16),
        VMEM((ft * fd, precision.shape[0] // fd * LANES), BF16),
    ]


def part_shape(fd, ft, tiles):
    return (tiles // TILE_DEV, TILE_DEV * ft // (LANES // fd), LANES)


def plain_partial_sums(x, low, high, taps, rows, owner, precision, half, fd, ft, tiles):
    dets, samples = x.shape
    width = 2 * half
    groups = precision.shape[0] // fd
    blocks = samples // width
    padded = jnp.concatenate([low[:, -half:], x, high[:, :half]], axis=1).reshape(dets, blocks + 1, width)
    length = 4 * half + 1
    tiled = jnp.broadcast_to(jnp.pad(taps, ((0, 0), (0, length - taps.shape[1])))[:, None, :], (dets, width, length))
    matrix = tiled.reshape(dets, width * length)[:, :width * 2 * width].reshape(dets, width, 2 * width)
    near = jnp.einsum("dbj,dij->dbi", padded, matrix[:, :, :width], preferred_element_type=F32)
    far = jnp.einsum("dbj,dij->dbi", padded, matrix[:, :, width:], preferred_element_type=F32)
    filtered = (near[:, :-1] + far[:, 1:]).astype(BF16).reshape(dets, samples // ft, ft)
    order = jnp.argsort(owner_rows(owner)).astype(jnp.int32)
    rows = rows.reshape(rows.shape[0], groups, -1).transpose(1, 0, 2).reshape(groups, 1, -1)
    picks = (rows == order[None, :, None]).astype(BF16)
    sums = jnp.einsum("gkt,dtf->gkfd", picks, filtered, preferred_element_type=F32).astype(BF16)
    out = jnp.einsum("gkfd,gad->kfa", sums, precision.reshape(groups, fd, dets), preferred_element_type=F32)
    across = LANES // fd
    low_part = ft // across
    out = out.reshape(tiles, across, low_part, fd).transpose(0, 2, 1, 3)
    return out.reshape(tiles // TILE_DEV, TILE_DEV * low_part, LANES).astype(BF16)


def peer(me, step, n_tm, n_det):
    other = lax.rem(me + step, n_tm * n_det)
    return other, (other // n_det, lax.rem(other, n_det))


def greet(n_tm, n_det):
    me = lax.axis_index("tm") * n_det + lax.axis_index("det")
    barrier = pltpu.get_barrier_semaphore()
    for step in range(1, n_tm * n_det):
        pl.semaphore_signal(barrier, inc=1, device_id=peer(me, step, n_tm, n_det)[1], device_id_type=MESH)
    return me, barrier


def gather_body(n_tm, n_det, me, part_ref, left_ref, right_ref, out_ref, held, send_sem, recv_sem, own_sem):
    count = n_tm * n_det
    fd = left_ref.shape[0]
    copies = []
    far = range(n_det, count)
    for step in [*far, *range(1, n_det)]:
        other, where = peer(me, step, n_tm, n_det)
        copy = pltpu.make_async_remote_copy(
            src_ref=part_ref.at[other], dst_ref=held.at[me], send_sem=send_sem.at[step], recv_sem=recv_sem.at[step],
            device_id=where, device_id_type=MESH)
        copy.start()
        copies.append(copy)
    own = pltpu.make_async_copy(part_ref.at[me], held.at[me], own_sem)
    own.start()
    own.wait()
    for copy in copies:
        copy.wait()
    total = jnp.sum(held[...].astype(F32), axis=0)
    low = total.shape[0] // TILE_DEV
    across = total.shape[1] // fd
    tiles = []
    for k in range(TILE_DEV):
        tile = total[k * low:(k + 1) * low, :]
        stacked = jnp.concatenate([tile[:, v * fd:(v + 1) * fd] for v in range(across)], axis=0)
        rows = jnp.dot(stacked, left_ref[...], precision=lax.Precision.HIGHEST, preferred_element_type=F32)
        tiles.append(lax.dot_general(
            rows, right_ref[...], (((0,), (0,)), ((), ())), precision=lax.Precision.HIGHEST,
            preferred_element_type=F32))
    width = right_ref.shape[1]
    for i in range(left_ref.shape[1]):
        out_ref[:, i * width:(i + 1) * width] = jnp.concatenate([tile[i:i + 1, :] for tile in tiles], axis=0)


def gather_kernel(n_tm, n_det, part_ref, left_ref, right_ref, out_ref, *scratch):
    me, barrier = greet(n_tm, n_det)
    pl.semaphore_wait(barrier, n_tm * n_det - 1)
    gather_body(n_tm, n_det, me, part_ref, left_ref, right_ref, out_ref, *scratch)


def greet_lines(n_tm, n_det):
    tm, det = lax.axis_index("tm"), lax.axis_index("det")
    barrier = pltpu.get_barrier_semaphore()
    for step in range(1, n_tm):
        pl.semaphore_signal(barrier, inc=1, device_id=(lax.rem(tm + step, n_tm), det), device_id_type=MESH)
    for step in range(1, n_det):
        pl.semaphore_signal(barrier, inc=1, device_id=(tm, lax.rem(det + step, n_det)), device_id_type=MESH)
    return lambda: pl.semaphore_wait(barrier, n_tm + n_det - 2)


def send_parts(n_det, half, part, held, send_sem, recv_sem, own_sem):
    tm, det = lax.axis_index("tm"), lax.axis_index("det")
    copies = []
    for step in range(1, n_det):
        other = lax.rem(det + step, n_det)
        copies.append(pltpu.make_async_remote_copy(
            src_ref=part.at[half, other], dst_ref=held.at[half, det], send_sem=send_sem.at[half, step],
            recv_sem=recv_sem.at[half, step], device_id=(tm, other), device_id_type=MESH))
    copies.append(pltpu.make_async_copy(part.at[half, det], held.at[half, det], own_sem.at[half]))
    for copy in copies:
        copy.start()
    return copies


def send_sums(n_tm, half, copies, held, sums, line, last, send_sem, recv_sem, own_sem):
    tm, det = lax.axis_index("tm"), lax.axis_index("det")
    for copy in copies:
        copy.wait()
    sums[half] = jnp.sum(held[half].astype(F32), axis=0)
    rows = n_tm * TILE_DEV
    low = sums.shape[1] // rows
    for z in range(n_tm):
        mine = [sums[half, pl.ds(z * TILE_DEV + k, low, stride=rows), :] for k in range(TILE_DEV)]
        line[half, z] = jnp.concatenate(mine, axis=0)
    copies = []
    for step in range(1, n_tm):
        other = lax.rem(tm + step, n_tm)
        copies.append(pltpu.make_async_remote_copy(
            src_ref=line.at[half, other], dst_ref=last.at[half, tm], send_sem=send_sem.at[half, step],
            recv_sem=recv_sem.at[half, step], device_id=(other, det), device_id_type=MESH))
    copies.append(pltpu.make_async_copy(line.at[half, tm], last.at[half, tm], own_sem.at[half]))
    for copy in copies:
        copy.start()
    return copies


def whole_kernel(n_tm, n_det, sizes, x_hbm, tapst_ref, owner_ref, prec_hbm, tile_ref, count_ref, out_ref, low, high, held_rows, own_rows, *rest):
    half, fd, ft, tiles = sizes
    edge, reduce = rest[:5], rest[5:15]
    (x_ref, prec_ref, load_sem, prec_sem, pair_send, pair_recv, wide, taps_ref, cur, mid, stage, kept, sent, picks,
     whitened) = rest[15:]
    part, held, part_send, part_recv, part_own, sums, line, last, line_sems, line_own = reduce
    tm, det = lax.axis_index("tm"), lax.axis_index("det")
    core = lax.rem(det, 2)
    dets = x_ref.shape[0]
    pitch = dets + PITCH
    unroll = sent.shape[2]
    build = load_blocks(half, x_hbm, x_ref, load_sem, cur, mid, pitch)
    first = pl.multiple_of((det - core) * dets, 2 * dets)
    load = pltpu.make_async_copy(prec_hbm.at[:, pl.ds(first, 2 * dets)], prec_ref, prec_sem)
    load.start()
    meet = greet_lines(n_tm, n_det)
    live_rows(tile_ref, count_ref, own_rows)
    meet()
    finish = start_edges(n_tm, n_det, 2 * half, x_hbm, low, high, held_rows, own_rows, *edge)
    spread_taps(tapst_ref, wide, taps_ref)
    build()
    finish()
    edge_blocks(half, x_ref, low, high, cur, mid, pitch)

    def send(c):
        at = pl.multiple_of(core * dets + c * unroll, unroll)
        return pltpu.make_async_remote_copy(
            src_ref=sent.at[c], dst_ref=kept.at[:, pl.ds(at, unroll), :], send_sem=pair_send.at[c],
            recv_sem=pair_recv.at[c], device_id=(tm, det + 1 - 2 * core), device_id_type=MESH)

    filter_chunks(half, ft, core, cur, mid, pitch, taps_ref, stage, kept, sent, send)
    pick_frames(core, fd, ft, owner_order(n_tm, n_det, owner_ref, tiles), held_rows, picks)
    load.wait()
    for c in range(sent.shape[0]):
        send(c).wait()
    waits = []
    for h in range(2):
        whiten(fd, h, prec_ref, kept, whitened)
        tile_sums(h, picks, whitened, part)
        waits.append(send_parts(n_det, h, part, held, part_send, part_recv, part_own))
    waits = [
        send_sums(n_tm, h, waits[h], held, sums, line, last, line_sems.at[0], line_sems.at[1], line_own)
        for h in range(2)]
    for h in range(2):
        for copy in waits[h]:
            copy.wait()
        out_ref[h] = jnp.sum(last[h], axis=0)


def reduce_scratch(n_tm, n_det, fd, ft):
    rows = n_tm * TILE_DEV * ft * fd // LANES // 2
    mine = rows // n_tm
    return [
        VMEM((2, n_det, rows, LANES), BF16),
        VMEM((2, n_det, rows, LANES), BF16),
        pltpu.SemaphoreType.DMA((2, n_det)),
        pltpu.SemaphoreType.DMA((2, n_det)),
        pltpu.SemaphoreType.DMA((2,)),
        VMEM((2, rows, LANES), F32),
        VMEM((2, n_tm, mine, LANES), F32),
        VMEM((2, n_tm, mine, LANES), F32),
        pltpu.SemaphoreType.DMA((2, 2, n_tm)),
        pltpu.SemaphoreType.DMA((2,)),
    ]


def project_kernel(sums_ref, left_ref, right_ref, out_ref):
    fd = left_ref.shape[0]
    low = sums_ref.shape[1] // TILE_DEV
    tiles = []
    for k in range(TILE_DEV):
        tile = jnp.concatenate([sums_ref[h, k * low:(k + 1) * low, :] for h in range(2)], axis=0)
        stacked = jnp.concatenate([tile[:, v * fd:(v + 1) * fd] for v in range(LANES // fd)], axis=0)
        rows = jnp.dot(stacked, left_ref[...], precision=lax.Precision.HIGHEST, preferred_element_type=F32)
        tiles.append(lax.dot_general(
            rows, right_ref[...], (((0,), (0,)), ((), ())), precision=lax.Precision.HIGHEST,
            preferred_element_type=F32))
    width = right_ref.shape[1]
    for i in range(left_ref.shape[1]):
        out_ref[:, i * width:(i + 1) * width] = jnp.concatenate([tile[i:i + 1, :] for tile in tiles], axis=0)


def gather_scratch(count, shape):
    return [
        VMEM(shape, BF16),
        pltpu.SemaphoreType.DMA((count,)),
        pltpu.SemaphoreType.DMA((count,)),
        pltpu.SemaphoreType.DMA,
    ]


def call(kernel, specs, inputs, scratch, out, name):
    return pl.pallas_call(
        kernel,
        out_shape=jax.ShapeDtypeStruct(out, F32),
        in_specs=[pl.BlockSpec(memory_space=space) for space in specs],
        out_specs=pl.BlockSpec(memory_space=VMEM),
        scratch_shapes=scratch,
        compiler_params=pltpu.CompilerParams(
            collective_id=1, has_side_effects=True, vmem_limit_bytes=60 * 1024 * 1024),
        name=name,
    )(*inputs)


def local(
    n_tm, n_det,
    time_stream, filter_taps, det_precision, left_weight, right_weight, frame_tile, tile_owner, frame_count,
):
    half = filter_taps.shape[1] // 2
    fd, ft = left_weight.shape[1], right_weight.shape[1]
    dets = time_stream.shape[0]
    tiles = tile_owner.shape[0]
    count = n_tm * n_det
    tile = frame_tile.reshape(-1, LANES)
    sizes = (half, fd, ft, tiles)
    shape = part_shape(fd, ft, tiles)
    flat = left_weight.shape[0] * right_weight.shape[0]
    weights = (left_weight.T, right_weight.T)
    gather = gather_scratch(count, shape)
    if fast_path(n_tm, n_det, half, fd, ft, time_stream):
        inputs = (time_stream, filter_taps.T, tile_owner.reshape(1, -1), det_precision, tile, frame_count)
        specs = (pl.ANY, VMEM, VMEM, pl.ANY, VMEM, pltpu.SMEM)
        halo = VMEM((dets, 2 * half), BF16)
        scratch = [halo, halo, VMEM((n_det,) + tile.shape, tile.dtype), VMEM(tile.shape, tile.dtype)]
        scratch += edge_sems(n_det) + reduce_scratch(n_tm, n_det, fd, ft)
        scratch += partial_scratch(half, fd, ft, tiles, time_stream, det_precision)
        out = (2, TILE_DEV * ft * fd // LANES // 2, LANES)
        sums = call(functools.partial(whole_kernel, n_tm, n_det, sizes), specs, inputs, scratch, out, "whole")
        return pl.pallas_call(
            project_kernel,
            out_shape=jax.ShapeDtypeStruct((TILE_DEV, flat), F32),
            in_specs=[pl.BlockSpec(memory_space=VMEM)] * 3,
            out_specs=pl.BlockSpec(memory_space=VMEM),
            name="project",
        )(sums, *weights)
    low, high, rows = exchange_edges(n_tm, n_det, 2 * half, time_stream, tile, frame_count)
    precision = lax.dynamic_slice_in_dim(det_precision, lax.axis_index("det") * dets, dets, axis=1)
    part = plain_partial_sums(time_stream, low, high, filter_taps, rows, tile_owner, precision, *sizes)
    return call(functools.partial(gather_kernel, n_tm, n_det), (VMEM,) * 3, (part,) + weights, gather, (TILE_DEV, flat), "gather")


def solution(mesh):
    return jax.shard_map(
        functools.partial(local, mesh.shape["tm"], mesh.shape["det"]),
        mesh=mesh,
        in_specs=(
            P("det", "tm"),
            P("det", None),
            P(),
            P(),
            P(),
            P(("tm", "det"), None),
            P(),
            P(("tm", "det")),
        ),
        out_specs=P(("tm", "det"), None),
        check_vma=False,
    )
```

```python
import functools

import jax
import jax.numpy as jnp
from jax import lax
from jax.experimental import pallas as pl
from jax.experimental.pallas import tpu as pltpu
from jax.sharding import PartitionSpec as P

TILE_DEV = 2
LANES = 128
MESH = pl.DeviceIdType.MESH
VMEM = pltpu.VMEM
F32 = jnp.float32
BF16 = jnp.bfloat16
CONTRACT = (((1,), (1,)), ((), ()))


def owner_rows(tile_owner):
    total_tiles = tile_owner.shape[0]
    same_owner = tile_owner[:, None] == tile_owner[None, :]
    earlier = jnp.arange(total_tiles)[None, :] < jnp.arange(total_tiles)[:, None]
    slot_rank = jnp.sum((same_owner & earlier).astype(jnp.int32), axis=1)
    return tile_owner * TILE_DEV + slot_rank


def start_edges(n_tm, n_det, width, x_ref, low_ref, high_ref, all_ref, rows_ref, send_sem, recv_sem, halo_send, halo_recv, own_sem):
    tm, det = lax.axis_index("tm"), lax.axis_index("det")
    has_low, has_high = tm > 0, tm < n_tm - 1
    down = pltpu.make_async_remote_copy(
        src_ref=x_ref.at[:, 0:width], dst_ref=high_ref, send_sem=halo_send.at[0], recv_sem=halo_recv.at[0],
        device_id=(tm - 1, det), device_id_type=MESH)
    up = pltpu.make_async_remote_copy(
        src_ref=x_ref.at[:, x_ref.shape[1] - width:], dst_ref=low_ref, send_sem=halo_send.at[1], recv_sem=halo_recv.at[1],
        device_id=(tm + 1, det), device_id_type=MESH)

    @pl.when(has_low)
    def _():
        down.start()

    @pl.when(has_high)
    def _():
        up.start()

    copies = []
    for step in range(1, n_det):
        copy = pltpu.make_async_remote_copy(
            src_ref=rows_ref, dst_ref=all_ref.at[det], send_sem=send_sem.at[step], recv_sem=recv_sem.at[step],
            device_id=(tm, lax.rem(det + step, n_det)), device_id_type=MESH)
        copy.start()
        copies.append(copy)
    own = pltpu.make_async_copy(rows_ref, all_ref.at[det], own_sem)
    own.start()

    @pl.when(jnp.logical_not(has_low))
    def _():
        low_ref[...] = jnp.zeros_like(low_ref)

    @pl.when(jnp.logical_not(has_high))
    def _():
        high_ref[...] = jnp.zeros_like(high_ref)

    def finish():
        own.wait()
        for copy in copies:
            copy.wait()

        @pl.when(has_low)
        def _():
            down.wait_send()
            up.wait_recv()

        @pl.when(has_high)
        def _():
            up.wait_send()
            down.wait_recv()

    return finish


def live_rows(tile_ref, count, rows_ref):
    tile = tile_ref[...]
    frame = lax.broadcasted_iota(jnp.int32, tile.shape, 0) * tile.shape[1] + lax.broadcasted_iota(jnp.int32, tile.shape, 1)
    rows_ref[...] = jnp.where(frame < count, tile, -1)


def edge_kernel(n_tm, n_det, width, x_ref, tile_ref, count_ref, low_ref, high_ref, all_ref, rows_ref, *sems):
    tm, det = lax.axis_index("tm"), lax.axis_index("det")
    has_low, has_high = tm > 0, tm < n_tm - 1
    barrier = pltpu.get_barrier_semaphore()
    for step in range(1, n_det):
        pl.semaphore_signal(barrier, inc=1, device_id=(tm, lax.rem(det + step, n_det)), device_id_type=MESH)

    @pl.when(has_low)
    def _():
        pl.semaphore_signal(barrier, inc=1, device_id=(tm - 1, det), device_id_type=MESH)

    @pl.when(has_high)
    def _():
        pl.semaphore_signal(barrier, inc=1, device_id=(tm + 1, det), device_id_type=MESH)

    live_rows(tile_ref, count_ref[0], rows_ref)
    pl.semaphore_wait(barrier, n_det - 1 + has_low.astype(jnp.int32) + has_high.astype(jnp.int32))
    start_edges(n_tm, n_det, width, x_ref, low_ref, high_ref, all_ref, rows_ref, *sems)()


def edge_sems(n_det):
    return [
        pltpu.SemaphoreType.DMA((n_det,)),
        pltpu.SemaphoreType.DMA((n_det,)),
        pltpu.SemaphoreType.DMA((2,)),
        pltpu.SemaphoreType.DMA((2,)),
        pltpu.SemaphoreType.DMA,
    ]


def exchange_edges(n_tm, n_det, width, x, tile, count):
    vmem = pl.BlockSpec(memory_space=VMEM)
    halo = jax.ShapeDtypeStruct((x.shape[0], width), x.dtype)
    return pl.pallas_call(
        functools.partial(edge_kernel, n_tm, n_det, width),
        out_shape=(halo, halo, jax.ShapeDtypeStruct((n_det,) + tile.shape, tile.dtype)),
        in_specs=[pl.BlockSpec(memory_space=pl.ANY), vmem, pl.BlockSpec(memory_space=pltpu.SMEM)],
        out_specs=(vmem,) * 3,
        scratch_shapes=[
            VMEM(tile.shape, tile.dtype),
        ] + edge_sems(n_det),
        compiler_params=pltpu.CompilerParams(collective_id=0, has_side_effects=True),
        name="edges",
    )(x, tile, count)


def fast_path(n_tm, n_det, half, fd, ft, x):
    width = 2 * half
    return (
        n_det % 2 == 0 and x.shape[0] == LANES and width == LANES and x.shape[1] == half * LANES
        and fd == ft and half == 2 * ft and (x.shape[1] // ft) % (4 * n_det) == 0)


def load_blocks(half, x_hbm, x_ref, load_sem, cur, mid, pitch):
    dets, samples = x_ref.shape
    width = 2 * half
    pieces = load_sem.shape[0]
    span = samples // pieces
    loads = []
    for piece in range(pieces):
        part = pl.ds(piece * span, span)
        load = pltpu.make_async_copy(x_hbm.at[:, part], x_ref.at[:, part], load_sem.at[piece])
        load.start()
        loads.append(load)

    def finish():
        per = span // width
        for piece, load in enumerate(loads):
            load.wait()
            for b in range(piece * per, (piece + 1) * per):
                at = b * width
                cur[b * pitch:b * pitch + dets, :] = x_ref[:, at:at + width].astype(F32)
                if b:
                    mid[b * pitch:b * pitch + dets, :] = x_ref[:, at - half:at + half].astype(F32)

    return finish


def edge_blocks(half, x_ref, low_ref, high_ref, cur, mid, pitch):
    dets, samples = x_ref.shape
    last = samples // (2 * half) * pitch
    first = jnp.concatenate([low_ref[:, half:], x_ref[:, 0:half]], axis=1)
    mid[0:dets, :] = first.astype(F32)
    mid[last:last + dets, :] = jnp.concatenate([x_ref[:, samples - half:], high_ref[:, 0:half]], axis=1).astype(F32)
    cur[last:last + dets, :] = high_ref[...].astype(F32)


def spread_taps(tapst_ref, wide, taps_ref):
    wide[...] = jnp.zeros(wide.shape, F32)
    wide[0:tapst_ref.shape[0], :] = tapst_ref[...].astype(F32)
    taps_ref[...] = wide[...].T


def owner_order(owner_ref, tiles):
    across_owner = jnp.broadcast_to(owner_ref[...].astype(F32), (tiles, tiles))
    down = lax.broadcasted_iota(jnp.int32, (tiles, tiles), 0)
    across_tile = lax.broadcasted_iota(jnp.int32, (tiles, tiles), 1)
    earlier = (across_owner.T == across_owner) & (down < across_tile)
    rank = jnp.sum(jnp.where(earlier, 1.0, 0.0), axis=0, keepdims=True)
    place = across_owner * TILE_DEV + rank
    order = jnp.sum(jnp.where(place == down.astype(F32), across_tile.astype(F32), 0.0), axis=1, keepdims=True)
    return jnp.broadcast_to(order, (tiles, LANES))


def filter_chunks(half, ft, core, cur, mid, pitch, taps_ref, stage, kept, sent, send):
    chunks, frames, unroll, _ = sent.shape
    dets = chunks * unroll
    blocks = LANES // 2
    step_rows = stage.shape[1] // ft

    def chunk_step(c, carry):
        for k in range(unroll):
            d = c * unroll + k
            spread = jnp.broadcast_to(taps_ref[pl.ds(d, 1), :], (half, 4 * half))
            matrix = pltpu.roll(spread, 0, 1, stride=1, stride_axis=0).astype(BF16)
            rows = []
            for source in (mid, cur):
                lower = source[pl.ds(d, blocks, stride=pitch), :]
                upper = source[pl.ds(d + pitch, blocks, stride=pitch), :]
                rows.append(jnp.concatenate([lower, upper], axis=1))
            window = jnp.concatenate(rows, axis=0).astype(BF16)
            result = lax.dot_general(matrix, window, CONTRACT, preferred_element_type=F32)
            for q in range(2):
                stage[q, pl.ds(k, ft, stride=step_rows), :] = result[q * ft:(q + 1) * ft, :]
        at = pl.multiple_of(core * dets + c * unroll, unroll)
        for f in range(frames):
            rows = slice(f * step_rows, f * step_rows + unroll)
            kept[f, pl.ds(at, unroll), :] = stage[core, rows, :].astype(BF16)
            sent[c, f] = stage[1 - core, rows, :].astype(BF16)
        send(c).start()
        return carry

    lax.fori_loop(0, chunks, chunk_step, 0)


def pick_frames(core, fd, ft, order, rows_ref, picks):
    segments, rows, width = rows_ref.shape
    tiles = order.shape[0]
    per_row = width // fd
    spans = LANES // 2 // segments
    lane = lax.broadcasted_iota(jnp.int32, (LANES, per_row * LANES), 1)
    at = lax.broadcasted_iota(jnp.int32, (LANES, per_row * LANES), 0)
    h, inner = lane // LANES, lane % LANES
    p, m = inner // (LANES // 2), inner % (LANES // 2)
    target = (m // spans) * width + h * fd + 4 * (m % spans) + 2 * p + core - at
    found = jnp.zeros((2 * rows, per_row * LANES), F32)
    for s in range(segments):
        one = jnp.where(target == s * width, 1.0, 0.0).astype(BF16)
        tile = rows_ref[s].astype(F32)
        found += jnp.dot(jnp.concatenate([tile, tile], axis=0).astype(BF16), one, preferred_element_type=F32)
    for r in range(rows):
        for k in range(per_row):
            g = r * per_row + k
            picks[:, g * LANES:(g + 1) * LANES] = jnp.where(
                order == found[r:r + 1, k * LANES:(k + 1) * LANES], 1.0, 0.0).astype(BF16)


def whiten(fd, half, prec_ref, kept, whitened):
    frames = kept.shape[0]
    across = LANES // fd
    low = frames // across
    groups = prec_ref.shape[0] // fd
    for u in range(half * low // 2, (half + 1) * low // 2):
        for v in range(0, across, 2):
            weight = jnp.concatenate([kept[(v + i) * low + u] for i in range(2)], axis=1)
            result = jnp.dot(prec_ref[...], weight, preferred_element_type=F32).astype(BF16)
            for i in range(2):
                at = (u * across + v + i) * fd
                for g in range(groups):
                    whitened[at:at + fd, g * LANES:(g + 1) * LANES] = (
                        result[g * fd:(g + 1) * fd, i * LANES:(i + 1) * LANES])


def tile_sums(half, picks, whitened, packed, part):
    tiles = picks.shape[0]
    size = whitened.shape[0] // 2
    wide = 2 * LANES
    low = size // LANES
    for n in range(size // wide):
        at = half * size + n * wide
        sums = lax.dot_general(picks[...], whitened[at:at + wide, :], CONTRACT, preferred_element_type=F32)
        for i in range(2):
            packed[half, pl.ds(2 * n + i, tiles, stride=low), :] = sums[:, i * LANES:(i + 1) * LANES]
    rows = part.shape[2]
    for owner in range(part.shape[1]):
        part[half, owner] = packed[half, owner * rows:(owner + 1) * rows, :].astype(part.dtype)


CHUNK = 32
PITCH = 4


def partial_scratch(half, fd, ft, tiles, x, precision):
    dets, samples = x.shape
    width = 2 * half
    blocks = (samples // width + 1) * (dets + PITCH)
    chunks = dets // CHUNK
    return [
        VMEM(x.shape, BF16),
        VMEM((precision.shape[0], 2 * dets), BF16),
        pltpu.SemaphoreType.DMA((4,)),
        pltpu.SemaphoreType.DMA,
        pltpu.SemaphoreType.DMA((chunks,)),
        pltpu.SemaphoreType.DMA((chunks,)),
        VMEM((2 * width, dets), F32),
        VMEM((dets, 2 * width), F32),
        VMEM((blocks, width), F32),
        VMEM((blocks, width), F32),
        VMEM((2, ft * (CHUNK + 1), LANES), F32),
        VMEM((ft, 2 * dets, LANES), BF16),
        VMEM((chunks, ft, CHUNK, LANES), BF16),
        VMEM((tiles, precision.shape[0] // fd * LANES), BF16),
        VMEM((ft * fd, precision.shape[0] // fd * LANES), BF16),
    ]


def part_shape(fd, ft, tiles):
    return (tiles // TILE_DEV, TILE_DEV * ft // (LANES // fd), LANES)


def plain_partial_sums(x, low, high, taps, rows, owner, precision, half, fd, ft, tiles):
    dets, samples = x.shape
    width = 2 * half
    groups = precision.shape[0] // fd
    blocks = samples // width
    padded = jnp.concatenate([low[:, -half:], x, high[:, :half]], axis=1).reshape(dets, blocks + 1, width)
    length = 4 * half + 1
    tiled = jnp.broadcast_to(jnp.pad(taps, ((0, 0), (0, length - taps.shape[1])))[:, None, :], (dets, width, length))
    matrix = tiled.reshape(dets, width * length)[:, :width * 2 * width].reshape(dets, width, 2 * width)
    near = jnp.einsum("dbj,dij->dbi", padded, matrix[:, :, :width], preferred_element_type=F32)
    far = jnp.einsum("dbj,dij->dbi", padded, matrix[:, :, width:], preferred_element_type=F32)
    filtered = (near[:, :-1] + far[:, 1:]).astype(BF16).reshape(dets, samples // ft, ft)
    order = jnp.argsort(owner_rows(owner)).astype(jnp.int32)
    rows = rows.reshape(rows.shape[0], groups, -1).transpose(1, 0, 2).reshape(groups, 1, -1)
    picks = (rows == order[None, :, None]).astype(BF16)
    sums = jnp.einsum("gkt,dtf->gkfd", picks, filtered, preferred_element_type=F32).astype(BF16)
    out = jnp.einsum("gkfd,gad->kfa", sums, precision.reshape(groups, fd, dets), preferred_element_type=F32)
    across = LANES // fd
    low_part = ft // across
    out = out.reshape(tiles, across, low_part, fd).transpose(0, 2, 1, 3)
    return out.reshape(tiles // TILE_DEV, TILE_DEV * low_part, LANES).astype(BF16)


def peer(me, step, n_tm, n_det):
    other = lax.rem(me + step, n_tm * n_det)
    return other, (other // n_det, lax.rem(other, n_det))


def greet(n_tm, n_det):
    me = lax.axis_index("tm") * n_det + lax.axis_index("det")
    barrier = pltpu.get_barrier_semaphore()
    for step in range(1, n_tm * n_det):
        pl.semaphore_signal(barrier, inc=1, device_id=peer(me, step, n_tm, n_det)[1], device_id_type=MESH)
    return me, barrier


def gather_body(n_tm, n_det, me, part_ref, left_ref, right_ref, out_ref, held, send_sem, recv_sem, own_sem):
    count = n_tm * n_det
    fd = left_ref.shape[0]
    copies = []
    far = range(n_det, count)
    for step in [*far, *range(1, n_det)]:
        other, where = peer(me, step, n_tm, n_det)
        copy = pltpu.make_async_remote_copy(
            src_ref=part_ref.at[other], dst_ref=held.at[me], send_sem=send_sem.at[step], recv_sem=recv_sem.at[step],
            device_id=where, device_id_type=MESH)
        copy.start()
        copies.append(copy)
    own = pltpu.make_async_copy(part_ref.at[me], held.at[me], own_sem)
    own.start()
    own.wait()
    for copy in copies:
        copy.wait()
    total = jnp.sum(held[...].astype(F32), axis=0)
    low = total.shape[0] // TILE_DEV
    across = total.shape[1] // fd
    tiles = []
    for k in range(TILE_DEV):
        tile = total[k * low:(k + 1) * low, :]
        stacked = jnp.concatenate([tile[:, v * fd:(v + 1) * fd] for v in range(across)], axis=0)
        rows = jnp.dot(stacked, left_ref[...], precision=lax.Precision.HIGHEST, preferred_element_type=F32)
        tiles.append(lax.dot_general(
            rows, right_ref[...], (((0,), (0,)), ((), ())), precision=lax.Precision.HIGHEST,
            preferred_element_type=F32))
    width = right_ref.shape[1]
    for i in range(left_ref.shape[1]):
        out_ref[:, i * width:(i + 1) * width] = jnp.concatenate([tile[i:i + 1, :] for tile in tiles], axis=0)


def gather_kernel(n_tm, n_det, part_ref, left_ref, right_ref, out_ref, *scratch):
    me, barrier = greet(n_tm, n_det)
    pl.semaphore_wait(barrier, n_tm * n_det - 1)
    gather_body(n_tm, n_det, me, part_ref, left_ref, right_ref, out_ref, *scratch)


def greet_lines(n_tm, n_det):
    tm, det = lax.axis_index("tm"), lax.axis_index("det")
    barrier = pltpu.get_barrier_semaphore()
    for step in range(1, n_tm):
        pl.semaphore_signal(barrier, inc=1, device_id=(lax.rem(tm + step, n_tm), det), device_id_type=MESH)
    for step in range(1, n_det):
        pl.semaphore_signal(barrier, inc=1, device_id=(tm, lax.rem(det + step, n_det)), device_id_type=MESH)
    return lambda: pl.semaphore_wait(barrier, n_tm + n_det - 2)


def send_parts(n_tm, n_det, half, part, held, send_sem, recv_sem, own_sem):
    me = lax.axis_index("tm") * n_det + lax.axis_index("det")
    count = n_tm * n_det
    copies = []
    for step in [*range(n_det, count), *range(1, n_det)]:
        other, where = peer(me, step, n_tm, n_det)
        copies.append(pltpu.make_async_remote_copy(
            src_ref=part.at[half, other], dst_ref=held.at[half, me], send_sem=send_sem.at[half, step],
            recv_sem=recv_sem.at[half, step], device_id=where, device_id_type=MESH))
    copies.append(pltpu.make_async_copy(part.at[half, me], held.at[half, me], own_sem.at[half]))
    for copy in copies:
        copy.start()
    return copies


def whole_kernel(n_tm, n_det, sizes, x_hbm, tapst_hbm, owner_hbm, prec_hbm, tile_hbm, count_hbm, out_ref, low, high, held_rows, own_rows, *rest):
    half, fd, ft, tiles = sizes
    edge, rest = rest[:5], rest[5:]
    (part, held, part_send, part_recv, part_own, packed, planes, tapst_ref, owner_ref, tile_ref, count_ref, small_sem), rest = rest[:12], rest[12:]
    (x_ref, prec_ref, load_sem, prec_sem, pair_send, pair_recv, wide, taps_ref, cur, mid, stage, kept, sent, picks,
     whitened) = rest
    tm, det = lax.axis_index("tm"), lax.axis_index("det")
    core = lax.rem(det, 2)
    dets = x_ref.shape[0]
    pitch = dets + PITCH
    unroll = sent.shape[2]
    meet = greet_lines(n_tm, n_det)
    small = [
        pltpu.make_async_copy(source, target, small_sem.at[i]) for i, (source, target) in enumerate((
            (tile_hbm, tile_ref), (count_hbm, count_ref), (tapst_hbm, tapst_ref), (owner_hbm, owner_ref)))]
    for copy in small:
        copy.start()
    build = load_blocks(half, x_hbm, x_ref, load_sem, cur, mid, pitch)
    first = pl.multiple_of((det - core) * dets, 2 * dets)
    load = pltpu.make_async_copy(prec_hbm.at[:, pl.ds(first, 2 * dets)], prec_ref, prec_sem)
    load.start()
    small[0].wait()
    small[1].wait()
    live_rows(tile_ref, count_ref[0], own_rows)
    meet()
    finish = start_edges(n_tm, n_det, 2 * half, x_hbm, low, high, held_rows, own_rows, *edge)
    for step in range(1, n_tm):
        pl.semaphore_signal(planes, inc=1, device_id=(lax.rem(tm + step, n_tm), det), device_id_type=MESH)
    small[2].wait()
    spread_taps(tapst_ref, wide, taps_ref)
    build()
    finish()
    edge_blocks(half, x_ref, low, high, cur, mid, pitch)

    def send(c):
        at = pl.multiple_of(core * dets + c * unroll, unroll)
        return pltpu.make_async_remote_copy(
            src_ref=sent.at[c], dst_ref=kept.at[:, pl.ds(at, unroll), :], send_sem=pair_send.at[c],
            recv_sem=pair_recv.at[c], device_id=(tm, det + 1 - 2 * core), device_id_type=MESH)

    filter_chunks(half, ft, core, cur, mid, pitch, taps_ref, stage, kept, sent, send)
    small[3].wait()
    pick_frames(core, fd, ft, owner_order(owner_ref, tiles), held_rows, picks)
    load.wait()
    for c in range(sent.shape[0]):
        send(c).wait()
    waits = []
    for h in range(2):
        whiten(fd, h, prec_ref, kept, whitened)
        tile_sums(h, picks, whitened, packed, part)
        if h == 0:
            pl.semaphore_wait(planes, n_tm - 1)
        waits.append(send_parts(n_tm, n_det, h, part, held, part_send, part_recv, part_own))
    for h in range(2):
        for copy in waits[h]:
            copy.wait()
        out_ref[h] = jnp.sum(held[h].astype(F32), axis=0)


def reduce_scratch(count, fd, ft, tiles, small, live):
    rows = TILE_DEV * ft * fd // LANES // 2
    return [
        VMEM((2, count, rows, LANES), BF16),
        VMEM((2, count, rows, LANES), BF16),
        pltpu.SemaphoreType.DMA((2, count)),
        pltpu.SemaphoreType.DMA((2, count)),
        pltpu.SemaphoreType.DMA((2,)),
        VMEM((2, count * rows, LANES), F32),
        pltpu.SemaphoreType.REGULAR,
    ] + [VMEM(array.shape, array.dtype) for array in small] + [
        pltpu.SMEM(live.shape, live.dtype),
        pltpu.SemaphoreType.DMA((len(small) + 1,)),
    ]


def project_kernel(sums_ref, left_ref, right_ref, out_ref):
    fd = left_ref.shape[0]
    low = sums_ref.shape[1] // TILE_DEV
    tiles = []
    for k in range(TILE_DEV):
        tile = jnp.concatenate([sums_ref[h, k * low:(k + 1) * low, :] for h in range(2)], axis=0)
        stacked = jnp.concatenate([tile[:, v * fd:(v + 1) * fd] for v in range(LANES // fd)], axis=0)
        rows = jnp.dot(stacked, left_ref[...], precision=lax.Precision.HIGHEST, preferred_element_type=F32)
        tiles.append(lax.dot_general(
            rows, right_ref[...], (((0,), (0,)), ((), ())), precision=lax.Precision.HIGHEST,
            preferred_element_type=F32))
    width = right_ref.shape[1]
    for i in range(left_ref.shape[1]):
        out_ref[:, i * width:(i + 1) * width] = jnp.concatenate([tile[i:i + 1, :] for tile in tiles], axis=0)


def gather_scratch(count, shape):
    return [
        VMEM(shape, BF16),
        pltpu.SemaphoreType.DMA((count,)),
        pltpu.SemaphoreType.DMA((count,)),
        pltpu.SemaphoreType.DMA,
    ]


def call(kernel, specs, inputs, scratch, out, name):
    return pl.pallas_call(
        kernel,
        out_shape=jax.ShapeDtypeStruct(out, F32),
        in_specs=[pl.BlockSpec(memory_space=space) for space in specs],
        out_specs=pl.BlockSpec(memory_space=VMEM),
        scratch_shapes=scratch,
        compiler_params=pltpu.CompilerParams(
            collective_id=1, has_side_effects=True, vmem_limit_bytes=60 * 1024 * 1024),
        name=name,
    )(*inputs)


def local(
    n_tm, n_det,
    time_stream, filter_taps, det_precision, left_weight, right_weight, frame_tile, tile_owner, frame_count,
):
    half = filter_taps.shape[1] // 2
    fd, ft = left_weight.shape[1], right_weight.shape[1]
    dets = time_stream.shape[0]
    tiles = tile_owner.shape[0]
    count = n_tm * n_det
    tile = frame_tile.reshape(-1, LANES)
    sizes = (half, fd, ft, tiles)
    shape = part_shape(fd, ft, tiles)
    flat = left_weight.shape[0] * right_weight.shape[0]
    weights = (left_weight.T, right_weight.T)
    gather = gather_scratch(count, shape)
    if fast_path(n_tm, n_det, half, fd, ft, time_stream):
        taps, owner = filter_taps.T, tile_owner.reshape(1, -1)
        inputs = (time_stream, taps, owner, det_precision, tile, frame_count)
        specs = (pl.ANY,) * len(inputs)
        halo = VMEM((dets, 2 * half), BF16)
        scratch = [halo, halo, VMEM((n_det,) + tile.shape, tile.dtype), VMEM(tile.shape, tile.dtype)]
        scratch += edge_sems(n_det) + reduce_scratch(count, fd, ft, tiles, (taps, owner, tile), frame_count)
        scratch += partial_scratch(half, fd, ft, tiles, time_stream, det_precision)
        out = (2, TILE_DEV * ft * fd // LANES // 2, LANES)
        sums = call(functools.partial(whole_kernel, n_tm, n_det, sizes), specs, inputs, scratch, out, "whole")
        return pl.pallas_call(
            project_kernel,
            out_shape=jax.ShapeDtypeStruct((TILE_DEV, flat), F32),
            in_specs=[pl.BlockSpec(memory_space=VMEM)] * 3,
            out_specs=pl.BlockSpec(memory_space=VMEM),
            name="project",
        )(sums, *weights)
    low, high, rows = exchange_edges(n_tm, n_det, 2 * half, time_stream, tile, frame_count)
    precision = lax.dynamic_slice_in_dim(det_precision, lax.axis_index("det") * dets, dets, axis=1)
    part = plain_partial_sums(time_stream, low, high, filter_taps, rows, tile_owner, precision, *sizes)
    return call(functools.partial(gather_kernel, n_tm, n_det), (VMEM,) * 3, (part,) + weights, gather, (TILE_DEV, flat), "gather")


def solution(mesh):
    return jax.shard_map(
        functools.partial(local, mesh.shape["tm"], mesh.shape["det"]),
        mesh=mesh,
        in_specs=(
            P("det", "tm"),
            P("det", None),
            P(),
            P(),
            P(),
            P(("tm", "det"), None),
            P(),
            P(("tm", "det")),
        ),
        out_specs=P(("tm", "det"), None),
        check_vma=False,
    )
```

```python
import functools

import jax
import jax.numpy as jnp
from jax import lax
from jax.experimental import pallas as pl
from jax.experimental.pallas import tpu as pltpu
from jax.sharding import PartitionSpec as P

TILE_DEV = 2
LANES = 128
MESH = pl.DeviceIdType.MESH
VMEM = pltpu.VMEM
F32 = jnp.float32
BF16 = jnp.bfloat16
CONTRACT = (((1,), (1,)), ((), ()))


def owner_rows(tile_owner):
    total_tiles = tile_owner.shape[0]
    same_owner = tile_owner[:, None] == tile_owner[None, :]
    earlier = jnp.arange(total_tiles)[None, :] < jnp.arange(total_tiles)[:, None]
    slot_rank = jnp.sum((same_owner & earlier).astype(jnp.int32), axis=1)
    return tile_owner * TILE_DEV + slot_rank


def start_edges(n_tm, n_det, width, x_ref, low_ref, high_ref, all_ref, rows_ref, send_sem, recv_sem, halo_send, halo_recv, own_sem):
    tm, det = lax.axis_index("tm"), lax.axis_index("det")
    has_low, has_high = tm > 0, tm < n_tm - 1
    down = pltpu.make_async_remote_copy(
        src_ref=x_ref.at[:, 0:width], dst_ref=high_ref, send_sem=halo_send.at[0], recv_sem=halo_recv.at[0],
        device_id=(tm - 1, det), device_id_type=MESH)
    up = pltpu.make_async_remote_copy(
        src_ref=x_ref.at[:, x_ref.shape[1] - width:], dst_ref=low_ref, send_sem=halo_send.at[1], recv_sem=halo_recv.at[1],
        device_id=(tm + 1, det), device_id_type=MESH)

    @pl.when(has_low)
    def _():
        down.start()

    @pl.when(has_high)
    def _():
        up.start()

    copies = []
    for step in range(1, n_det):
        copy = pltpu.make_async_remote_copy(
            src_ref=rows_ref, dst_ref=all_ref.at[det], send_sem=send_sem.at[step], recv_sem=recv_sem.at[step],
            device_id=(tm, lax.rem(det + step, n_det)), device_id_type=MESH)
        copy.start()
        copies.append(copy)
    own = pltpu.make_async_copy(rows_ref, all_ref.at[det], own_sem)
    own.start()

    @pl.when(jnp.logical_not(has_low))
    def _():
        low_ref[...] = jnp.zeros_like(low_ref)

    @pl.when(jnp.logical_not(has_high))
    def _():
        high_ref[...] = jnp.zeros_like(high_ref)

    def finish():
        own.wait()
        for copy in copies:
            copy.wait()

        @pl.when(has_low)
        def _():
            down.wait_send()
            up.wait_recv()

        @pl.when(has_high)
        def _():
            up.wait_send()
            down.wait_recv()

    return finish


def live_rows(tile_ref, count, rows_ref):
    tile = tile_ref[...]
    frame = lax.broadcasted_iota(jnp.int32, tile.shape, 0) * tile.shape[1] + lax.broadcasted_iota(jnp.int32, tile.shape, 1)
    rows_ref[...] = jnp.where(frame < count, tile, -1)


def edge_kernel(n_tm, n_det, width, x_ref, tile_ref, count_ref, low_ref, high_ref, all_ref, rows_ref, *sems):
    tm, det = lax.axis_index("tm"), lax.axis_index("det")
    has_low, has_high = tm > 0, tm < n_tm - 1
    barrier = pltpu.get_barrier_semaphore()
    for step in range(1, n_det):
        pl.semaphore_signal(barrier, inc=1, device_id=(tm, lax.rem(det + step, n_det)), device_id_type=MESH)

    @pl.when(has_low)
    def _():
        pl.semaphore_signal(barrier, inc=1, device_id=(tm - 1, det), device_id_type=MESH)

    @pl.when(has_high)
    def _():
        pl.semaphore_signal(barrier, inc=1, device_id=(tm + 1, det), device_id_type=MESH)

    live_rows(tile_ref, count_ref[0], rows_ref)
    pl.semaphore_wait(barrier, n_det - 1 + has_low.astype(jnp.int32) + has_high.astype(jnp.int32))
    start_edges(n_tm, n_det, width, x_ref, low_ref, high_ref, all_ref, rows_ref, *sems)()


def edge_sems(n_det):
    return [
        pltpu.SemaphoreType.DMA((n_det,)),
        pltpu.SemaphoreType.DMA((n_det,)),
        pltpu.SemaphoreType.DMA((2,)),
        pltpu.SemaphoreType.DMA((2,)),
        pltpu.SemaphoreType.DMA,
    ]


def exchange_edges(n_tm, n_det, width, x, tile, count):
    vmem = pl.BlockSpec(memory_space=VMEM)
    halo = jax.ShapeDtypeStruct((x.shape[0], width), x.dtype)
    return pl.pallas_call(
        functools.partial(edge_kernel, n_tm, n_det, width),
        out_shape=(halo, halo, jax.ShapeDtypeStruct((n_det,) + tile.shape, tile.dtype)),
        in_specs=[pl.BlockSpec(memory_space=pl.ANY), vmem, pl.BlockSpec(memory_space=pltpu.SMEM)],
        out_specs=(vmem,) * 3,
        scratch_shapes=[
            VMEM(tile.shape, tile.dtype),
        ] + edge_sems(n_det),
        compiler_params=pltpu.CompilerParams(collective_id=0, has_side_effects=True),
        name="edges",
    )(x, tile, count)


def fast_path(n_tm, n_det, half, fd, ft, x):
    width = 2 * half
    return (
        n_det % 2 == 0 and x.shape[0] == LANES and width == LANES and x.shape[1] == half * LANES
        and fd == ft and half == 2 * ft and (x.shape[1] // ft) % (4 * n_det) == 0)


def load_blocks(half, x_hbm, x_ref, load_sem, cur, mid, pitch):
    dets, samples = x_ref.shape
    width = 2 * half
    pieces = load_sem.shape[0]
    span = samples // pieces
    loads = []
    for piece in range(pieces):
        part = pl.ds(piece * span, span)
        load = pltpu.make_async_copy(x_hbm.at[:, part], x_ref.at[:, part], load_sem.at[piece])
        load.start()
        loads.append(load)

    def finish():
        per = span // width
        for piece, load in enumerate(loads):
            load.wait()
            for b in range(piece * per, (piece + 1) * per):
                at = b * width
                cur[b * pitch:b * pitch + dets, :] = x_ref[:, at:at + width].astype(F32)
                if b:
                    mid[b * pitch:b * pitch + dets, :] = x_ref[:, at - half:at + half].astype(F32)

    return finish


def edge_blocks(half, x_ref, cur, mid, pitch):
    dets, samples = x_ref.shape
    last = samples // (2 * half) * pitch
    none = jnp.zeros((dets, half), BF16)
    mid[0:dets, :] = jnp.concatenate([none, x_ref[:, 0:half]], axis=1).astype(F32)
    mid[last:last + dets, :] = jnp.concatenate([x_ref[:, samples - half:], none], axis=1).astype(F32)
    cur[last:last + dets, :] = jnp.zeros((dets, 2 * half), F32)


def filter_edges(half, ft, x_ref, low_ref, high_ref, cur, mid, pitch, wide, turned, ends):
    dets, samples = x_ref.shape
    width = 2 * half
    last = (samples // width - 1) * pitch
    first = jnp.concatenate([low_ref[:, half:], x_ref[:, 0:half]], axis=1)
    turned[0, 0:width, :] = first.astype(F32).T
    turned[0, width:, :] = mid[pitch:pitch + dets, :].T
    turned[1, 0:width, :] = cur[last:last + dets, :].T
    turned[1, width:, :] = high_ref[...].astype(F32).T
    sums = []
    for e in range(2):
        total = jnp.zeros((half, dets), F32)
        for r in range(8):
            taps = range(r, width + 1, 8)
            shifted = turned[e, r:taps[-1] + half, :]
            for k in taps:
                total += shifted[k - r:k - r + half, :] * wide[k:k + 1, :]
        sums.append(total)
    low, high = sums
    for q in range(2):
        ends[pl.ds(q * half, ft, stride=2), :] = low[q * ft:(q + 1) * ft, :]
    ends[pl.ds(half - 1, ft, stride=2), :] = high[ft:, :]
    ends[pl.ds(1, ft - 1, stride=2), :] = high[1:ft, :]
    ends[width - 1:, :] = high[0:1, :]
    return ends[...].T


def spread_taps(tapst_ref, wide, taps_ref):
    wide[...] = jnp.zeros(wide.shape, F32)
    wide[0:tapst_ref.shape[0], :] = tapst_ref[...].astype(F32)
    taps_ref[...] = wide[...].T


def owner_order(owner_ref, tiles):
    across_owner = jnp.broadcast_to(owner_ref[...].astype(F32), (tiles, tiles))
    down = lax.broadcasted_iota(jnp.int32, (tiles, tiles), 0)
    across_tile = lax.broadcasted_iota(jnp.int32, (tiles, tiles), 1)
    earlier = (across_owner.T == across_owner) & (down < across_tile)
    rank = jnp.sum(jnp.where(earlier, 1.0, 0.0), axis=0, keepdims=True)
    place = across_owner * TILE_DEV + rank
    order = jnp.sum(jnp.where(place == down.astype(F32), across_tile.astype(F32), 0.0), axis=1, keepdims=True)
    return jnp.broadcast_to(order, (tiles, LANES))


def filter_chunks(half, ft, core, cur, mid, pitch, taps_ref, stage, kept, sent, send, before_last):
    chunks, frames, unroll, _ = sent.shape
    dets = chunks * unroll
    blocks = LANES // 2
    step_rows = stage.shape[1] // ft

    def chunk_step(c, carry):
        for k in range(unroll):
            d = c * unroll + k
            spread = jnp.broadcast_to(taps_ref[pl.ds(d, 1), :], (half, 4 * half))
            matrix = pltpu.roll(spread, 0, 1, stride=1, stride_axis=0).astype(BF16)
            rows = []
            for source in (mid, cur):
                lower = source[pl.ds(d, blocks, stride=pitch), :]
                upper = source[pl.ds(d + pitch, blocks, stride=pitch), :]
                rows.append(jnp.concatenate([lower, upper], axis=1))
            window = jnp.concatenate(rows, axis=0).astype(BF16)
            result = lax.dot_general(matrix, window, CONTRACT, preferred_element_type=F32)
            for q in range(2):
                stage[q, pl.ds(k, ft, stride=step_rows), :] = result[q * ft:(q + 1) * ft, :]
        at = pl.multiple_of(core * dets + c * unroll, unroll)
        for f in range(frames):
            rows = slice(f * step_rows, f * step_rows + unroll)
            kept[f, pl.ds(at, unroll), :] = stage[core, rows, :].astype(BF16)
            sent[c, f] = stage[1 - core, rows, :].astype(BF16)
        send(c).start()
        return carry

    lax.fori_loop(0, chunks - 1, chunk_step, 0)
    before_last()
    chunk_step(chunks - 1, 0)


def pick_frames(core, fd, ft, order, rows_ref, picks):
    segments, rows, width = rows_ref.shape
    tiles = order.shape[0]
    per_row = width // fd
    spans = LANES // 2 // segments
    lane = lax.broadcasted_iota(jnp.int32, (LANES, per_row * LANES), 1)
    at = lax.broadcasted_iota(jnp.int32, (LANES, per_row * LANES), 0)
    h, inner = lane // LANES, lane % LANES
    p, m = inner // (LANES // 2), inner % (LANES // 2)
    target = (m // spans) * width + h * fd + 4 * (m % spans) + 2 * p + core - at
    found = jnp.zeros((2 * rows, per_row * LANES), F32)
    for s in range(segments):
        one = jnp.where(target == s * width, 1.0, 0.0).astype(BF16)
        tile = rows_ref[s].astype(F32)
        found += jnp.dot(jnp.concatenate([tile, tile], axis=0).astype(BF16), one, preferred_element_type=F32)
    for r in range(rows):
        for k in range(per_row):
            g = r * per_row + k
            picks[:, g * LANES:(g + 1) * LANES] = jnp.where(
                order == found[r:r + 1, k * LANES:(k + 1) * LANES], 1.0, 0.0).astype(BF16)


def whiten(fd, half, prec_ref, kept, edges, whitened):
    frames = kept.shape[0]
    across = LANES // fd
    low = frames // across
    groups = prec_ref.shape[0] // fd
    lane = lax.broadcasted_iota(jnp.int32, edges.shape, 1)
    outer = (lane == 0) | (lane == LANES - 1)

    def frame_samples(f):
        ends = pltpu.roll(edges[...], (LANES - 2 * f) % LANES, 1)
        return jnp.where(outer, ends, kept[f].astype(F32)).astype(BF16)

    for u in range(half * low // 2, (half + 1) * low // 2):
        for v in range(0, across, 2):
            weight = jnp.concatenate([frame_samples((v + i) * low + u) for i in range(2)], axis=1)
            result = jnp.dot(prec_ref[...], weight, preferred_element_type=F32).astype(BF16)
            for i in range(2):
                at = (u * across + v + i) * fd
                for g in range(groups):
                    whitened[at:at + fd, g * LANES:(g + 1) * LANES] = (
                        result[g * fd:(g + 1) * fd, i * LANES:(i + 1) * LANES])


def tile_sums(half, picks, whitened, packed, part):
    tiles = picks.shape[0]
    size = whitened.shape[0] // 2
    wide = 2 * LANES
    low = size // LANES
    for n in range(size // wide):
        at = half * size + n * wide
        sums = lax.dot_general(picks[...], whitened[at:at + wide, :], CONTRACT, preferred_element_type=F32)
        for i in range(2):
            packed[half, pl.ds(2 * n + i, tiles, stride=low), :] = sums[:, i * LANES:(i + 1) * LANES]
    rows = part.shape[2]
    for owner in range(part.shape[1]):
        part[half, owner] = packed[half, owner * rows:(owner + 1) * rows, :].astype(part.dtype)


CHUNK = 32
PITCH = 4


def partial_scratch(half, fd, ft, tiles, x, precision):
    dets, samples = x.shape
    width = 2 * half
    blocks = (samples // width + 1) * (dets + PITCH)
    chunks = dets // CHUNK
    return [
        VMEM(x.shape, BF16),
        VMEM((precision.shape[0], 2 * dets), BF16),
        pltpu.SemaphoreType.DMA((4,)),
        pltpu.SemaphoreType.DMA,
        pltpu.SemaphoreType.DMA((chunks,)),
        pltpu.SemaphoreType.DMA((chunks,)),
        VMEM((2 * width, dets), F32),
        VMEM((dets, 2 * width), F32),
        VMEM((blocks, width), F32),
        VMEM((blocks, width), F32),
        VMEM((2, ft * (CHUNK + 1), LANES), F32),
        VMEM((ft, 2 * dets, LANES), BF16),
        VMEM((chunks, ft, CHUNK, LANES), BF16),
        VMEM((tiles, precision.shape[0] // fd * LANES), BF16),
        VMEM((ft * fd, precision.shape[0] // fd * LANES), BF16),
        VMEM((2, 2 * width, dets), F32),
        VMEM((width, dets), F32),
        VMEM((2 * dets, LANES), BF16),
        VMEM((2 * dets, LANES), F32),
        pltpu.SemaphoreType.DMA((2,)),
    ]


def part_shape(fd, ft, tiles):
    return (tiles // TILE_DEV, TILE_DEV * ft // (LANES // fd), LANES)


def plain_partial_sums(x, low, high, taps, rows, owner, precision, half, fd, ft, tiles):
    dets, samples = x.shape
    width = 2 * half
    groups = precision.shape[0] // fd
    blocks = samples // width
    padded = jnp.concatenate([low[:, -half:], x, high[:, :half]], axis=1).reshape(dets, blocks + 1, width)
    length = 4 * half + 1
    tiled = jnp.broadcast_to(jnp.pad(taps, ((0, 0), (0, length - taps.shape[1])))[:, None, :], (dets, width, length))
    matrix = tiled.reshape(dets, width * length)[:, :width * 2 * width].reshape(dets, width, 2 * width)
    near = jnp.einsum("dbj,dij->dbi", padded, matrix[:, :, :width], preferred_element_type=F32)
    far = jnp.einsum("dbj,dij->dbi", padded, matrix[:, :, width:], preferred_element_type=F32)
    filtered = (near[:, :-1] + far[:, 1:]).astype(BF16).reshape(dets, samples // ft, ft)
    order = jnp.argsort(owner_rows(owner)).astype(jnp.int32)
    rows = rows.reshape(rows.shape[0], groups, -1).transpose(1, 0, 2).reshape(groups, 1, -1)
    picks = (rows == order[None, :, None]).astype(BF16)
    sums = jnp.einsum("gkt,dtf->gkfd", picks, filtered, preferred_element_type=F32).astype(BF16)
    out = jnp.einsum("gkfd,gad->kfa", sums, precision.reshape(groups, fd, dets), preferred_element_type=F32)
    across = LANES // fd
    low_part = ft // across
    out = out.reshape(tiles, across, low_part, fd).transpose(0, 2, 1, 3)
    return out.reshape(tiles // TILE_DEV, TILE_DEV * low_part, LANES).astype(BF16)


def peer(me, step, n_tm, n_det):
    other = lax.rem(me + step, n_tm * n_det)
    return other, (other // n_det, lax.rem(other, n_det))


def greet(n_tm, n_det):
    me = lax.axis_index("tm") * n_det + lax.axis_index("det")
    barrier = pltpu.get_barrier_semaphore()
    for step in range(1, n_tm * n_det):
        pl.semaphore_signal(barrier, inc=1, device_id=peer(me, step, n_tm, n_det)[1], device_id_type=MESH)
    return me, barrier


def gather_body(n_tm, n_det, me, part_ref, left_ref, right_ref, out_ref, held, send_sem, recv_sem, own_sem):
    count = n_tm * n_det
    fd = left_ref.shape[0]
    copies = []
    far = range(n_det, count)
    for step in [*far, *range(1, n_det)]:
        other, where = peer(me, step, n_tm, n_det)
        copy = pltpu.make_async_remote_copy(
            src_ref=part_ref.at[other], dst_ref=held.at[me], send_sem=send_sem.at[step], recv_sem=recv_sem.at[step],
            device_id=where, device_id_type=MESH)
        copy.start()
        copies.append(copy)
    own = pltpu.make_async_copy(part_ref.at[me], held.at[me], own_sem)
    own.start()
    own.wait()
    for copy in copies:
        copy.wait()
    total = jnp.sum(held[...].astype(F32), axis=0)
    low = total.shape[0] // TILE_DEV
    across = total.shape[1] // fd
    tiles = []
    for k in range(TILE_DEV):
        tile = total[k * low:(k + 1) * low, :]
        stacked = jnp.concatenate([tile[:, v * fd:(v + 1) * fd] for v in range(across)], axis=0)
        rows = jnp.dot(stacked, left_ref[...], precision=lax.Precision.HIGHEST, preferred_element_type=F32)
        tiles.append(lax.dot_general(
            rows, right_ref[...], (((0,), (0,)), ((), ())), precision=lax.Precision.HIGHEST,
            preferred_element_type=F32))
    width = right_ref.shape[1]
    for i in range(left_ref.shape[1]):
        out_ref[:, i * width:(i + 1) * width] = jnp.concatenate([tile[i:i + 1, :] for tile in tiles], axis=0)


def gather_kernel(n_tm, n_det, part_ref, left_ref, right_ref, out_ref, *scratch):
    me, barrier = greet(n_tm, n_det)
    pl.semaphore_wait(barrier, n_tm * n_det - 1)
    gather_body(n_tm, n_det, me, part_ref, left_ref, right_ref, out_ref, *scratch)


def greet_lines(n_tm, n_det):
    tm, det = lax.axis_index("tm"), lax.axis_index("det")
    barrier = pltpu.get_barrier_semaphore()
    for step in range(1, n_tm):
        pl.semaphore_signal(barrier, inc=1, device_id=(lax.rem(tm + step, n_tm), det), device_id_type=MESH)
    for step in range(1, n_det):
        pl.semaphore_signal(barrier, inc=1, device_id=(tm, lax.rem(det + step, n_det)), device_id_type=MESH)
    return lambda: pl.semaphore_wait(barrier, n_tm + n_det - 2)


def send_parts(n_tm, n_det, half, part, held, send_sem, recv_sem, own_sem):
    me = lax.axis_index("tm") * n_det + lax.axis_index("det")
    count = n_tm * n_det
    copies = []
    for step in [*range(n_det, count), *range(1, n_det)]:
        other, where = peer(me, step, n_tm, n_det)
        copies.append(pltpu.make_async_remote_copy(
            src_ref=part.at[half, other], dst_ref=held.at[half, me], send_sem=send_sem.at[half, step],
            recv_sem=recv_sem.at[half, step], device_id=where, device_id_type=MESH))
    copies.append(pltpu.make_async_copy(part.at[half, me], held.at[half, me], own_sem.at[half]))
    for copy in copies:
        copy.start()
    return copies


def whole_kernel(n_tm, n_det, sizes, x_hbm, tapst_hbm, owner_hbm, prec_hbm, tile_hbm, count_hbm, out_ref, low, high, held_rows, own_rows, *rest):
    half, fd, ft, tiles = sizes
    edge, rest = rest[:5], rest[5:]
    (part, held, part_send, part_recv, part_own, packed, planes, tapst_ref, owner_ref, tile_ref, count_ref, small_sem), rest = rest[:12], rest[12:]
    (x_ref, prec_ref, load_sem, prec_sem, pair_send, pair_recv, wide, taps_ref, cur, mid, stage, kept, sent, picks,
     whitened, turned, ends, both, edges, swap_sem) = rest
    tm, det = lax.axis_index("tm"), lax.axis_index("det")
    core = lax.rem(det, 2)
    dets = x_ref.shape[0]
    pitch = dets + PITCH
    unroll = sent.shape[2]
    meet = greet_lines(n_tm, n_det)
    small = [
        pltpu.make_async_copy(source, target, small_sem.at[i]) for i, (source, target) in enumerate((
            (tile_hbm, tile_ref), (count_hbm, count_ref), (tapst_hbm, tapst_ref), (owner_hbm, owner_ref)))]
    for copy in small:
        copy.start()
    build = load_blocks(half, x_hbm, x_ref, load_sem, cur, mid, pitch)
    first = pl.multiple_of((det - core) * dets, 2 * dets)
    load = pltpu.make_async_copy(prec_hbm.at[:, pl.ds(first, 2 * dets)], prec_ref, prec_sem)
    load.start()
    small[0].wait()
    small[1].wait()
    live_rows(tile_ref, count_ref[0], own_rows)
    meet()
    finish = start_edges(n_tm, n_det, 2 * half, x_hbm, low, high, held_rows, own_rows, *edge)
    for step in range(1, n_tm):
        pl.semaphore_signal(planes, inc=1, device_id=(lax.rem(tm + step, n_tm), det), device_id_type=MESH)
    small[2].wait()
    spread_taps(tapst_ref, wide, taps_ref)
    build()
    edge_blocks(half, x_ref, cur, mid, pitch)

    def send(c):
        at = pl.multiple_of(core * dets + c * unroll, unroll)
        return pltpu.make_async_remote_copy(
            src_ref=sent.at[c], dst_ref=kept.at[:, pl.ds(at, unroll), :], send_sem=pair_send.at[c],
            recv_sem=pair_recv.at[c], device_id=(tm, det + 1 - 2 * core), device_id_type=MESH)

    own = pl.ds(pl.multiple_of(core * dets, dets), dets)
    swap = pltpu.make_async_remote_copy(
        src_ref=both.at[own], dst_ref=both.at[own], send_sem=swap_sem.at[0], recv_sem=swap_sem.at[1],
        device_id=(tm, det + 1 - 2 * core), device_id_type=MESH)

    def edges_between():
        finish()
        both[own, :] = filter_edges(
            half, ft, x_ref, low, high, cur, mid, pitch, wide, turned, ends).astype(BF16)
        swap.start()

    filter_chunks(half, ft, core, cur, mid, pitch, taps_ref, stage, kept, sent, send, edges_between)
    small[3].wait()
    pick_frames(core, fd, ft, owner_order(owner_ref, tiles), held_rows, picks)
    load.wait()
    swap.wait()
    edges[...] = pltpu.roll(both[...].astype(F32), half * core, 1)
    for c in range(sent.shape[0]):
        send(c).wait()
    waits = []
    for h in range(2):
        whiten(fd, h, prec_ref, kept, edges, whitened)
        tile_sums(h, picks, whitened, packed, part)
        if h == 0:
            pl.semaphore_wait(planes, n_tm - 1)
        waits.append(send_parts(n_tm, n_det, h, part, held, part_send, part_recv, part_own))
    for h in range(2):
        for copy in waits[h]:
            copy.wait()
        out_ref[h] = jnp.sum(held[h].astype(F32), axis=0)


def reduce_scratch(count, fd, ft, tiles, small, live):
    rows = TILE_DEV * ft * fd // LANES // 2
    return [
        VMEM((2, count, rows, LANES), BF16),
        VMEM((2, count, rows, LANES), BF16),
        pltpu.SemaphoreType.DMA((2, count)),
        pltpu.SemaphoreType.DMA((2, count)),
        pltpu.SemaphoreType.DMA((2,)),
        VMEM((2, count * rows, LANES), F32),
        pltpu.SemaphoreType.REGULAR,
    ] + [VMEM(array.shape, array.dtype) for array in small] + [
        pltpu.SMEM(live.shape, live.dtype),
        pltpu.SemaphoreType.DMA((len(small) + 1,)),
    ]


def project_kernel(sums_ref, left_ref, right_ref, out_ref):
    fd = left_ref.shape[0]
    low = sums_ref.shape[1] // TILE_DEV
    tiles = []
    for k in range(TILE_DEV):
        tile = jnp.concatenate([sums_ref[h, k * low:(k + 1) * low, :] for h in range(2)], axis=0)
        stacked = jnp.concatenate([tile[:, v * fd:(v + 1) * fd] for v in range(LANES // fd)], axis=0)
        rows = jnp.dot(stacked, left_ref[...], precision=lax.Precision.HIGHEST, preferred_element_type=F32)
        tiles.append(lax.dot_general(
            rows, right_ref[...], (((0,), (0,)), ((), ())), precision=lax.Precision.HIGHEST,
            preferred_element_type=F32))
    width = right_ref.shape[1]
    for i in range(left_ref.shape[1]):
        out_ref[:, i * width:(i + 1) * width] = jnp.concatenate([tile[i:i + 1, :] for tile in tiles], axis=0)


def gather_scratch(count, shape):
    return [
        VMEM(shape, BF16),
        pltpu.SemaphoreType.DMA((count,)),
        pltpu.SemaphoreType.DMA((count,)),
        pltpu.SemaphoreType.DMA,
    ]


def call(kernel, specs, inputs, scratch, out, name):
    return pl.pallas_call(
        kernel,
        out_shape=jax.ShapeDtypeStruct(out, F32),
        in_specs=[pl.BlockSpec(memory_space=space) for space in specs],
        out_specs=pl.BlockSpec(memory_space=VMEM),
        scratch_shapes=scratch,
        compiler_params=pltpu.CompilerParams(
            collective_id=1, has_side_effects=True, vmem_limit_bytes=60 * 1024 * 1024),
        name=name,
    )(*inputs)


def local(
    n_tm, n_det,
    time_stream, filter_taps, det_precision, left_weight, right_weight, frame_tile, tile_owner, frame_count,
):
    half = filter_taps.shape[1] // 2
    fd, ft = left_weight.shape[1], right_weight.shape[1]
    dets = time_stream.shape[0]
    tiles = tile_owner.shape[0]
    count = n_tm * n_det
    tile = frame_tile.reshape(-1, LANES)
    sizes = (half, fd, ft, tiles)
    shape = part_shape(fd, ft, tiles)
    flat = left_weight.shape[0] * right_weight.shape[0]
    weights = (left_weight.T, right_weight.T)
    gather = gather_scratch(count, shape)
    if fast_path(n_tm, n_det, half, fd, ft, time_stream):
        taps, owner = filter_taps.T, tile_owner.reshape(1, -1)
        inputs = (time_stream, taps, owner, det_precision, tile, frame_count)
        specs = (pl.ANY,) * len(inputs)
        halo = VMEM((dets, 2 * half), BF16)
        scratch = [halo, halo, VMEM((n_det,) + tile.shape, tile.dtype), VMEM(tile.shape, tile.dtype)]
        scratch += edge_sems(n_det) + reduce_scratch(count, fd, ft, tiles, (taps, owner, tile), frame_count)
        scratch += partial_scratch(half, fd, ft, tiles, time_stream, det_precision)
        out = (2, TILE_DEV * ft * fd // LANES // 2, LANES)
        sums = call(functools.partial(whole_kernel, n_tm, n_det, sizes), specs, inputs, scratch, out, "whole")
        return pl.pallas_call(
            project_kernel,
            out_shape=jax.ShapeDtypeStruct((TILE_DEV, flat), F32),
            in_specs=[pl.BlockSpec(memory_space=VMEM)] * 3,
            out_specs=pl.BlockSpec(memory_space=VMEM),
            name="project",
        )(sums, *weights)
    low, high, rows = exchange_edges(n_tm, n_det, 2 * half, time_stream, tile, frame_count)
    precision = lax.dynamic_slice_in_dim(det_precision, lax.axis_index("det") * dets, dets, axis=1)
    part = plain_partial_sums(time_stream, low, high, filter_taps, rows, tile_owner, precision, *sizes)
    return call(functools.partial(gather_kernel, n_tm, n_det), (VMEM,) * 3, (part,) + weights, gather, (TILE_DEV, flat), "gather")


def solution(mesh):
    return jax.shard_map(
        functools.partial(local, mesh.shape["tm"], mesh.shape["det"]),
        mesh=mesh,
        in_specs=(
            P("det", "tm"),
            P("det", None),
            P(),
            P(),
            P(),
            P(("tm", "det"), None),
            P(),
            P(("tm", "det")),
        ),
        out_specs=P(("tm", "det"), None),
        check_vma=False,
    )
```

```python
import functools

import jax
import jax.numpy as jnp
from jax import lax
from jax.experimental import pallas as pl
from jax.experimental.pallas import tpu as pltpu
from jax.sharding import PartitionSpec as P

TILE_DEV = 2
LANES = 128
MESH = pl.DeviceIdType.MESH
VMEM = pltpu.VMEM
F32 = jnp.float32
BF16 = jnp.bfloat16
CONTRACT = (((1,), (1,)), ((), ()))


def owner_rows(tile_owner):
    total_tiles = tile_owner.shape[0]
    same_owner = tile_owner[:, None] == tile_owner[None, :]
    earlier = jnp.arange(total_tiles)[None, :] < jnp.arange(total_tiles)[:, None]
    slot_rank = jnp.sum((same_owner & earlier).astype(jnp.int32), axis=1)
    return tile_owner * TILE_DEV + slot_rank


def start_edges(n_tm, n_det, first_ref, last_ref, low_ref, high_ref, all_ref, rows_ref, send_sem, recv_sem, halo_send, halo_recv, own_sem):
    tm, det = lax.axis_index("tm"), lax.axis_index("det")
    has_low, has_high = tm > 0, tm < n_tm - 1
    down = pltpu.make_async_remote_copy(
        src_ref=first_ref, dst_ref=high_ref, send_sem=halo_send.at[0], recv_sem=halo_recv.at[0],
        device_id=(tm - 1, det), device_id_type=MESH)
    up = pltpu.make_async_remote_copy(
        src_ref=last_ref, dst_ref=low_ref, send_sem=halo_send.at[1], recv_sem=halo_recv.at[1],
        device_id=(tm + 1, det), device_id_type=MESH)

    @pl.when(has_low)
    def _():
        down.start()

    @pl.when(has_high)
    def _():
        up.start()

    copies = []
    for step in range(1, n_det):
        copy = pltpu.make_async_remote_copy(
            src_ref=rows_ref, dst_ref=all_ref.at[det], send_sem=send_sem.at[step], recv_sem=recv_sem.at[step],
            device_id=(tm, lax.rem(det + step, n_det)), device_id_type=MESH)
        copy.start()
        copies.append(copy)
    own = pltpu.make_async_copy(rows_ref, all_ref.at[det], own_sem)
    own.start()

    @pl.when(jnp.logical_not(has_low))
    def _():
        low_ref[...] = jnp.zeros_like(low_ref)

    @pl.when(jnp.logical_not(has_high))
    def _():
        high_ref[...] = jnp.zeros_like(high_ref)

    def finish_rows():
        own.wait()
        for copy in copies:
            copy.wait()

    def finish_edges():
        @pl.when(has_low)
        def _():
            down.wait_send()
            up.wait_recv()

        @pl.when(has_high)
        def _():
            up.wait_send()
            down.wait_recv()

    return finish_edges, finish_rows


def live_rows(tile_ref, count, rows_ref):
    tile = tile_ref[...]
    frame = lax.broadcasted_iota(jnp.int32, tile.shape, 0) * tile.shape[1] + lax.broadcasted_iota(jnp.int32, tile.shape, 1)
    rows_ref[...] = jnp.where(frame < count, tile, -1)


def edge_kernel(n_tm, n_det, width, x_ref, tile_ref, count_ref, low_ref, high_ref, all_ref, rows_ref, *sems):
    tm, det = lax.axis_index("tm"), lax.axis_index("det")
    has_low, has_high = tm > 0, tm < n_tm - 1
    barrier = pltpu.get_barrier_semaphore()
    for step in range(1, n_det):
        pl.semaphore_signal(barrier, inc=1, device_id=(tm, lax.rem(det + step, n_det)), device_id_type=MESH)

    @pl.when(has_low)
    def _():
        pl.semaphore_signal(barrier, inc=1, device_id=(tm - 1, det), device_id_type=MESH)

    @pl.when(has_high)
    def _():
        pl.semaphore_signal(barrier, inc=1, device_id=(tm + 1, det), device_id_type=MESH)

    live_rows(tile_ref, count_ref[0], rows_ref)
    pl.semaphore_wait(barrier, n_det - 1 + has_low.astype(jnp.int32) + has_high.astype(jnp.int32))
    for finish in start_edges(
            n_tm, n_det, x_ref.at[:, 0:width], x_ref.at[:, x_ref.shape[1] - width:], low_ref, high_ref, all_ref, rows_ref,
            *sems):
        finish()


def edge_sems(n_det):
    return [
        pltpu.SemaphoreType.DMA((n_det,)),
        pltpu.SemaphoreType.DMA((n_det,)),
        pltpu.SemaphoreType.DMA((2,)),
        pltpu.SemaphoreType.DMA((2,)),
        pltpu.SemaphoreType.DMA,
    ]


def exchange_edges(n_tm, n_det, width, x, tile, count):
    vmem = pl.BlockSpec(memory_space=VMEM)
    halo = jax.ShapeDtypeStruct((x.shape[0], width), x.dtype)
    return pl.pallas_call(
        functools.partial(edge_kernel, n_tm, n_det, width),
        out_shape=(halo, halo, jax.ShapeDtypeStruct((n_det,) + tile.shape, tile.dtype)),
        in_specs=[pl.BlockSpec(memory_space=pl.ANY), vmem, pl.BlockSpec(memory_space=pltpu.SMEM)],
        out_specs=(vmem,) * 3,
        scratch_shapes=[
            VMEM(tile.shape, tile.dtype),
        ] + edge_sems(n_det),
        compiler_params=pltpu.CompilerParams(collective_id=0, has_side_effects=True),
        name="edges",
    )(x, tile, count)


def fast_path(n_tm, n_det, half, fd, ft, x):
    width = 2 * half
    return (
        n_det % 2 == 0 and x.shape[0] == LANES and width == LANES and x.shape[1] == half * LANES
        and fd == ft and half == 2 * ft and (x.shape[1] // ft) % (4 * n_det) == 0)


def load_blocks(half, x_hbm, x_ref, load_sem, cur, mid, pitch):
    dets, samples = x_ref.shape
    width = 2 * half
    pieces = load_sem.shape[0]
    span = samples // pieces
    loads = []
    for piece in range(pieces):
        part = pl.ds(piece * span, span)
        load = pltpu.make_async_copy(x_hbm.at[:, part], x_ref.at[:, part], load_sem.at[piece])
        load.start()
        loads.append(load)

    def finish():
        per = span // width
        left = lax.broadcasted_iota(jnp.int32, (dets, width), 1) < half
        before = None
        for piece, load in enumerate(loads):
            load.wait()
            for b in range(piece * per, (piece + 1) * per):
                at = b * width
                block = x_ref[:, at:at + width].astype(F32)
                cur[b * pitch:b * pitch + dets, :] = block
                turned = pltpu.roll(block, half, 1)
                if b:
                    mid[b * pitch:b * pitch + dets, :] = jnp.where(left, before, turned)
                before = turned

    return finish


def edge_blocks(half, x_ref, cur, mid, pitch):
    dets, samples = x_ref.shape
    last = samples // (2 * half) * pitch
    none = jnp.zeros((dets, half), BF16)
    mid[0:dets, :] = jnp.concatenate([none, x_ref[:, 0:half]], axis=1).astype(F32)
    mid[last:last + dets, :] = jnp.concatenate([x_ref[:, samples - half:], none], axis=1).astype(F32)
    cur[last:last + dets, :] = jnp.zeros((dets, 2 * half), F32)


def filter_edges(half, ft, x_ref, low_ref, high_ref, cur, mid, pitch, wide, turned, ends):
    dets, samples = x_ref.shape
    width = 2 * half
    last = (samples // width - 1) * pitch
    first = jnp.concatenate([low_ref[:, half:], x_ref[:, 0:half]], axis=1)
    turned[0, 0:width, :] = first.astype(F32).T
    turned[0, width:, :] = mid[pitch:pitch + dets, :].T
    turned[1, 0:width, :] = cur[last:last + dets, :].T
    turned[1, width:, :] = high_ref[...].astype(F32).T
    sums = []
    for e in range(2):
        total = jnp.zeros((half, dets), F32)
        for r in range(8):
            taps = range(r, width + 1, 8)
            shifted = turned[e, r:taps[-1] + half, :]
            for k in taps:
                total += shifted[k - r:k - r + half, :] * wide[k:k + 1, :]
        sums.append(total)
    low, high = sums
    for q in range(2):
        ends[pl.ds(q * half, ft, stride=2), :] = low[q * ft:(q + 1) * ft, :]
    ends[pl.ds(half - 1, ft, stride=2), :] = high[ft:, :]
    ends[pl.ds(1, ft - 1, stride=2), :] = high[1:ft, :]
    ends[width - 1:, :] = high[0:1, :]
    return ends[...].T


def spread_taps(tapst_ref, wide, taps_ref):
    wide[...] = jnp.zeros(wide.shape, F32)
    wide[0:tapst_ref.shape[0], :] = tapst_ref[...].astype(F32)
    taps_ref[...] = wide[...].T


def owner_order(owner_ref, tiles):
    across_owner = jnp.broadcast_to(owner_ref[...].astype(F32), (tiles, tiles))
    down = lax.broadcasted_iota(jnp.int32, (tiles, tiles), 0)
    across_tile = lax.broadcasted_iota(jnp.int32, (tiles, tiles), 1)
    earlier = (across_owner.T == across_owner) & (down < across_tile)
    rank = jnp.sum(jnp.where(earlier, 1.0, 0.0), axis=0, keepdims=True)
    place = across_owner * TILE_DEV + rank
    order = jnp.sum(jnp.where(place == down.astype(F32), across_tile.astype(F32), 0.0), axis=1, keepdims=True)
    return jnp.broadcast_to(order, (tiles, LANES))


def filter_chunks(half, ft, core, cur, mid, pitch, taps_ref, stage, kept, sent, send, before_last):
    chunks, frames, unroll, _ = sent.shape
    dets = chunks * unroll
    blocks = LANES // 2
    step_rows = stage.shape[1] // ft

    def chunk_step(c, carry):
        for k in range(unroll):
            d = c * unroll + k
            spread = jnp.broadcast_to(taps_ref[pl.ds(d, 1), :], (half, 4 * half))
            matrix = pltpu.roll(spread, 0, 1, stride=1, stride_axis=0).astype(BF16)
            rows = []
            for source in (mid, cur):
                lower = source[pl.ds(d, blocks, stride=pitch), :]
                upper = source[pl.ds(d + pitch, blocks, stride=pitch), :]
                rows.append(jnp.concatenate([lower, upper], axis=1))
            window = jnp.concatenate(rows, axis=0).astype(BF16)
            result = lax.dot_general(matrix, window, CONTRACT, preferred_element_type=F32)
            for q in range(2):
                stage[q, pl.ds(k, ft, stride=step_rows), :] = result[q * ft:(q + 1) * ft, :]
        at = pl.multiple_of(core * dets + c * unroll, unroll)
        for f in range(frames):
            rows = slice(f * step_rows, f * step_rows + unroll)
            kept[f, pl.ds(at, unroll), :] = stage[core, rows, :].astype(BF16)
            sent[c, f] = stage[1 - core, rows, :].astype(BF16)
        send(c).start()
        return carry

    lax.fori_loop(0, chunks - 1, chunk_step, 0)
    before_last()
    chunk_step(chunks - 1, 0)


def pick_frames(core, fd, ft, order, rows_ref, picks):
    segments, rows, width = rows_ref.shape
    tiles = order.shape[0]
    per_row = width // fd
    spans = LANES // 2 // segments
    lane = lax.broadcasted_iota(jnp.int32, (LANES, per_row * LANES), 1)
    at = lax.broadcasted_iota(jnp.int32, (LANES, per_row * LANES), 0)
    h, inner = lane // LANES, lane % LANES
    p, m = inner // (LANES // 2), inner % (LANES // 2)
    target = (m // spans) * width + h * fd + 4 * (m % spans) + 2 * p + core - at
    found = jnp.zeros((2 * rows, per_row * LANES), F32)
    for s in range(segments):
        one = jnp.where(target == s * width, 1.0, 0.0).astype(BF16)
        tile = rows_ref[s].astype(F32)
        found += jnp.dot(jnp.concatenate([tile, tile], axis=0).astype(BF16), one, preferred_element_type=F32)
    for r in range(rows):
        for k in range(per_row):
            g = r * per_row + k
            picks[:, g * LANES:(g + 1) * LANES] = jnp.where(
                order == found[r:r + 1, k * LANES:(k + 1) * LANES], 1.0, 0.0).astype(BF16)


def whiten(fd, half, prec_ref, kept, edges, whitened):
    frames = kept.shape[0]
    across = LANES // fd
    low = frames // across
    groups = prec_ref.shape[0] // fd
    lane = lax.broadcasted_iota(jnp.int32, edges.shape, 1)
    outer = (lane == 0) | (lane == LANES - 1)

    def frame_samples(f):
        ends = pltpu.roll(edges[...], (LANES - 2 * f) % LANES, 1)
        return jnp.where(outer, ends, kept[f].astype(F32)).astype(BF16)

    for u in range(half * low // 2, (half + 1) * low // 2):
        for v in range(0, across, 2):
            weight = jnp.concatenate([frame_samples((v + i) * low + u) for i in range(2)], axis=1)
            result = jnp.dot(prec_ref[...], weight, preferred_element_type=F32).astype(BF16)
            for i in range(2):
                at = (u * across + v + i) * fd
                for g in range(groups):
                    whitened[at:at + fd, g * LANES:(g + 1) * LANES] = (
                        result[g * fd:(g + 1) * fd, i * LANES:(i + 1) * LANES])


def tile_sums(half, picks, whitened, packed, part):
    tiles = picks.shape[0]
    size = whitened.shape[0] // 2
    wide = 2 * LANES
    low = size // LANES
    for n in range(size // wide):
        at = half * size + n * wide
        sums = lax.dot_general(picks[...], whitened[at:at + wide, :], CONTRACT, preferred_element_type=F32)
        for i in range(2):
            packed[half, pl.ds(2 * n + i, tiles, stride=low), :] = sums[:, i * LANES:(i + 1) * LANES]
    rows = part.shape[2]
    for owner in range(part.shape[1]):
        part[half, owner] = packed[half, owner * rows:(owner + 1) * rows, :].astype(part.dtype)


CHUNK = 32
PITCH = 4


def partial_scratch(half, fd, ft, tiles, x, precision):
    dets, samples = x.shape
    width = 2 * half
    blocks = (samples // width + 1) * (dets + PITCH)
    chunks = dets // CHUNK
    return [
        VMEM(x.shape, BF16),
        VMEM((precision.shape[0], 2 * dets), BF16),
        pltpu.SemaphoreType.DMA((8,)),
        pltpu.SemaphoreType.DMA,
        pltpu.SemaphoreType.DMA((chunks,)),
        pltpu.SemaphoreType.DMA((chunks,)),
        VMEM((2 * width, dets), F32),
        VMEM((dets, 2 * width), F32),
        VMEM((blocks, width), F32),
        VMEM((blocks, width), F32),
        VMEM((2, ft * (CHUNK + 1), LANES), F32),
        VMEM((ft, 2 * dets, LANES), BF16),
        VMEM((chunks, ft, CHUNK, LANES), BF16),
        VMEM((tiles, precision.shape[0] // fd * LANES), BF16),
        VMEM((ft * fd, precision.shape[0] // fd * LANES), BF16),
        VMEM((2, 2 * width, dets), F32),
        VMEM((width, dets), F32),
        VMEM((2 * dets, LANES), BF16),
        VMEM((2 * dets, LANES), F32),
        pltpu.SemaphoreType.DMA((2,)),
        VMEM((2, dets, width), BF16),
    ]


def part_shape(fd, ft, tiles):
    return (tiles // TILE_DEV, TILE_DEV * ft // (LANES // fd), LANES)


def plain_partial_sums(x, low, high, taps, rows, owner, precision, half, fd, ft, tiles):
    dets, samples = x.shape
    width = 2 * half
    groups = precision.shape[0] // fd
    blocks = samples // width
    padded = jnp.concatenate([low[:, -half:], x, high[:, :half]], axis=1).reshape(dets, blocks + 1, width)
    length = 4 * half + 1
    tiled = jnp.broadcast_to(jnp.pad(taps, ((0, 0), (0, length - taps.shape[1])))[:, None, :], (dets, width, length))
    matrix = tiled.reshape(dets, width * length)[:, :width * 2 * width].reshape(dets, width, 2 * width)
    near = jnp.einsum("dbj,dij->dbi", padded, matrix[:, :, :width], preferred_element_type=F32)
    far = jnp.einsum("dbj,dij->dbi", padded, matrix[:, :, width:], preferred_element_type=F32)
    filtered = (near[:, :-1] + far[:, 1:]).astype(BF16).reshape(dets, samples // ft, ft)
    order = jnp.argsort(owner_rows(owner)).astype(jnp.int32)
    rows = rows.reshape(rows.shape[0], groups, -1).transpose(1, 0, 2).reshape(groups, 1, -1)
    picks = (rows == order[None, :, None]).astype(BF16)
    sums = jnp.einsum("gkt,dtf->gkfd", picks, filtered, preferred_element_type=F32).astype(BF16)
    out = jnp.einsum("gkfd,gad->kfa", sums, precision.reshape(groups, fd, dets), preferred_element_type=F32)
    across = LANES // fd
    low_part = ft // across
    out = out.reshape(tiles, across, low_part, fd).transpose(0, 2, 1, 3)
    return out.reshape(tiles // TILE_DEV, TILE_DEV * low_part, LANES).astype(BF16)


def peer(me, step, n_tm, n_det):
    other = lax.rem(me + step, n_tm * n_det)
    return other, (other // n_det, lax.rem(other, n_det))


def greet(n_tm, n_det):
    me = lax.axis_index("tm") * n_det + lax.axis_index("det")
    barrier = pltpu.get_barrier_semaphore()
    for step in range(1, n_tm * n_det):
        pl.semaphore_signal(barrier, inc=1, device_id=peer(me, step, n_tm, n_det)[1], device_id_type=MESH)
    return me, barrier


def gather_body(n_tm, n_det, me, part_ref, left_ref, right_ref, out_ref, held, send_sem, recv_sem, own_sem):
    count = n_tm * n_det
    fd = left_ref.shape[0]
    copies = []
    far = range(n_det, count)
    for step in [*far, *range(1, n_det)]:
        other, where = peer(me, step, n_tm, n_det)
        copy = pltpu.make_async_remote_copy(
            src_ref=part_ref.at[other], dst_ref=held.at[me], send_sem=send_sem.at[step], recv_sem=recv_sem.at[step],
            device_id=where, device_id_type=MESH)
        copy.start()
        copies.append(copy)
    own = pltpu.make_async_copy(part_ref.at[me], held.at[me], own_sem)
    own.start()
    own.wait()
    for copy in copies:
        copy.wait()
    total = jnp.sum(held[...].astype(F32), axis=0)
    low = total.shape[0] // TILE_DEV
    across = total.shape[1] // fd
    tiles = []
    for k in range(TILE_DEV):
        tile = total[k * low:(k + 1) * low, :]
        stacked = jnp.concatenate([tile[:, v * fd:(v + 1) * fd] for v in range(across)], axis=0)
        rows = jnp.dot(stacked, left_ref[...], precision=lax.Precision.HIGHEST, preferred_element_type=F32)
        tiles.append(lax.dot_general(
            rows, right_ref[...], (((0,), (0,)), ((), ())), precision=lax.Precision.HIGHEST,
            preferred_element_type=F32))
    width = right_ref.shape[1]
    for i in range(left_ref.shape[1]):
        out_ref[:, i * width:(i + 1) * width] = jnp.concatenate([tile[i:i + 1, :] for tile in tiles], axis=0)


def gather_kernel(n_tm, n_det, part_ref, left_ref, right_ref, out_ref, *scratch):
    me, barrier = greet(n_tm, n_det)
    pl.semaphore_wait(barrier, n_tm * n_det - 1)
    gather_body(n_tm, n_det, me, part_ref, left_ref, right_ref, out_ref, *scratch)


def greet_lines(n_tm, n_det):
    tm, det = lax.axis_index("tm"), lax.axis_index("det")
    barrier = pltpu.get_barrier_semaphore()
    for step in range(1, n_tm):
        pl.semaphore_signal(barrier, inc=1, device_id=(lax.rem(tm + step, n_tm), det), device_id_type=MESH)
    for step in range(1, n_det):
        pl.semaphore_signal(barrier, inc=1, device_id=(tm, lax.rem(det + step, n_det)), device_id_type=MESH)
    return lambda: pl.semaphore_wait(barrier, n_tm + n_det - 2)


def send_parts(n_tm, n_det, half, part, held, send_sem, recv_sem, own_sem):
    me = lax.axis_index("tm") * n_det + lax.axis_index("det")
    count = n_tm * n_det
    copies = []
    for step in [*range(n_det, count), *range(1, n_det)]:
        other, where = peer(me, step, n_tm, n_det)
        copies.append(pltpu.make_async_remote_copy(
            src_ref=part.at[half, other], dst_ref=held.at[half, me], send_sem=send_sem.at[half, step],
            recv_sem=recv_sem.at[half, step], device_id=where, device_id_type=MESH))
    copies.append(pltpu.make_async_copy(part.at[half, me], held.at[half, me], own_sem.at[half]))
    for copy in copies:
        copy.start()
    return copies


def whole_kernel(n_tm, n_det, sizes, x_hbm, tapst_hbm, owner_hbm, prec_hbm, tile_hbm, count_hbm, out_ref, low, high, held_rows, own_rows, *rest):
    half, fd, ft, tiles = sizes
    edge, rest = rest[:5], rest[5:]
    (part, held, part_send, part_recv, part_own, packed, planes, tapst_ref, owner_ref, tile_ref, count_ref, small_sem), rest = rest[:12], rest[12:]
    (x_ref, prec_ref, load_sem, prec_sem, pair_send, pair_recv, wide, taps_ref, cur, mid, stage, kept, sent, picks,
     whitened, turned, ends, both, edges, swap_sem, rims) = rest
    tm, det = lax.axis_index("tm"), lax.axis_index("det")
    core = lax.rem(det, 2)
    dets = x_ref.shape[0]
    pitch = dets + PITCH
    unroll = sent.shape[2]
    meet = greet_lines(n_tm, n_det)
    small = [
        pltpu.make_async_copy(source, target, small_sem.at[i]) for i, (source, target) in enumerate((
            (tile_hbm, tile_ref), (count_hbm, count_ref), (tapst_hbm, tapst_ref), (owner_hbm, owner_ref),
            (x_hbm.at[:, 0:2 * half], rims.at[0]), (x_hbm.at[:, x_ref.shape[1] - 2 * half:], rims.at[1])))]
    for copy in small:
        copy.start()
    build = load_blocks(half, x_hbm, x_ref, load_sem, cur, mid, pitch)
    first = pl.multiple_of((det - core) * dets, 2 * dets)
    load = pltpu.make_async_copy(prec_hbm.at[:, pl.ds(first, 2 * dets)], prec_ref, prec_sem)
    load.start()
    small[0].wait()
    small[1].wait()
    live_rows(tile_ref, count_ref[0], own_rows)
    meet()
    for copy in small[4:]:
        copy.wait()
    finish_edges, finish_rows = start_edges(
        n_tm, n_det, rims.at[0], rims.at[1], low, high, held_rows, own_rows, *edge)
    for step in range(1, n_tm):
        pl.semaphore_signal(planes, inc=1, device_id=(lax.rem(tm + step, n_tm), det), device_id_type=MESH)
    small[2].wait()
    spread_taps(tapst_ref, wide, taps_ref)
    build()
    edge_blocks(half, x_ref, cur, mid, pitch)

    def send(c):
        at = pl.multiple_of(core * dets + c * unroll, unroll)
        return pltpu.make_async_remote_copy(
            src_ref=sent.at[c], dst_ref=kept.at[:, pl.ds(at, unroll), :], send_sem=pair_send.at[c],
            recv_sem=pair_recv.at[c], device_id=(tm, det + 1 - 2 * core), device_id_type=MESH)

    own = pl.ds(pl.multiple_of(core * dets, dets), dets)
    swap = pltpu.make_async_remote_copy(
        src_ref=both.at[own], dst_ref=both.at[own], send_sem=swap_sem.at[0], recv_sem=swap_sem.at[1],
        device_id=(tm, det + 1 - 2 * core), device_id_type=MESH)

    def edges_between():
        finish_edges()
        both[own, :] = filter_edges(
            half, ft, x_ref, low, high, cur, mid, pitch, wide, turned, ends).astype(BF16)

    filter_chunks(half, ft, core, cur, mid, pitch, taps_ref, stage, kept, sent, send, edges_between)
    swap.start()
    small[3].wait()
    finish_rows()
    pick_frames(core, fd, ft, owner_order(owner_ref, tiles), held_rows, picks)
    load.wait()
    swap.wait()
    edges[...] = pltpu.roll(both[...].astype(F32), half * core, 1)
    for c in range(sent.shape[0]):
        send(c).wait()
    waits = []
    for h in range(2):
        whiten(fd, h, prec_ref, kept, edges, whitened)
    for h in range(2):
        tile_sums(h, picks, whitened, packed, part)
        if h == 0:
            pl.semaphore_wait(planes, n_tm - 1)
        waits.append(send_parts(n_tm, n_det, h, part, held, part_send, part_recv, part_own))
    for h in range(2):
        for copy in waits[h]:
            copy.wait()
        out_ref[h] = jnp.sum(held[h].astype(F32), axis=0)


def reduce_scratch(count, fd, ft, tiles, small, live):
    rows = TILE_DEV * ft * fd // LANES // 2
    return [
        VMEM((2, count, rows, LANES), BF16),
        VMEM((2, count, rows, LANES), BF16),
        pltpu.SemaphoreType.DMA((2, count)),
        pltpu.SemaphoreType.DMA((2, count)),
        pltpu.SemaphoreType.DMA((2,)),
        VMEM((2, count * rows, LANES), F32),
        pltpu.SemaphoreType.REGULAR,
    ] + [VMEM(array.shape, array.dtype) for array in small] + [
        pltpu.SMEM(live.shape, live.dtype),
        pltpu.SemaphoreType.DMA((len(small) + 3,)),
    ]


def project_kernel(sums_ref, left_ref, right_ref, out_hbm, out_ref, sem):
    fd = left_ref.shape[0]
    low = sums_ref.shape[1] // TILE_DEV
    tiles = []
    for k in range(TILE_DEV):
        tile = jnp.concatenate([sums_ref[h, k * low:(k + 1) * low, :] for h in range(2)], axis=0)
        stacked = jnp.concatenate([tile[:, v * fd:(v + 1) * fd] for v in range(LANES // fd)], axis=0)
        rows = jnp.dot(stacked, left_ref[...], precision=lax.Precision.HIGHEST, preferred_element_type=F32)
        tiles.append(lax.dot_general(
            rows, right_ref[...], (((0,), (0,)), ((), ())), precision=lax.Precision.HIGHEST,
            preferred_element_type=F32))
    width = right_ref.shape[1]
    total = left_ref.shape[1]
    pieces = sem.shape[0]
    span = total // pieces
    copies = []
    for piece in range(pieces):
        for i in range(piece * span, (piece + 1) * span):
            out_ref[:, i * width:(i + 1) * width] = jnp.concatenate([tile[i:i + 1, :] for tile in tiles], axis=0)
        part = pl.ds(piece * span * width, span * width)
        copy = pltpu.make_async_copy(out_ref.at[:, part], out_hbm.at[:, part], sem.at[piece])
        copy.start()
        copies.append(copy)
    for copy in copies:
        copy.wait()


def gather_scratch(count, shape):
    return [
        VMEM(shape, BF16),
        pltpu.SemaphoreType.DMA((count,)),
        pltpu.SemaphoreType.DMA((count,)),
        pltpu.SemaphoreType.DMA,
    ]


def call(kernel, specs, inputs, scratch, out, name):
    return pl.pallas_call(
        kernel,
        out_shape=jax.ShapeDtypeStruct(out, F32),
        in_specs=[pl.BlockSpec(memory_space=space) for space in specs],
        out_specs=pl.BlockSpec(memory_space=VMEM),
        scratch_shapes=scratch,
        compiler_params=pltpu.CompilerParams(
            collective_id=1, has_side_effects=True, vmem_limit_bytes=60 * 1024 * 1024),
        name=name,
    )(*inputs)


def local(
    n_tm, n_det,
    time_stream, filter_taps, det_precision, left_weight, right_weight, frame_tile, tile_owner, frame_count,
):
    half = filter_taps.shape[1] // 2
    fd, ft = left_weight.shape[1], right_weight.shape[1]
    dets = time_stream.shape[0]
    tiles = tile_owner.shape[0]
    count = n_tm * n_det
    tile = frame_tile.reshape(-1, LANES)
    sizes = (half, fd, ft, tiles)
    shape = part_shape(fd, ft, tiles)
    flat = left_weight.shape[0] * right_weight.shape[0]
    weights = (left_weight.T, right_weight.T)
    gather = gather_scratch(count, shape)
    if fast_path(n_tm, n_det, half, fd, ft, time_stream):
        taps, owner = filter_taps.T, tile_owner.reshape(1, -1)
        inputs = (time_stream, taps, owner, det_precision, tile, frame_count)
        specs = (pl.ANY,) * len(inputs)
        halo = VMEM((dets, 2 * half), BF16)
        scratch = [halo, halo, VMEM((n_det,) + tile.shape, tile.dtype), VMEM(tile.shape, tile.dtype)]
        scratch += edge_sems(n_det) + reduce_scratch(count, fd, ft, tiles, (taps, owner, tile), frame_count)
        scratch += partial_scratch(half, fd, ft, tiles, time_stream, det_precision)
        out = (2, TILE_DEV * ft * fd // LANES // 2, LANES)
        sums = call(functools.partial(whole_kernel, n_tm, n_det, sizes), specs, inputs, scratch, out, "whole")
        return pl.pallas_call(
            project_kernel,
            out_shape=jax.ShapeDtypeStruct((TILE_DEV, flat), F32),
            in_specs=[pl.BlockSpec(memory_space=VMEM)] * 3,
            out_specs=pl.BlockSpec(memory_space=pl.ANY),
            scratch_shapes=[VMEM((TILE_DEV, flat), F32), pltpu.SemaphoreType.DMA((4,))],
            name="project",
        )(sums, *weights)
    low, high, rows = exchange_edges(n_tm, n_det, 2 * half, time_stream, tile, frame_count)
    precision = lax.dynamic_slice_in_dim(det_precision, lax.axis_index("det") * dets, dets, axis=1)
    part = plain_partial_sums(time_stream, low, high, filter_taps, rows, tile_owner, precision, *sizes)
    return call(functools.partial(gather_kernel, n_tm, n_det), (VMEM,) * 3, (part,) + weights, gather, (TILE_DEV, flat), "gather")


def solution(mesh):
    return jax.shard_map(
        functools.partial(local, mesh.shape["tm"], mesh.shape["det"]),
        mesh=mesh,
        in_specs=(
            P("det", "tm"),
            P("det", None),
            P(),
            P(),
            P(),
            P(("tm", "det"), None),
            P(),
            P(("tm", "det")),
        ),
        out_specs=P(("tm", "det"), None),
        check_vma=False,
    )
```

```python
import functools

import jax
import jax.numpy as jnp
from jax import lax
from jax.experimental import pallas as pl
from jax.experimental.pallas import tpu as pltpu
from jax.sharding import PartitionSpec as P

TILE_DEV = 2
LANES = 128
MESH = pl.DeviceIdType.MESH
VMEM = pltpu.VMEM
F32 = jnp.float32
BF16 = jnp.bfloat16
CONTRACT = (((1,), (1,)), ((), ()))


def owner_rows(tile_owner):
    total_tiles = tile_owner.shape[0]
    same_owner = tile_owner[:, None] == tile_owner[None, :]
    earlier = jnp.arange(total_tiles)[None, :] < jnp.arange(total_tiles)[:, None]
    slot_rank = jnp.sum((same_owner & earlier).astype(jnp.int32), axis=1)
    return tile_owner * TILE_DEV + slot_rank


def start_edges(n_tm, n_det, first_ref, last_ref, low_ref, high_ref, all_ref, rows_ref, send_sem, recv_sem, halo_send, halo_recv, own_sem):
    tm, det = lax.axis_index("tm"), lax.axis_index("det")
    has_low, has_high = tm > 0, tm < n_tm - 1
    down = pltpu.make_async_remote_copy(
        src_ref=first_ref, dst_ref=high_ref, send_sem=halo_send.at[0], recv_sem=halo_recv.at[0],
        device_id=(tm - 1, det), device_id_type=MESH)
    up = pltpu.make_async_remote_copy(
        src_ref=last_ref, dst_ref=low_ref, send_sem=halo_send.at[1], recv_sem=halo_recv.at[1],
        device_id=(tm + 1, det), device_id_type=MESH)

    @pl.when(has_low)
    def _():
        down.start()

    @pl.when(has_high)
    def _():
        up.start()

    copies = []
    for step in range(1, n_det):
        copy = pltpu.make_async_remote_copy(
            src_ref=rows_ref, dst_ref=all_ref.at[det], send_sem=send_sem.at[step], recv_sem=recv_sem.at[step],
            device_id=(tm, lax.rem(det + step, n_det)), device_id_type=MESH)
        copy.start()
        copies.append(copy)
    own = pltpu.make_async_copy(rows_ref, all_ref.at[det], own_sem)
    own.start()

    @pl.when(jnp.logical_not(has_low))
    def _():
        low_ref[...] = jnp.zeros_like(low_ref)

    @pl.when(jnp.logical_not(has_high))
    def _():
        high_ref[...] = jnp.zeros_like(high_ref)

    def finish_rows():
        own.wait()
        for copy in copies:
            copy.wait()

    def finish_edges():
        @pl.when(has_low)
        def _():
            down.wait_send()
            up.wait_recv()

        @pl.when(has_high)
        def _():
            up.wait_send()
            down.wait_recv()

    return finish_edges, finish_rows


def live_rows(tile_ref, count, rows_ref):
    tile = tile_ref[...]
    frame = lax.broadcasted_iota(jnp.int32, tile.shape, 0) * tile.shape[1] + lax.broadcasted_iota(jnp.int32, tile.shape, 1)
    rows_ref[...] = jnp.where(frame < count, tile, -1)


def edge_kernel(n_tm, n_det, width, x_ref, tile_ref, count_ref, low_ref, high_ref, all_ref, rows_ref, *sems):
    tm, det = lax.axis_index("tm"), lax.axis_index("det")
    has_low, has_high = tm > 0, tm < n_tm - 1
    barrier = pltpu.get_barrier_semaphore()
    for step in range(1, n_det):
        pl.semaphore_signal(barrier, inc=1, device_id=(tm, lax.rem(det + step, n_det)), device_id_type=MESH)

    @pl.when(has_low)
    def _():
        pl.semaphore_signal(barrier, inc=1, device_id=(tm - 1, det), device_id_type=MESH)

    @pl.when(has_high)
    def _():
        pl.semaphore_signal(barrier, inc=1, device_id=(tm + 1, det), device_id_type=MESH)

    live_rows(tile_ref, count_ref[0], rows_ref)
    pl.semaphore_wait(barrier, n_det - 1 + has_low.astype(jnp.int32) + has_high.astype(jnp.int32))
    for finish in start_edges(
            n_tm, n_det, x_ref.at[:, 0:width], x_ref.at[:, x_ref.shape[1] - width:], low_ref, high_ref, all_ref, rows_ref,
            *sems):
        finish()


def edge_sems(n_det):
    return [
        pltpu.SemaphoreType.DMA((n_det,)),
        pltpu.SemaphoreType.DMA((n_det,)),
        pltpu.SemaphoreType.DMA((2,)),
        pltpu.SemaphoreType.DMA((2,)),
        pltpu.SemaphoreType.DMA,
    ]


def exchange_edges(n_tm, n_det, width, x, tile, count):
    vmem = pl.BlockSpec(memory_space=VMEM)
    halo = jax.ShapeDtypeStruct((x.shape[0], width), x.dtype)
    return pl.pallas_call(
        functools.partial(edge_kernel, n_tm, n_det, width),
        out_shape=(halo, halo, jax.ShapeDtypeStruct((n_det,) + tile.shape, tile.dtype)),
        in_specs=[pl.BlockSpec(memory_space=pl.ANY), vmem, pl.BlockSpec(memory_space=pltpu.SMEM)],
        out_specs=(vmem,) * 3,
        scratch_shapes=[
            VMEM(tile.shape, tile.dtype),
        ] + edge_sems(n_det),
        compiler_params=pltpu.CompilerParams(collective_id=0, has_side_effects=True),
        name="edges",
    )(x, tile, count)


def fast_path(n_tm, n_det, half, fd, ft, x):
    width = 2 * half
    return (
        n_det % 2 == 0 and x.shape[0] == LANES and width == LANES and x.shape[1] == half * LANES
        and fd == ft and half == 2 * ft and (x.shape[1] // ft) % (4 * n_det) == 0)


def load_blocks(half, x_hbm, x_ref, load_sem, cur, mid, pitch):
    dets, samples = x_ref.shape
    width = 2 * half
    pieces = load_sem.shape[0]
    span = samples // pieces
    loads = []
    for piece in range(pieces):
        part = pl.ds(piece * span, span)
        load = pltpu.make_async_copy(x_hbm.at[:, part], x_ref.at[:, part], load_sem.at[piece])
        load.start()
        loads.append(load)

    def finish():
        per = span // width
        left = lax.broadcasted_iota(jnp.int32, (dets, width), 1) < half
        before = None
        for piece, load in enumerate(loads):
            load.wait()
            for b in range(piece * per, (piece + 1) * per):
                at = b * width
                block = x_ref[:, at:at + width].astype(F32)
                cur[b * pitch:b * pitch + dets, :] = block
                turned = pltpu.roll(block, half, 1)
                if b:
                    mid[b * pitch:b * pitch + dets, :] = jnp.where(left, before, turned)
                before = turned
            if piece == pieces // 2 - 1:
                yield

    return finish()


def edge_blocks(half, x_ref, cur, mid, pitch):
    dets, samples = x_ref.shape
    last = samples // (2 * half) * pitch
    none = jnp.zeros((dets, half), BF16)
    mid[0:dets, :] = jnp.concatenate([none, x_ref[:, 0:half]], axis=1).astype(F32)
    mid[last:last + dets, :] = jnp.concatenate([x_ref[:, samples - half:], none], axis=1).astype(F32)
    cur[last:last + dets, :] = jnp.zeros((dets, 2 * half), F32)


def filter_edges(half, ft, x_ref, low_ref, high_ref, cur, mid, pitch, wide, turned, ends):
    dets, samples = x_ref.shape
    width = 2 * half
    last = (samples // width - 1) * pitch
    first = jnp.concatenate([low_ref[:, half:], x_ref[:, 0:half]], axis=1)
    turned[0, 0:width, :] = first.astype(F32).T
    turned[0, width:, :] = mid[pitch:pitch + dets, :].T
    turned[1, 0:width, :] = cur[last:last + dets, :].T
    turned[1, width:, :] = high_ref[...].astype(F32).T
    sums = []
    for e in range(2):
        total = jnp.zeros((half, dets), F32)
        for r in range(8):
            taps = range(r, width + 1, 8)
            shifted = turned[e, r:taps[-1] + half, :]
            for k in taps:
                total += shifted[k - r:k - r + half, :] * wide[k:k + 1, :]
        sums.append(total)
    low, high = sums
    for q in range(2):
        ends[pl.ds(q * half, ft, stride=2), :] = low[q * ft:(q + 1) * ft, :]
    ends[pl.ds(half - 1, ft, stride=2), :] = high[ft:, :]
    ends[pl.ds(1, ft - 1, stride=2), :] = high[1:ft, :]
    ends[width - 1:, :] = high[0:1, :]
    return ends[...].T


def spread_taps(tapst_ref, wide, taps_ref):
    wide[...] = jnp.zeros(wide.shape, F32)
    wide[0:tapst_ref.shape[0], :] = tapst_ref[...].astype(F32)
    taps_ref[...] = wide[...].T


def owner_order(owner_ref, tiles):
    across_owner = jnp.broadcast_to(owner_ref[...].astype(F32), (tiles, tiles))
    down = lax.broadcasted_iota(jnp.int32, (tiles, tiles), 0)
    across_tile = lax.broadcasted_iota(jnp.int32, (tiles, tiles), 1)
    earlier = (across_owner.T == across_owner) & (down < across_tile)
    rank = jnp.sum(jnp.where(earlier, 1.0, 0.0), axis=0, keepdims=True)
    place = across_owner * TILE_DEV + rank
    order = jnp.sum(jnp.where(place == down.astype(F32), across_tile.astype(F32), 0.0), axis=1, keepdims=True)
    return jnp.broadcast_to(order, (tiles, LANES))


def filter_chunks(half, ft, core, cur, mid, pitch, taps_ref, stage, kept, sent, send, before_last):
    chunks, frames, unroll, _ = sent.shape
    dets = chunks * unroll
    blocks = LANES // 2
    step_rows = stage.shape[1] // ft

    def chunk_step(c, carry):
        for k in range(unroll):
            d = c * unroll + k
            spread = jnp.broadcast_to(taps_ref[pl.ds(d, 1), :], (half, 4 * half))
            matrix = pltpu.roll(spread, 0, 1, stride=1, stride_axis=0).astype(BF16)
            rows = []
            for source in (mid, cur):
                lower = source[pl.ds(d, blocks, stride=pitch), :]
                upper = source[pl.ds(d + pitch, blocks, stride=pitch), :]
                rows.append(jnp.concatenate([lower, upper], axis=1))
            window = jnp.concatenate(rows, axis=0).astype(BF16)
            result = lax.dot_general(matrix, window, CONTRACT, preferred_element_type=F32)
            for q in range(2):
                stage[q, pl.ds(k, ft, stride=step_rows), :] = result[q * ft:(q + 1) * ft, :]
        at = pl.multiple_of(core * dets + c * unroll, unroll)
        for f in range(frames):
            rows = slice(f * step_rows, f * step_rows + unroll)
            kept[f, pl.ds(at, unroll), :] = stage[core, rows, :].astype(BF16)
            sent[c, f] = stage[1 - core, rows, :].astype(BF16)
        send(c).start()
        return carry

    lax.fori_loop(0, chunks - 1, chunk_step, 0)
    before_last()
    chunk_step(chunks - 1, 0)


def pick_frames(core, fd, ft, order, rows_ref, picks):
    segments, rows, width = rows_ref.shape
    tiles = order.shape[0]
    per_row = width // fd
    spans = LANES // 2 // segments
    lane = lax.broadcasted_iota(jnp.int32, (LANES, per_row * LANES), 1)
    at = lax.broadcasted_iota(jnp.int32, (LANES, per_row * LANES), 0)
    h, inner = lane // LANES, lane % LANES
    p, m = inner // (LANES // 2), inner % (LANES // 2)
    target = (m // spans) * width + h * fd + 4 * (m % spans) + 2 * p + core - at
    found = jnp.zeros((2 * rows, per_row * LANES), F32)
    for s in range(segments):
        one = jnp.where(target == s * width, 1.0, 0.0).astype(BF16)
        tile = rows_ref[s].astype(F32)
        found += jnp.dot(jnp.concatenate([tile, tile], axis=0).astype(BF16), one, preferred_element_type=F32)
    for r in range(rows):
        for k in range(per_row):
            g = r * per_row + k
            picks[:, g * LANES:(g + 1) * LANES] = jnp.where(
                order == found[r:r + 1, k * LANES:(k + 1) * LANES], 1.0, 0.0).astype(BF16)


def whiten(fd, half, prec_ref, kept, edges, whitened):
    frames = kept.shape[0]
    across = LANES // fd
    low = frames // across
    groups = prec_ref.shape[0] // fd
    lane = lax.broadcasted_iota(jnp.int32, edges.shape, 1)
    outer = (lane == 0) | (lane == LANES - 1)

    def frame_samples(f):
        ends = pltpu.roll(edges[...], (LANES - 2 * f) % LANES, 1)
        return jnp.where(outer, ends, kept[f].astype(F32)).astype(BF16)

    for u in range(half * low // 2, (half + 1) * low // 2):
        for v in range(0, across, 2):
            weight = jnp.concatenate([frame_samples((v + i) * low + u) for i in range(2)], axis=1)
            result = jnp.dot(prec_ref[...], weight, preferred_element_type=F32).astype(BF16)
            for i in range(2):
                at = (u * across + v + i) * fd
                for g in range(groups):
                    whitened[at:at + fd, g * LANES:(g + 1) * LANES] = (
                        result[g * fd:(g + 1) * fd, i * LANES:(i + 1) * LANES])


def tile_sums(half, picks, whitened, packed, part):
    tiles = picks.shape[0]
    size = whitened.shape[0] // 2
    wide = 2 * LANES
    low = size // LANES
    for n in range(size // wide):
        at = half * size + n * wide
        sums = lax.dot_general(picks[...], whitened[at:at + wide, :], CONTRACT, preferred_element_type=F32)
        for i in range(2):
            packed[half, pl.ds(2 * n + i, tiles, stride=low), :] = sums[:, i * LANES:(i + 1) * LANES]
    rows = part.shape[2]
    for owner in range(part.shape[1]):
        part[half, owner] = packed[half, owner * rows:(owner + 1) * rows, :].astype(part.dtype)


CHUNK = 32
PITCH = 4


def partial_scratch(half, fd, ft, tiles, x, precision):
    dets, samples = x.shape
    width = 2 * half
    blocks = (samples // width + 1) * (dets + PITCH)
    chunks = dets // CHUNK
    return [
        VMEM(x.shape, BF16),
        VMEM((precision.shape[0], 2 * dets), BF16),
        pltpu.SemaphoreType.DMA((8,)),
        pltpu.SemaphoreType.DMA,
        pltpu.SemaphoreType.DMA((chunks,)),
        pltpu.SemaphoreType.DMA((chunks,)),
        VMEM((2 * width, dets), F32),
        VMEM((dets, 2 * width), F32),
        VMEM((blocks, width), F32),
        VMEM((blocks, width), F32),
        VMEM((2, ft * (CHUNK + 1), LANES), F32),
        VMEM((ft, 2 * dets, LANES), BF16),
        VMEM((chunks, ft, CHUNK, LANES), BF16),
        VMEM((tiles, precision.shape[0] // fd * LANES), BF16),
        VMEM((ft * fd, precision.shape[0] // fd * LANES), BF16),
        VMEM((2, 2 * width, dets), F32),
        VMEM((width, dets), F32),
        VMEM((2 * dets, LANES), BF16),
        VMEM((2 * dets, LANES), F32),
        pltpu.SemaphoreType.DMA((2,)),
        VMEM((2, dets, width), BF16),
    ]


def part_shape(fd, ft, tiles):
    return (tiles // TILE_DEV, TILE_DEV * ft // (LANES // fd), LANES)


def plain_partial_sums(x, low, high, taps, rows, owner, precision, half, fd, ft, tiles):
    dets, samples = x.shape
    width = 2 * half
    groups = precision.shape[0] // fd
    blocks = samples // width
    padded = jnp.concatenate([low[:, -half:], x, high[:, :half]], axis=1).reshape(dets, blocks + 1, width)
    length = 4 * half + 1
    tiled = jnp.broadcast_to(jnp.pad(taps, ((0, 0), (0, length - taps.shape[1])))[:, None, :], (dets, width, length))
    matrix = tiled.reshape(dets, width * length)[:, :width * 2 * width].reshape(dets, width, 2 * width)
    near = jnp.einsum("dbj,dij->dbi", padded, matrix[:, :, :width], preferred_element_type=F32)
    far = jnp.einsum("dbj,dij->dbi", padded, matrix[:, :, width:], preferred_element_type=F32)
    filtered = (near[:, :-1] + far[:, 1:]).astype(BF16).reshape(dets, samples // ft, ft)
    order = jnp.argsort(owner_rows(owner)).astype(jnp.int32)
    rows = rows.reshape(rows.shape[0], groups, -1).transpose(1, 0, 2).reshape(groups, 1, -1)
    picks = (rows == order[None, :, None]).astype(BF16)
    sums = jnp.einsum("gkt,dtf->gkfd", picks, filtered, preferred_element_type=F32).astype(BF16)
    out = jnp.einsum("gkfd,gad->kfa", sums, precision.reshape(groups, fd, dets), preferred_element_type=F32)
    across = LANES // fd
    low_part = ft // across
    out = out.reshape(tiles, across, low_part, fd).transpose(0, 2, 1, 3)
    return out.reshape(tiles // TILE_DEV, TILE_DEV * low_part, LANES).astype(BF16)


def peer(me, step, n_tm, n_det):
    other = lax.rem(me + step, n_tm * n_det)
    return other, (other // n_det, lax.rem(other, n_det))


def greet(n_tm, n_det):
    me = lax.axis_index("tm") * n_det + lax.axis_index("det")
    barrier = pltpu.get_barrier_semaphore()
    for step in range(1, n_tm * n_det):
        pl.semaphore_signal(barrier, inc=1, device_id=peer(me, step, n_tm, n_det)[1], device_id_type=MESH)
    return me, barrier


def gather_body(n_tm, n_det, me, part_ref, left_ref, right_ref, out_ref, held, send_sem, recv_sem, own_sem):
    count = n_tm * n_det
    fd = left_ref.shape[0]
    copies = []
    far = range(n_det, count)
    for step in [*far, *range(1, n_det)]:
        other, where = peer(me, step, n_tm, n_det)
        copy = pltpu.make_async_remote_copy(
            src_ref=part_ref.at[other], dst_ref=held.at[me], send_sem=send_sem.at[step], recv_sem=recv_sem.at[step],
            device_id=where, device_id_type=MESH)
        copy.start()
        copies.append(copy)
    own = pltpu.make_async_copy(part_ref.at[me], held.at[me], own_sem)
    own.start()
    own.wait()
    for copy in copies:
        copy.wait()
    total = jnp.sum(held[...].astype(F32), axis=0)
    low = total.shape[0] // TILE_DEV
    across = total.shape[1] // fd
    tiles = []
    for k in range(TILE_DEV):
        tile = total[k * low:(k + 1) * low, :]
        stacked = jnp.concatenate([tile[:, v * fd:(v + 1) * fd] for v in range(across)], axis=0)
        rows = jnp.dot(stacked, left_ref[...], precision=lax.Precision.HIGHEST, preferred_element_type=F32)
        tiles.append(lax.dot_general(
            rows, right_ref[...], (((0,), (0,)), ((), ())), precision=lax.Precision.HIGHEST,
            preferred_element_type=F32))
    width = right_ref.shape[1]
    for i in range(left_ref.shape[1]):
        out_ref[:, i * width:(i + 1) * width] = jnp.concatenate([tile[i:i + 1, :] for tile in tiles], axis=0)


def gather_kernel(n_tm, n_det, part_ref, left_ref, right_ref, out_ref, *scratch):
    me, barrier = greet(n_tm, n_det)
    pl.semaphore_wait(barrier, n_tm * n_det - 1)
    gather_body(n_tm, n_det, me, part_ref, left_ref, right_ref, out_ref, *scratch)


def greet_lines(n_tm, n_det):
    tm, det = lax.axis_index("tm"), lax.axis_index("det")
    barrier = pltpu.get_barrier_semaphore()
    for step in range(1, n_tm):
        pl.semaphore_signal(barrier, inc=1, device_id=(lax.rem(tm + step, n_tm), det), device_id_type=MESH)
    for step in range(1, n_det):
        pl.semaphore_signal(barrier, inc=1, device_id=(tm, lax.rem(det + step, n_det)), device_id_type=MESH)
    return lambda: pl.semaphore_wait(barrier, n_tm + n_det - 2)


def send_parts(n_tm, n_det, half, part, held, send_sem, recv_sem, own_sem):
    me = lax.axis_index("tm") * n_det + lax.axis_index("det")
    count = n_tm * n_det
    copies = []
    for step in [*range(n_det, count), *range(1, n_det)]:
        other, where = peer(me, step, n_tm, n_det)
        copies.append(pltpu.make_async_remote_copy(
            src_ref=part.at[half, other], dst_ref=held.at[half, me], send_sem=send_sem.at[half, step],
            recv_sem=recv_sem.at[half, step], device_id=where, device_id_type=MESH))
    copies.append(pltpu.make_async_copy(part.at[half, me], held.at[half, me], own_sem.at[half]))
    for copy in copies:
        copy.start()
    return copies


def whole_kernel(n_tm, n_det, sizes, x_hbm, tapst_hbm, owner_hbm, prec_hbm, tile_hbm, count_hbm, out_ref, low, high, held_rows, own_rows, *rest):
    half, fd, ft, tiles = sizes
    edge, rest = rest[:5], rest[5:]
    (part, held, part_send, part_recv, part_own, packed, planes, tapst_ref, owner_ref, tile_ref, count_ref, small_sem), rest = rest[:12], rest[12:]
    (x_ref, prec_ref, load_sem, prec_sem, pair_send, pair_recv, wide, taps_ref, cur, mid, stage, kept, sent, picks,
     whitened, turned, ends, both, edges, swap_sem, rims) = rest
    tm, det = lax.axis_index("tm"), lax.axis_index("det")
    core = lax.rem(det, 2)
    dets = x_ref.shape[0]
    pitch = dets + PITCH
    unroll = sent.shape[2]
    meet = greet_lines(n_tm, n_det)
    small = [
        pltpu.make_async_copy(source, target, small_sem.at[i]) for i, (source, target) in enumerate((
            (tile_hbm, tile_ref), (count_hbm, count_ref), (tapst_hbm, tapst_ref), (owner_hbm, owner_ref),
            (x_hbm.at[:, 0:2 * half], rims.at[0]), (x_hbm.at[:, x_ref.shape[1] - 2 * half:], rims.at[1])))]
    for copy in small:
        copy.start()
    build = load_blocks(half, x_hbm, x_ref, load_sem, cur, mid, pitch)
    first = pl.multiple_of((det - core) * dets, 2 * dets)
    load = pltpu.make_async_copy(prec_hbm.at[:, pl.ds(first, 2 * dets)], prec_ref, prec_sem)
    load.start()
    next(build)
    small[0].wait()
    small[1].wait()
    live_rows(tile_ref, count_ref[0], own_rows)
    meet()
    for copy in small[4:]:
        copy.wait()
    finish_edges, finish_rows = start_edges(
        n_tm, n_det, rims.at[0], rims.at[1], low, high, held_rows, own_rows, *edge)
    for step in range(1, n_tm):
        pl.semaphore_signal(planes, inc=1, device_id=(lax.rem(tm + step, n_tm), det), device_id_type=MESH)
    small[2].wait()
    spread_taps(tapst_ref, wide, taps_ref)
    for _ in build:
        pass
    edge_blocks(half, x_ref, cur, mid, pitch)

    def send(c):
        at = pl.multiple_of(core * dets + c * unroll, unroll)
        return pltpu.make_async_remote_copy(
            src_ref=sent.at[c], dst_ref=kept.at[:, pl.ds(at, unroll), :], send_sem=pair_send.at[c],
            recv_sem=pair_recv.at[c], device_id=(tm, det + 1 - 2 * core), device_id_type=MESH)

    own = pl.ds(pl.multiple_of(core * dets, dets), dets)
    swap = pltpu.make_async_remote_copy(
        src_ref=both.at[own], dst_ref=both.at[own], send_sem=swap_sem.at[0], recv_sem=swap_sem.at[1],
        device_id=(tm, det + 1 - 2 * core), device_id_type=MESH)

    def edges_between():
        finish_edges()
        both[own, :] = filter_edges(
            half, ft, x_ref, low, high, cur, mid, pitch, wide, turned, ends).astype(BF16)

    filter_chunks(half, ft, core, cur, mid, pitch, taps_ref, stage, kept, sent, send, edges_between)
    swap.start()
    small[3].wait()
    finish_rows()
    pick_frames(core, fd, ft, owner_order(owner_ref, tiles), held_rows, picks)
    load.wait()
    swap.wait()
    edges[...] = pltpu.roll(both[...].astype(F32), half * core, 1)
    for c in range(sent.shape[0]):
        send(c).wait()
    waits = []
    for h in range(2):
        whiten(fd, h, prec_ref, kept, edges, whitened)
    for h in range(2):
        tile_sums(h, picks, whitened, packed, part)
        if h == 0:
            pl.semaphore_wait(planes, n_tm - 1)
        waits.append(send_parts(n_tm, n_det, h, part, held, part_send, part_recv, part_own))
    for h in range(2):
        for copy in waits[h]:
            copy.wait()
        out_ref[h] = jnp.sum(held[h].astype(F32), axis=0)


def reduce_scratch(count, fd, ft, tiles, small, live):
    rows = TILE_DEV * ft * fd // LANES // 2
    return [
        VMEM((2, count, rows, LANES), BF16),
        VMEM((2, count, rows, LANES), BF16),
        pltpu.SemaphoreType.DMA((2, count)),
        pltpu.SemaphoreType.DMA((2, count)),
        pltpu.SemaphoreType.DMA((2,)),
        VMEM((2, count * rows, LANES), F32),
        pltpu.SemaphoreType.REGULAR,
    ] + [VMEM(array.shape, array.dtype) for array in small] + [
        pltpu.SMEM(live.shape, live.dtype),
        pltpu.SemaphoreType.DMA((len(small) + 3,)),
    ]


def project_kernel(sums_ref, left_ref, right_ref, out_hbm, out_ref, sem):
    fd = left_ref.shape[0]
    low = sums_ref.shape[1] // TILE_DEV
    tiles = []
    for k in range(TILE_DEV):
        tile = jnp.concatenate([sums_ref[h, k * low:(k + 1) * low, :] for h in range(2)], axis=0)
        stacked = jnp.concatenate([tile[:, v * fd:(v + 1) * fd] for v in range(LANES // fd)], axis=0)
        rows = jnp.dot(stacked, left_ref[...], precision=lax.Precision.HIGHEST, preferred_element_type=F32)
        tiles.append(lax.dot_general(
            rows, right_ref[...], (((0,), (0,)), ((), ())), precision=lax.Precision.HIGHEST,
            preferred_element_type=F32))
    width = right_ref.shape[1]
    total = left_ref.shape[1]
    pieces = sem.shape[0]
    span = total // pieces
    copies = []
    for piece in range(pieces):
        for i in range(piece * span, (piece + 1) * span):
            out_ref[:, i * width:(i + 1) * width] = jnp.concatenate([tile[i:i + 1, :] for tile in tiles], axis=0)
        part = pl.ds(piece * span * width, span * width)
        copy = pltpu.make_async_copy(out_ref.at[:, part], out_hbm.at[:, part], sem.at[piece])
        copy.start()
        copies.append(copy)
    for copy in copies:
        copy.wait()


def gather_scratch(count, shape):
    return [
        VMEM(shape, BF16),
        pltpu.SemaphoreType.DMA((count,)),
        pltpu.SemaphoreType.DMA((count,)),
        pltpu.SemaphoreType.DMA,
    ]


def call(kernel, specs, inputs, scratch, out, name):
    return pl.pallas_call(
        kernel,
        out_shape=jax.ShapeDtypeStruct(out, F32),
        in_specs=[pl.BlockSpec(memory_space=space) for space in specs],
        out_specs=pl.BlockSpec(memory_space=VMEM),
        scratch_shapes=scratch,
        compiler_params=pltpu.CompilerParams(
            collective_id=1, has_side_effects=True, vmem_limit_bytes=60 * 1024 * 1024),
        name=name,
    )(*inputs)


def local(
    n_tm, n_det,
    time_stream, filter_taps, det_precision, left_weight, right_weight, frame_tile, tile_owner, frame_count,
):
    half = filter_taps.shape[1] // 2
    fd, ft = left_weight.shape[1], right_weight.shape[1]
    dets = time_stream.shape[0]
    tiles = tile_owner.shape[0]
    count = n_tm * n_det
    tile = frame_tile.reshape(-1, LANES)
    sizes = (half, fd, ft, tiles)
    shape = part_shape(fd, ft, tiles)
    flat = left_weight.shape[0] * right_weight.shape[0]
    weights = (left_weight.T, right_weight.T)
    gather = gather_scratch(count, shape)
    if fast_path(n_tm, n_det, half, fd, ft, time_stream):
        taps, owner = filter_taps.T, tile_owner.reshape(1, -1)
        inputs = (time_stream, taps, owner, det_precision, tile, frame_count)
        specs = (pl.ANY,) * len(inputs)
        halo = VMEM((dets, 2 * half), BF16)
        scratch = [halo, halo, VMEM((n_det,) + tile.shape, tile.dtype), VMEM(tile.shape, tile.dtype)]
        scratch += edge_sems(n_det) + reduce_scratch(count, fd, ft, tiles, (taps, owner, tile), frame_count)
        scratch += partial_scratch(half, fd, ft, tiles, time_stream, det_precision)
        out = (2, TILE_DEV * ft * fd // LANES // 2, LANES)
        sums = call(functools.partial(whole_kernel, n_tm, n_det, sizes), specs, inputs, scratch, out, "whole")
        return pl.pallas_call(
            project_kernel,
            out_shape=jax.ShapeDtypeStruct((TILE_DEV, flat), F32),
            in_specs=[pl.BlockSpec(memory_space=VMEM)] * 3,
            out_specs=pl.BlockSpec(memory_space=pl.ANY),
            scratch_shapes=[VMEM((TILE_DEV, flat), F32), pltpu.SemaphoreType.DMA((4,))],
            name="project",
        )(sums, *weights)
    low, high, rows = exchange_edges(n_tm, n_det, 2 * half, time_stream, tile, frame_count)
    precision = lax.dynamic_slice_in_dim(det_precision, lax.axis_index("det") * dets, dets, axis=1)
    part = plain_partial_sums(time_stream, low, high, filter_taps, rows, tile_owner, precision, *sizes)
    return call(functools.partial(gather_kernel, n_tm, n_det), (VMEM,) * 3, (part,) + weights, gather, (TILE_DEV, flat), "gather")


def solution(mesh):
    return jax.shard_map(
        functools.partial(local, mesh.shape["tm"], mesh.shape["det"]),
        mesh=mesh,
        in_specs=(
            P("det", "tm"),
            P("det", None),
            P(),
            P(),
            P(),
            P(("tm", "det"), None),
            P(),
            P(("tm", "det")),
        ),
        out_specs=P(("tm", "det"), None),
        check_vma=False,
    )
```

```python
import functools

import jax
import jax.numpy as jnp
from jax import lax
from jax.experimental import pallas as pl
from jax.experimental.pallas import tpu as pltpu
from jax.sharding import PartitionSpec as P

TILE_DEV = 2
LANES = 128
MESH = pl.DeviceIdType.MESH
VMEM = pltpu.VMEM
F32 = jnp.float32
BF16 = jnp.bfloat16
CONTRACT = (((1,), (1,)), ((), ()))


def owner_rows(tile_owner):
    total_tiles = tile_owner.shape[0]
    same_owner = tile_owner[:, None] == tile_owner[None, :]
    earlier = jnp.arange(total_tiles)[None, :] < jnp.arange(total_tiles)[:, None]
    slot_rank = jnp.sum((same_owner & earlier).astype(jnp.int32), axis=1)
    return tile_owner * TILE_DEV + slot_rank


def start_edges(n_tm, n_det, first_ref, last_ref, low_ref, high_ref, all_ref, rows_ref, send_sem, recv_sem, halo_send, halo_recv, own_sem):
    tm, det = lax.axis_index("tm"), lax.axis_index("det")
    has_low, has_high = tm > 0, tm < n_tm - 1
    down = pltpu.make_async_remote_copy(
        src_ref=first_ref, dst_ref=high_ref, send_sem=halo_send.at[0], recv_sem=halo_recv.at[0],
        device_id=(tm - 1, det), device_id_type=MESH)
    up = pltpu.make_async_remote_copy(
        src_ref=last_ref, dst_ref=low_ref, send_sem=halo_send.at[1], recv_sem=halo_recv.at[1],
        device_id=(tm + 1, det), device_id_type=MESH)

    @pl.when(has_low)
    def _():
        down.start()

    @pl.when(has_high)
    def _():
        up.start()

    copies = []
    for step in range(1, n_det):
        copy = pltpu.make_async_remote_copy(
            src_ref=rows_ref, dst_ref=all_ref.at[det], send_sem=send_sem.at[step], recv_sem=recv_sem.at[step],
            device_id=(tm, lax.rem(det + step, n_det)), device_id_type=MESH)
        copy.start()
        copies.append(copy)
    own = pltpu.make_async_copy(rows_ref, all_ref.at[det], own_sem)
    own.start()

    @pl.when(jnp.logical_not(has_low))
    def _():
        low_ref[...] = jnp.zeros_like(low_ref)

    @pl.when(jnp.logical_not(has_high))
    def _():
        high_ref[...] = jnp.zeros_like(high_ref)

    def finish_rows():
        own.wait()
        for copy in copies:
            copy.wait()

    def finish_edges():
        @pl.when(has_low)
        def _():
            down.wait_send()
            up.wait_recv()

        @pl.when(has_high)
        def _():
            up.wait_send()
            down.wait_recv()

    return finish_edges, finish_rows


def live_rows(tile_ref, count, rows_ref):
    tile = tile_ref[...]
    frame = lax.broadcasted_iota(jnp.int32, tile.shape, 0) * tile.shape[1] + lax.broadcasted_iota(jnp.int32, tile.shape, 1)
    rows_ref[...] = jnp.where(frame < count, tile, -1)


def edge_kernel(n_tm, n_det, width, x_ref, tile_ref, count_ref, low_ref, high_ref, all_ref, rows_ref, *sems):
    tm, det = lax.axis_index("tm"), lax.axis_index("det")
    has_low, has_high = tm > 0, tm < n_tm - 1
    barrier = pltpu.get_barrier_semaphore()
    for step in range(1, n_det):
        pl.semaphore_signal(barrier, inc=1, device_id=(tm, lax.rem(det + step, n_det)), device_id_type=MESH)

    @pl.when(has_low)
    def _():
        pl.semaphore_signal(barrier, inc=1, device_id=(tm - 1, det), device_id_type=MESH)

    @pl.when(has_high)
    def _():
        pl.semaphore_signal(barrier, inc=1, device_id=(tm + 1, det), device_id_type=MESH)

    live_rows(tile_ref, count_ref[0], rows_ref)
    pl.semaphore_wait(barrier, n_det - 1 + has_low.astype(jnp.int32) + has_high.astype(jnp.int32))
    for finish in start_edges(
            n_tm, n_det, x_ref.at[:, 0:width], x_ref.at[:, x_ref.shape[1] - width:], low_ref, high_ref, all_ref, rows_ref,
            *sems):
        finish()


def edge_sems(n_det):
    return [
        pltpu.SemaphoreType.DMA((n_det,)),
        pltpu.SemaphoreType.DMA((n_det,)),
        pltpu.SemaphoreType.DMA((2,)),
        pltpu.SemaphoreType.DMA((2,)),
        pltpu.SemaphoreType.DMA,
    ]


def exchange_edges(n_tm, n_det, width, x, tile, count):
    vmem = pl.BlockSpec(memory_space=VMEM)
    halo = jax.ShapeDtypeStruct((x.shape[0], width), x.dtype)
    return pl.pallas_call(
        functools.partial(edge_kernel, n_tm, n_det, width),
        out_shape=(halo, halo, jax.ShapeDtypeStruct((n_det,) + tile.shape, tile.dtype)),
        in_specs=[pl.BlockSpec(memory_space=pl.ANY), vmem, pl.BlockSpec(memory_space=pltpu.SMEM)],
        out_specs=(vmem,) * 3,
        scratch_shapes=[
            VMEM(tile.shape, tile.dtype),
        ] + edge_sems(n_det),
        compiler_params=pltpu.CompilerParams(collective_id=0, has_side_effects=True),
        name="edges",
    )(x, tile, count)


def fast_path(n_tm, n_det, half, fd, ft, x):
    width = 2 * half
    return (
        n_det % 2 == 0 and x.shape[0] == LANES and width == LANES and x.shape[1] == half * LANES
        and fd == ft and half == 2 * ft and (x.shape[1] // ft) % (4 * n_det) == 0)


def load_blocks(half, x_hbm, x_ref, load_sem, cur, mid, pitch):
    dets, samples = x_ref.shape
    width = 2 * half
    pieces = load_sem.shape[0]
    span = samples // pieces
    loads = []
    for piece in range(pieces):
        part = pl.ds(piece * span, span)
        load = pltpu.make_async_copy(x_hbm.at[:, part], x_ref.at[:, part], load_sem.at[piece])
        load.start()
        loads.append(load)

    def finish():
        per = span // width
        left = lax.broadcasted_iota(jnp.int32, (dets, width), 1) < half
        before = None
        for piece, load in enumerate(loads):
            load.wait()
            for b in range(piece * per, (piece + 1) * per):
                at = b * width
                block = x_ref[:, at:at + width].astype(F32)
                cur[b * pitch:b * pitch + dets, :] = block
                turned = pltpu.roll(block, half, 1)
                if b:
                    mid[b * pitch:b * pitch + dets, :] = jnp.where(left, before, turned)
                before = turned
            if piece == pieces * 3 // 4 - 1:
                yield

    return finish()


def edge_blocks(half, x_ref, cur, mid, pitch):
    dets, samples = x_ref.shape
    last = samples // (2 * half) * pitch
    none = jnp.zeros((dets, half), BF16)
    mid[0:dets, :] = jnp.concatenate([none, x_ref[:, 0:half]], axis=1).astype(F32)
    mid[last:last + dets, :] = jnp.concatenate([x_ref[:, samples - half:], none], axis=1).astype(F32)
    cur[last:last + dets, :] = jnp.zeros((dets, 2 * half), F32)


def filter_edges(half, ft, x_ref, low_ref, high_ref, cur, mid, pitch, wide, turned, ends):
    dets, samples = x_ref.shape
    width = 2 * half
    last = (samples // width - 1) * pitch
    first = jnp.concatenate([low_ref[:, half:], x_ref[:, 0:half]], axis=1)
    turned[0, 0:width, :] = first.astype(F32).T
    turned[0, width:, :] = mid[pitch:pitch + dets, :].T
    turned[1, 0:width, :] = cur[last:last + dets, :].T
    turned[1, width:, :] = high_ref[...].astype(F32).T
    sums = []
    for e in range(2):
        total = jnp.zeros((half, dets), F32)
        for r in range(8):
            taps = range(r, width + 1, 8)
            shifted = turned[e, r:taps[-1] + half, :]
            for k in taps:
                total += shifted[k - r:k - r + half, :] * wide[k:k + 1, :]
        sums.append(total)
    low, high = sums
    for q in range(2):
        ends[pl.ds(q * half, ft, stride=2), :] = low[q * ft:(q + 1) * ft, :]
    ends[pl.ds(half - 1, ft, stride=2), :] = high[ft:, :]
    ends[pl.ds(1, ft - 1, stride=2), :] = high[1:ft, :]
    ends[width - 1:, :] = high[0:1, :]
    return ends[...].T


def spread_taps(tapst_ref, wide, taps_ref):
    wide[...] = jnp.zeros(wide.shape, F32)
    wide[0:tapst_ref.shape[0], :] = tapst_ref[...].astype(F32)
    taps_ref[...] = wide[...].T


def owner_order(owner_ref, tiles):
    across_owner = jnp.broadcast_to(owner_ref[...].astype(F32), (tiles, tiles))
    down = lax.broadcasted_iota(jnp.int32, (tiles, tiles), 0)
    across_tile = lax.broadcasted_iota(jnp.int32, (tiles, tiles), 1)
    earlier = (across_owner.T == across_owner) & (down < across_tile)
    rank = jnp.sum(jnp.where(earlier, 1.0, 0.0), axis=0, keepdims=True)
    place = across_owner * TILE_DEV + rank
    order = jnp.sum(jnp.where(place == down.astype(F32), across_tile.astype(F32), 0.0), axis=1, keepdims=True)
    return jnp.broadcast_to(order, (tiles, LANES))


def filter_chunks(half, ft, core, cur, mid, pitch, taps_ref, stage, kept, sent, send, before_last):
    chunks, frames, unroll, _ = sent.shape
    dets = chunks * unroll
    blocks = LANES // 2
    step_rows = stage.shape[1] // ft

    def chunk_step(c, carry):
        for k in range(unroll):
            d = c * unroll + k
            spread = jnp.broadcast_to(taps_ref[pl.ds(d, 1), :], (half, 4 * half))
            matrix = pltpu.roll(spread, 0, 1, stride=1, stride_axis=0).astype(BF16)
            rows = []
            for source in (mid, cur):
                lower = source[pl.ds(d, blocks, stride=pitch), :]
                upper = source[pl.ds(d + pitch, blocks, stride=pitch), :]
                rows.append(jnp.concatenate([lower, upper], axis=1))
            window = jnp.concatenate(rows, axis=0).astype(BF16)
            result = lax.dot_general(matrix, window, CONTRACT, preferred_element_type=F32)
            for q in range(2):
                stage[q, pl.ds(k, ft, stride=step_rows), :] = result[q * ft:(q + 1) * ft, :]
        at = pl.multiple_of(core * dets + c * unroll, unroll)
        for f in range(frames):
            rows = slice(f * step_rows, f * step_rows + unroll)
            kept[f, pl.ds(at, unroll), :] = stage[core, rows, :].astype(BF16)
            sent[c, f] = stage[1 - core, rows, :].astype(BF16)
        send(c).start()
        return carry

    lax.fori_loop(0, chunks - 1, chunk_step, 0)
    before_last()
    chunk_step(chunks - 1, 0)


def pick_frames(core, fd, ft, order, rows_ref, picks):
    segments, rows, width = rows_ref.shape
    tiles = order.shape[0]
    per_row = width // fd
    spans = LANES // 2 // segments
    lane = lax.broadcasted_iota(jnp.int32, (LANES, per_row * LANES), 1)
    at = lax.broadcasted_iota(jnp.int32, (LANES, per_row * LANES), 0)
    h, inner = lane // LANES, lane % LANES
    p, m = inner // (LANES // 2), inner % (LANES // 2)
    target = (m // spans) * width + h * fd + 4 * (m % spans) + 2 * p + core - at
    found = jnp.zeros((2 * rows, per_row * LANES), F32)
    for s in range(segments):
        one = jnp.where(target == s * width, 1.0, 0.0).astype(BF16)
        tile = rows_ref[s].astype(F32)
        found += jnp.dot(jnp.concatenate([tile, tile], axis=0).astype(BF16), one, preferred_element_type=F32)
    for r in range(rows):
        for k in range(per_row):
            g = r * per_row + k
            picks[:, g * LANES:(g + 1) * LANES] = jnp.where(
                order == found[r:r + 1, k * LANES:(k + 1) * LANES], 1.0, 0.0).astype(BF16)


def whiten(fd, half, prec_ref, kept, edges, whitened):
    frames = kept.shape[0]
    across = LANES // fd
    low = frames // across
    groups = prec_ref.shape[0] // fd
    lane = lax.broadcasted_iota(jnp.int32, edges.shape, 1)
    outer = (lane == 0) | (lane == LANES - 1)

    def frame_samples(f):
        ends = pltpu.roll(edges[...], (LANES - 2 * f) % LANES, 1)
        return jnp.where(outer, ends, kept[f].astype(F32)).astype(BF16)

    for u in range(half * low // 2, (half + 1) * low // 2):
        for v in range(0, across, 2):
            weight = jnp.concatenate([frame_samples((v + i) * low + u) for i in range(2)], axis=1)
            result = jnp.dot(prec_ref[...], weight, preferred_element_type=F32).astype(BF16)
            for i in range(2):
                at = (u * across + v + i) * fd
                for g in range(groups):
                    whitened[at:at + fd, g * LANES:(g + 1) * LANES] = (
                        result[g * fd:(g + 1) * fd, i * LANES:(i + 1) * LANES])


def tile_sums(half, picks, whitened, packed, part):
    tiles = picks.shape[0]
    size = whitened.shape[0] // 2
    wide = 2 * LANES
    low = size // LANES
    for n in range(size // wide):
        at = half * size + n * wide
        sums = lax.dot_general(picks[...], whitened[at:at + wide, :], CONTRACT, preferred_element_type=F32)
        for i in range(2):
            packed[half, pl.ds(2 * n + i, tiles, stride=low), :] = sums[:, i * LANES:(i + 1) * LANES]
    rows = part.shape[2]
    for owner in range(part.shape[1]):
        part[half, owner] = packed[half, owner * rows:(owner + 1) * rows, :].astype(part.dtype)


CHUNK = 32
PITCH = 4


def partial_scratch(half, fd, ft, tiles, x, precision):
    dets, samples = x.shape
    width = 2 * half
    blocks = (samples // width + 1) * (dets + PITCH)
    chunks = dets // CHUNK
    return [
        VMEM(x.shape, BF16),
        VMEM((precision.shape[0], 2 * dets), BF16),
        pltpu.SemaphoreType.DMA((8,)),
        pltpu.SemaphoreType.DMA,
        pltpu.SemaphoreType.DMA((chunks,)),
        pltpu.SemaphoreType.DMA((chunks,)),
        VMEM((2 * width, dets), F32),
        VMEM((dets, 2 * width), F32),
        VMEM((blocks, width), F32),
        VMEM((blocks, width), F32),
        VMEM((2, ft * (CHUNK + 1), LANES), F32),
        VMEM((ft, 2 * dets, LANES), BF16),
        VMEM((chunks, ft, CHUNK, LANES), BF16),
        VMEM((tiles, precision.shape[0] // fd * LANES), BF16),
        VMEM((ft * fd, precision.shape[0] // fd * LANES), BF16),
        VMEM((2, 2 * width, dets), F32),
        VMEM((width, dets), F32),
        VMEM((2 * dets, LANES), BF16),
        VMEM((2 * dets, LANES), F32),
        pltpu.SemaphoreType.DMA((2,)),
        VMEM((2, dets, width), BF16),
    ]


def part_shape(fd, ft, tiles):
    return (tiles // TILE_DEV, TILE_DEV * ft // (LANES // fd), LANES)


def plain_partial_sums(x, low, high, taps, rows, owner, precision, half, fd, ft, tiles):
    dets, samples = x.shape
    width = 2 * half
    groups = precision.shape[0] // fd
    blocks = samples // width
    padded = jnp.concatenate([low[:, -half:], x, high[:, :half]], axis=1).reshape(dets, blocks + 1, width)
    length = 4 * half + 1
    tiled = jnp.broadcast_to(jnp.pad(taps, ((0, 0), (0, length - taps.shape[1])))[:, None, :], (dets, width, length))
    matrix = tiled.reshape(dets, width * length)[:, :width * 2 * width].reshape(dets, width, 2 * width)
    near = jnp.einsum("dbj,dij->dbi", padded, matrix[:, :, :width], preferred_element_type=F32)
    far = jnp.einsum("dbj,dij->dbi", padded, matrix[:, :, width:], preferred_element_type=F32)
    filtered = (near[:, :-1] + far[:, 1:]).astype(BF16).reshape(dets, samples // ft, ft)
    order = jnp.argsort(owner_rows(owner)).astype(jnp.int32)
    rows = rows.reshape(rows.shape[0], groups, -1).transpose(1, 0, 2).reshape(groups, 1, -1)
    picks = (rows == order[None, :, None]).astype(BF16)
    sums = jnp.einsum("gkt,dtf->gkfd", picks, filtered, preferred_element_type=F32).astype(BF16)
    out = jnp.einsum("gkfd,gad->kfa", sums, precision.reshape(groups, fd, dets), preferred_element_type=F32)
    across = LANES // fd
    low_part = ft // across
    out = out.reshape(tiles, across, low_part, fd).transpose(0, 2, 1, 3)
    return out.reshape(tiles // TILE_DEV, TILE_DEV * low_part, LANES).astype(BF16)


def peer(me, step, n_tm, n_det):
    other = lax.rem(me + step, n_tm * n_det)
    return other, (other // n_det, lax.rem(other, n_det))


def greet(n_tm, n_det):
    me = lax.axis_index("tm") * n_det + lax.axis_index("det")
    barrier = pltpu.get_barrier_semaphore()
    for step in range(1, n_tm * n_det):
        pl.semaphore_signal(barrier, inc=1, device_id=peer(me, step, n_tm, n_det)[1], device_id_type=MESH)
    return me, barrier


def gather_body(n_tm, n_det, me, part_ref, left_ref, right_ref, out_ref, held, send_sem, recv_sem, own_sem):
    count = n_tm * n_det
    fd = left_ref.shape[0]
    copies = []
    far = range(n_det, count)
    for step in [*far, *range(1, n_det)]:
        other, where = peer(me, step, n_tm, n_det)
        copy = pltpu.make_async_remote_copy(
            src_ref=part_ref.at[other], dst_ref=held.at[me], send_sem=send_sem.at[step], recv_sem=recv_sem.at[step],
            device_id=where, device_id_type=MESH)
        copy.start()
        copies.append(copy)
    own = pltpu.make_async_copy(part_ref.at[me], held.at[me], own_sem)
    own.start()
    own.wait()
    for copy in copies:
        copy.wait()
    total = jnp.sum(held[...].astype(F32), axis=0)
    low = total.shape[0] // TILE_DEV
    across = total.shape[1] // fd
    tiles = []
    for k in range(TILE_DEV):
        tile = total[k * low:(k + 1) * low, :]
        stacked = jnp.concatenate([tile[:, v * fd:(v + 1) * fd] for v in range(across)], axis=0)
        rows = jnp.dot(stacked, left_ref[...], precision=lax.Precision.HIGHEST, preferred_element_type=F32)
        tiles.append(lax.dot_general(
            rows, right_ref[...], (((0,), (0,)), ((), ())), precision=lax.Precision.HIGHEST,
            preferred_element_type=F32))
    width = right_ref.shape[1]
    for i in range(left_ref.shape[1]):
        out_ref[:, i * width:(i + 1) * width] = jnp.concatenate([tile[i:i + 1, :] for tile in tiles], axis=0)


def gather_kernel(n_tm, n_det, part_ref, left_ref, right_ref, out_ref, *scratch):
    me, barrier = greet(n_tm, n_det)
    pl.semaphore_wait(barrier, n_tm * n_det - 1)
    gather_body(n_tm, n_det, me, part_ref, left_ref, right_ref, out_ref, *scratch)


def greet_lines(n_tm, n_det):
    tm, det = lax.axis_index("tm"), lax.axis_index("det")
    barrier = pltpu.get_barrier_semaphore()
    for step in range(1, n_tm):
        pl.semaphore_signal(barrier, inc=1, device_id=(lax.rem(tm + step, n_tm), det), device_id_type=MESH)
    for step in range(1, n_det):
        pl.semaphore_signal(barrier, inc=1, device_id=(tm, lax.rem(det + step, n_det)), device_id_type=MESH)
    return lambda: pl.semaphore_wait(barrier, n_tm + n_det - 2)


def send_parts(n_tm, n_det, half, part, held, send_sem, recv_sem, own_sem):
    me = lax.axis_index("tm") * n_det + lax.axis_index("det")
    count = n_tm * n_det
    copies = []
    for step in [*range(n_det, count), *range(1, n_det)]:
        other, where = peer(me, step, n_tm, n_det)
        copies.append(pltpu.make_async_remote_copy(
            src_ref=part.at[half, other], dst_ref=held.at[half, me], send_sem=send_sem.at[half, step],
            recv_sem=recv_sem.at[half, step], device_id=where, device_id_type=MESH))
    copies.append(pltpu.make_async_copy(part.at[half, me], held.at[half, me], own_sem.at[half]))
    for copy in copies:
        copy.start()
    return copies


def whole_kernel(n_tm, n_det, sizes, x_hbm, tapst_hbm, owner_hbm, prec_hbm, tile_hbm, count_hbm, out_ref, low, high, held_rows, own_rows, *rest):
    half, fd, ft, tiles = sizes
    edge, rest = rest[:5], rest[5:]
    (part, held, part_send, part_recv, part_own, packed, planes, tapst_ref, owner_ref, tile_ref, count_ref, small_sem), rest = rest[:12], rest[12:]
    (x_ref, prec_ref, load_sem, prec_sem, pair_send, pair_recv, wide, taps_ref, cur, mid, stage, kept, sent, picks,
     whitened, turned, ends, both, edges, swap_sem, rims) = rest
    tm, det = lax.axis_index("tm"), lax.axis_index("det")
    core = lax.rem(det, 2)
    dets = x_ref.shape[0]
    pitch = dets + PITCH
    unroll = sent.shape[2]
    meet = greet_lines(n_tm, n_det)
    small = [
        pltpu.make_async_copy(source, target, small_sem.at[i]) for i, (source, target) in enumerate((
            (tile_hbm, tile_ref), (count_hbm, count_ref), (tapst_hbm, tapst_ref), (owner_hbm, owner_ref),
            (x_hbm.at[:, 0:2 * half], rims.at[0]), (x_hbm.at[:, x_ref.shape[1] - 2 * half:], rims.at[1])))]
    for copy in small:
        copy.start()
    build = load_blocks(half, x_hbm, x_ref, load_sem, cur, mid, pitch)
    first = pl.multiple_of((det - core) * dets, 2 * dets)
    load = pltpu.make_async_copy(prec_hbm.at[:, pl.ds(first, 2 * dets)], prec_ref, prec_sem)
    load.start()
    next(build)
    small[0].wait()
    small[1].wait()
    live_rows(tile_ref, count_ref[0], own_rows)
    meet()
    for copy in small[4:]:
        copy.wait()
    finish_edges, finish_rows = start_edges(
        n_tm, n_det, rims.at[0], rims.at[1], low, high, held_rows, own_rows, *edge)
    for step in range(1, n_tm):
        pl.semaphore_signal(planes, inc=1, device_id=(lax.rem(tm + step, n_tm), det), device_id_type=MESH)
    small[2].wait()
    spread_taps(tapst_ref, wide, taps_ref)
    for _ in build:
        pass
    edge_blocks(half, x_ref, cur, mid, pitch)

    def send(c):
        at = pl.multiple_of(core * dets + c * unroll, unroll)
        return pltpu.make_async_remote_copy(
            src_ref=sent.at[c], dst_ref=kept.at[:, pl.ds(at, unroll), :], send_sem=pair_send.at[c],
            recv_sem=pair_recv.at[c], device_id=(tm, det + 1 - 2 * core), device_id_type=MESH)

    own = pl.ds(pl.multiple_of(core * dets, dets), dets)
    swap = pltpu.make_async_remote_copy(
        src_ref=both.at[own], dst_ref=both.at[own], send_sem=swap_sem.at[0], recv_sem=swap_sem.at[1],
        device_id=(tm, det + 1 - 2 * core), device_id_type=MESH)

    def edges_between():
        finish_edges()
        both[own, :] = filter_edges(
            half, ft, x_ref, low, high, cur, mid, pitch, wide, turned, ends).astype(BF16)

    filter_chunks(half, ft, core, cur, mid, pitch, taps_ref, stage, kept, sent, send, edges_between)
    swap.start()
    small[3].wait()
    finish_rows()
    pick_frames(core, fd, ft, owner_order(owner_ref, tiles), held_rows, picks)
    load.wait()
    swap.wait()
    edges[...] = pltpu.roll(both[...].astype(F32), half * core, 1)
    for c in range(sent.shape[0]):
        send(c).wait()
    waits = []
    for h in range(2):
        whiten(fd, h, prec_ref, kept, edges, whitened)
    for h in range(2):
        tile_sums(h, picks, whitened, packed, part)
        if h == 0:
            pl.semaphore_wait(planes, n_tm - 1)
        waits.append(send_parts(n_tm, n_det, h, part, held, part_send, part_recv, part_own))
    for h in range(2):
        for copy in waits[h]:
            copy.wait()
        out_ref[h] = jnp.sum(held[h].astype(F32), axis=0)


def reduce_scratch(count, fd, ft, tiles, small, live):
    rows = TILE_DEV * ft * fd // LANES // 2
    return [
        VMEM((2, count, rows, LANES), BF16),
        VMEM((2, count, rows, LANES), BF16),
        pltpu.SemaphoreType.DMA((2, count)),
        pltpu.SemaphoreType.DMA((2, count)),
        pltpu.SemaphoreType.DMA((2,)),
        VMEM((2, count * rows, LANES), F32),
        pltpu.SemaphoreType.REGULAR,
    ] + [VMEM(array.shape, array.dtype) for array in small] + [
        pltpu.SMEM(live.shape, live.dtype),
        pltpu.SemaphoreType.DMA((len(small) + 3,)),
    ]


def project_kernel(sums_ref, left_ref, right_ref, out_hbm, out_ref, sem):
    fd = left_ref.shape[0]
    low = sums_ref.shape[1] // TILE_DEV
    tiles = []
    for k in range(TILE_DEV):
        tile = jnp.concatenate([sums_ref[h, k * low:(k + 1) * low, :] for h in range(2)], axis=0)
        stacked = jnp.concatenate([tile[:, v * fd:(v + 1) * fd] for v in range(LANES // fd)], axis=0)
        rows = jnp.dot(stacked, left_ref[...], precision=lax.Precision.HIGHEST, preferred_element_type=F32)
        tiles.append(lax.dot_general(
            rows, right_ref[...], (((0,), (0,)), ((), ())), precision=lax.Precision.HIGHEST,
            preferred_element_type=F32))
    width = right_ref.shape[1]
    total = left_ref.shape[1]
    pieces = sem.shape[0]
    span = total // pieces
    copies = []
    for piece in range(pieces):
        for i in range(piece * span, (piece + 1) * span):
            out_ref[:, i * width:(i + 1) * width] = jnp.concatenate([tile[i:i + 1, :] for tile in tiles], axis=0)
        part = pl.ds(piece * span * width, span * width)
        copy = pltpu.make_async_copy(out_ref.at[:, part], out_hbm.at[:, part], sem.at[piece])
        copy.start()
        copies.append(copy)
    for copy in copies:
        copy.wait()


def gather_scratch(count, shape):
    return [
        VMEM(shape, BF16),
        pltpu.SemaphoreType.DMA((count,)),
        pltpu.SemaphoreType.DMA((count,)),
        pltpu.SemaphoreType.DMA,
    ]


def call(kernel, specs, inputs, scratch, out, name):
    return pl.pallas_call(
        kernel,
        out_shape=jax.ShapeDtypeStruct(out, F32),
        in_specs=[pl.BlockSpec(memory_space=space) for space in specs],
        out_specs=pl.BlockSpec(memory_space=VMEM),
        scratch_shapes=scratch,
        compiler_params=pltpu.CompilerParams(
            collective_id=1, has_side_effects=True, vmem_limit_bytes=60 * 1024 * 1024),
        name=name,
    )(*inputs)


def local(
    n_tm, n_det,
    time_stream, filter_taps, det_precision, left_weight, right_weight, frame_tile, tile_owner, frame_count,
):
    half = filter_taps.shape[1] // 2
    fd, ft = left_weight.shape[1], right_weight.shape[1]
    dets = time_stream.shape[0]
    tiles = tile_owner.shape[0]
    count = n_tm * n_det
    tile = frame_tile.reshape(-1, LANES)
    sizes = (half, fd, ft, tiles)
    shape = part_shape(fd, ft, tiles)
    flat = left_weight.shape[0] * right_weight.shape[0]
    weights = (left_weight.T, right_weight.T)
    gather = gather_scratch(count, shape)
    if fast_path(n_tm, n_det, half, fd, ft, time_stream):
        taps, owner = filter_taps.T, tile_owner.reshape(1, -1)
        inputs = (time_stream, taps, owner, det_precision, tile, frame_count)
        specs = (pl.ANY,) * len(inputs)
        halo = VMEM((dets, 2 * half), BF16)
        scratch = [halo, halo, VMEM((n_det,) + tile.shape, tile.dtype), VMEM(tile.shape, tile.dtype)]
        scratch += edge_sems(n_det) + reduce_scratch(count, fd, ft, tiles, (taps, owner, tile), frame_count)
        scratch += partial_scratch(half, fd, ft, tiles, time_stream, det_precision)
        out = (2, TILE_DEV * ft * fd // LANES // 2, LANES)
        sums = call(functools.partial(whole_kernel, n_tm, n_det, sizes), specs, inputs, scratch, out, "whole")
        return pl.pallas_call(
            project_kernel,
            out_shape=jax.ShapeDtypeStruct((TILE_DEV, flat), F32),
            in_specs=[pl.BlockSpec(memory_space=VMEM)] * 3,
            out_specs=pl.BlockSpec(memory_space=pl.ANY),
            scratch_shapes=[VMEM((TILE_DEV, flat), F32), pltpu.SemaphoreType.DMA((4,))],
            name="project",
        )(sums, *weights)
    low, high, rows = exchange_edges(n_tm, n_det, 2 * half, time_stream, tile, frame_count)
    precision = lax.dynamic_slice_in_dim(det_precision, lax.axis_index("det") * dets, dets, axis=1)
    part = plain_partial_sums(time_stream, low, high, filter_taps, rows, tile_owner, precision, *sizes)
    return call(functools.partial(gather_kernel, n_tm, n_det), (VMEM,) * 3, (part,) + weights, gather, (TILE_DEV, flat), "gather")


def solution(mesh):
    return jax.shard_map(
        functools.partial(local, mesh.shape["tm"], mesh.shape["det"]),
        mesh=mesh,
        in_specs=(
            P("det", "tm"),
            P("det", None),
            P(),
            P(),
            P(),
            P(("tm", "det"), None),
            P(),
            P(("tm", "det")),
        ),
        out_specs=P(("tm", "det"), None),
        check_vma=False,
    )
```
